32 devices in a mesh: fsdp: 8 (over z, y), tp: 4 (over x, core).
Axes of the slice: x: 2, y: 2, z: 4, core: 2. Of those that a mesh axis runs over, the one named last changes fastest.
Arguments:
- tokens: bfloat16 [2048, 2048], P('fsdp'), may hold values from -6 to 6
- cotangent: bfloat16 [2048, 2048], P('fsdp'), may hold values from -6 to 6
- caption_lengths: int32 [16], P('fsdp'), may hold values from 1 to 64, 768 in all
- w_qkv: bfloat16 [2048, 3, 2048], P('fsdp', None, 'tp'), as said below
- head_biases: bfloat16 [4, 2048], P(None, ('tp', 'fsdp')), may hold values from -3 to 3
- head_gain: bfloat16 [2048], P(('tp', 'fsdp')), may hold values from 0.5 to 1.5
- w_out: bfloat16 [2048, 2048], P('tp', 'fsdp'), may hold values from -0.125 to 0.125
- model_gains: bfloat16 [2, 2048], P(None, 'fsdp'), may hold values from 0.5 to 1.5
- model_biases: bfloat16 [4, 2048], P(None, 'fsdp'), may hold values from -3 to 3
- w_fc1: bfloat16 [2048, 8192], P('fsdp', 'tp'), as said below
- w_fc2: bfloat16 [8192, 2048], P('tp', 'fsdp'), may hold values from -0.0625 to 0.0625
- ffn_gain: bfloat16 [8192], P(('tp', 'fsdp')), may hold values from 0.5 to 1.5
- ffn_biases: bfloat16 [2, 8192], P(None, ('tp', 'fsdp')), may hold values from -3 to 3
Outputs:
- layer_out: bfloat16 [2048, 2048], P('fsdp')
- grad_tokens: float32 [2048, 2048], P('fsdp')
- grad_w_qkv: float32 [2048, 3, 2048], P('fsdp', None, 'tp')
- grad_head_biases: float32 [4, 2048], P(None, ('tp', 'fsdp'))
- grad_head_gain: float32 [2048], P(('tp', 'fsdp'))
- grad_w_out: float32 [2048, 2048], P('tp', 'fsdp')
- grad_model_gains: float32 [2, 2048], P(None, 'fsdp')
- grad_model_biases: float32 [4, 2048], P(None, 'fsdp')
- grad_w_fc1: float32 [2048, 8192], P('fsdp', 'tp')
- grad_w_fc2: float32 [8192, 2048], P('tp', 'fsdp')
- grad_ffn_gain: float32 [8192], P(('tp', 'fsdp'))
- grad_ffn_biases: float32 [2, 8192], P(None, ('tp', 'fsdp'))
The draws below stay inside these ranges and needn't reach their ends.
Inputs may be any that keep to these rules, and one draw needn't show every extreme that they name: Pair p holds 64 image tokens, then caption_lengths[p] caption tokens; its other slots are padding. `w_qkv`: A projection matrix. `w_fc1`: A projection matrix.
All inputs are finite; a program needn't handle non-finite values. No bound on the sum of `caption_lengths` on one device may be relied on, other than what follows from the above.
Results may differ from the reference program's by a relative error of at most 0.014.
Values may be sent and summed in bfloat16 or wider, within the bound.
No kernel may reach another device: no remote copies, remote signals or barrier semaphores. Data moves between devices by JAX's collectives and lax.ppermute only.
A program may use at most 192 MiB of HBM per device.

```python
import math
import jax
import jax.numpy as jnp
import numpy as np
from jax import lax

D = 2048
HEADS = 32
FF = 8192
IMAGE = 64
CAPTION = 64
SLOTS = 128
PAIRS = 16
TOKENS = 2048


def draw_w_qkv(key, part):
    base = jnp.clip(jax.random.normal(key, (D, 3, D), jnp.float32), -3.0, 3.0)
    head_number = (jnp.arange(D) // (D // HEADS)).astype(jnp.float32)
    rising = jnp.exp(jnp.log(3.0) * head_number / (HEADS - 1))
    factor = jnp.where(jnp.arange(3)[:, None] == 2, rising[None, :], 1.0)
    return (base * factor[None, :, :] / jnp.sqrt(jnp.float32(D))).astype(jnp.bfloat16)


def draw_w_fc1(key, part):
    base = jnp.clip(jax.random.normal(key, (D, FF), jnp.float32), -3.0, 3.0)
    column = jnp.arange(FF).astype(jnp.float32)
    rising = jnp.exp(jnp.log(3.0) * column / (FF - 1))
    return (base * rising[None, :] / jnp.sqrt(jnp.float32(D))).astype(jnp.bfloat16)


def shard_levels(stream_key, shape, shards, smallest, top_value):
    def one(dim, shards_of):
        draws = jax.random.uniform(jax.random.fold_in(jax.random.fold_in(stream_key, 6), dim), (shards_of,), jnp.float32, smallest / len(shards), top_value / len(shards))
        return jnp.repeat(jnp.exp(draws), shape[dim] // shards_of).reshape((-1,) + (1,) * (len(shape) - dim - 1))

    gain = one(*shards[0])
    for cut in shards[1:]:
        gain = gain * one(*cut)
    return gain


def length_profile(number_of, total, reach, slope):
    weights = [(1 << 20) // math.isqrt(standing ** slope) + 1 for standing in range(2, number_of + 1)]
    surplus, given = total - reach - (number_of - 1), [1] * (number_of - 1)
    while surplus > 0:
        free = [i for i in range(number_of - 1) if given[i] < reach]
        whole, remaining = sum([weights[i] for i in free]), surplus
        for i in free:
            more = min(reach - given[i], max(1, remaining * weights[i] // whole), surplus)
            given[i] = given[i] + more
            surplus = surplus - more
    return np.array([reach] + given)


def ragged_sizes(key, number_of, total, reach, lean):
    if number_of == 2:
        one = jax.random.randint(key, (), max(1, total - reach), min(reach, total - 1) + 1)
        return jnp.stack([one, total - one])
    sizes = jnp.asarray(length_profile(number_of, total, reach, lean), jnp.int32)
    twos = (number_of - 1) // 2
    source_of, sink = sizes[1:1 + 2 * twos:2], sizes[2:2 + 2 * twos:2]
    margin = jnp.minimum(source_of - 1, reach - sink)
    shifted = jax.random.randint(jax.random.fold_in(key, 1), (twos,), 0, 1 << 20) % (margin + 1)
    sizes = sizes.at[1:1 + 2 * twos:2].set(source_of - shifted).at[2:2 + 2 * twos:2].set(sink + shifted)
    return sizes[jax.random.permutation(jax.random.fold_in(key, 2), number_of)]


def centred(stream_key, extent, scale, limit, cuts=(), held_as=jnp.bfloat16):
    values = scale * jax.random.normal(stream_key, extent, jnp.float32)
    if cuts:
        values = values * shard_levels(stream_key, extent, cuts, -0.22, 0.18)
    return jnp.clip(values, -limit, limit).astype(held_as)


def setup_inputs(seed: int = 0) -> dict:
    splits = jax.random.split(jax.random.key(seed), 14)
    return {
        "tokens": centred(splits[0], (TOKENS, D), 1.0, 6.0, ((0, 8),)),
        "cotangent": centred(splits[1], (TOKENS, D), 1.0, 6.0, ((0, 8),)),
        "caption_lengths": ragged_sizes(splits[2], PAIRS, 3 * PAIRS * CAPTION // 4, CAPTION, 1).astype(jnp.int32),
        "w_qkv": draw_w_qkv(jax.random.fold_in(splits[13], 71), 0),
        "head_biases": centred(splits[4], (4, D), 0.5, 3.0, ((1, 32),)),
        "head_gain": jnp.clip(1.0 + 0.1 * jax.random.normal(splits[5], (D,), jnp.float32), 0.5, 1.5).astype(jnp.bfloat16),
        "w_out": centred(splits[6], (D, D), D ** -0.5, 0.125, ((0, 4), (1, 8))),
        "model_gains": jnp.clip(1.0 + 0.1 * jax.random.normal(splits[7], (2, D), jnp.float32), 0.5, 1.5).astype(jnp.bfloat16),
        "model_biases": centred(splits[8], (4, D), 0.5, 3.0, ((1, 8),)),
        "w_fc1": draw_w_fc1(jax.random.fold_in(splits[13], 71), 0),
        "w_fc2": centred(splits[10], (FF, D), FF ** -0.5, 0.0625, ((0, 4), (1, 8))),
        "ffn_gain": jnp.clip(1.0 + 0.1 * jax.random.normal(splits[11], (FF,), jnp.float32), 0.5, 1.5).astype(jnp.bfloat16),
        "ffn_biases": centred(splits[12], (2, FF), 0.5, 3.0, ((1, 32),)),
    }


@jax.custom_vjp
def low(v):
    return lax.optimization_barrier(v.astype(jnp.bfloat16)).astype(jnp.float32)

@jax.custom_vjp
def low_back(v):
    return v

def low_keep(v):
    return (low(v), None)

def low_pass(kept, grad):
    return (grad,)

def back_keep(v):
    return (v, None)

def back_low(kept, grad):
    return (low(grad),)
low.defvjp(low_keep, low_pass)
low_back.defvjp(back_keep, back_low)
norm_eps = 1e-05
highest = lax.Precision.HIGHEST

def layer_norm(values, gain_vector, shift_vector):
    mean_value = lax.optimization_barrier(jnp.mean(values, axis=-1, keepdims=True))
    variance = lax.optimization_barrier(jnp.mean(values * values, axis=-1, keepdims=True)) - mean_value * mean_value
    return (values - mean_value) * lax.rsqrt(variance + norm_eps) * gain_vector + shift_vector

def rotation_tables(count, row_width):
    position = jnp.arange(count).astype(jnp.float32)[:, None]
    channel = jnp.arange(row_width // 2).astype(jnp.float32)[None, :]
    frequency = jnp.exp(-(2.0 * channel / row_width) * jnp.log(10000.0))
    angle = position * frequency
    zeta_base = (2.0 * channel + 0.4 * row_width) / (1.4 * row_width)
    growth = jnp.exp((position - count // 2) / 512.0 * jnp.log(zeta_base))
    return (jnp.cos(angle), jnp.sin(angle), growth)

def turn(values, cosine, sine_table, factor):
    paired = values.reshape(values.shape[:-1] + (values.shape[-1] // 2, 2))
    even_part = paired[..., 0]
    odd_part = paired[..., 1]
    cosine = cosine[:, None, :]
    sine_table = sine_table[:, None, :]
    factor = factor[:, None, :]
    new_even = (even_part * cosine - odd_part * sine_table) * factor
    new_odd = (odd_part * cosine + even_part * sine_table) * factor
    return jnp.stack([new_even, new_odd], axis=-1).reshape(values.shape)

def forward(tokens_f, weight_set, keep_rows, key_valid):
    w_qkv, head_biases, head_gain, w_out, model_gains, model_biases, w_fc1, w_fc2, ffn_gain, ffn_biases = weight_set
    head_dim = D // HEADS
    cosine, sine_table, growth = rotation_tables(SLOTS, head_dim)
    normed_in = low(layer_norm(tokens_f, model_gains[0], model_biases[0]))
    linear = jnp.einsum('td,dce->tce', normed_in, w_qkv, precision=highest) + head_biases[:3][None]
    linear = low_back(linear)
    shaped = linear.reshape(PAIRS, SLOTS, 3, HEADS, head_dim)
    queries = low(turn(shaped[:, :, 0], cosine, sine_table, growth))
    keys_rot = low(turn(shaped[:, :, 1], cosine, sine_table, 1.0 / growth))
    values_in = low(shaped[:, :, 2])
    group_size = math.gcd(PAIRS, max(1, 4096 // SLOTS))
    blocks = PAIRS // group_size

    def regroup(source):
        return source.reshape((blocks, group_size) + source.shape[1:])
    causal = jnp.arange(SLOTS)[:, None] >= jnp.arange(SLOTS)[None, :]
    scale_value = 1.0 / math.sqrt(head_dim)

    def attend(pieces):
        query_block, key_block, value_block, valid_block = pieces
        raw_scores = low_back(jnp.einsum('gqhe,gkhe->ghqk', query_block, key_block, precision=highest))
        allowed = causal[None, None] & (valid_block[:, None, None, :] > 0)
        scores = jnp.where(allowed, raw_scores * scale_value, -1e+30)
        probs = jax.nn.softmax(scores, axis=-1)
        mixed_values = jnp.einsum('ghqk,gkhe->gqhe', low(probs), value_block, precision=highest)
        return low_back(mixed_values)
    attended = lax.map(jax.checkpoint(attend), (regroup(queries), regroup(keys_rot), regroup(values_in), regroup(key_valid)))
    heads_out = attended.reshape(PAIRS * SLOTS, D)
    post_attn = low(layer_norm(heads_out, head_gain, head_biases[3]))
    branch = low_back(jnp.dot(post_attn, w_out, precision=highest))
    middle = tokens_f + branch + model_biases[2]
    normed_mid = low(layer_norm(middle, model_gains[1], model_biases[1]))
    before = low_back(jnp.dot(normed_mid, w_fc1, precision=highest) + ffn_biases[0])
    active = jax.nn.gelu(before, approximate=False)
    post_ffn = low(layer_norm(active, ffn_gain, ffn_biases[1]))
    second = low_back(jnp.dot(post_ffn, w_fc2, precision=highest))
    return (middle + second + model_biases[3]) * keep_rows[:, None]

def reference(tokens, cotangent, caption_lengths, w_qkv, head_biases, head_gain, w_out, model_gains, model_biases, w_fc1, w_fc2, ffn_gain, ffn_biases):
    slot_index = jnp.arange(SLOTS)[None, :]
    key_valid = (slot_index < IMAGE + caption_lengths[:, None]).astype(jnp.float32)
    keep_rows = key_valid.reshape(PAIRS * SLOTS)
    params = (w_qkv.astype(jnp.float32), head_biases.astype(jnp.float32), head_gain.astype(jnp.float32), w_out.astype(jnp.float32), model_gains.astype(jnp.float32), model_biases.astype(jnp.float32), w_fc1.astype(jnp.float32), w_fc2.astype(jnp.float32), ffn_gain.astype(jnp.float32), ffn_biases.astype(jnp.float32))
    tokens_f = tokens.astype(jnp.float32)

    def apply(tokens_in, weight_set):
        return forward(tokens_in, weight_set, keep_rows, key_valid)
    output, pullback = jax.vjp(apply, tokens_f, params)
    grad_tokens, grad_params = pullback(cotangent.astype(jnp.float32))
    return (output.astype(jnp.bfloat16), grad_tokens, grad_params[0], grad_params[1], grad_params[2], grad_params[3], grad_params[4], grad_params[5], grad_params[6], grad_params[7], grad_params[8], grad_params[9])
```

```python
import functools
import math

import jax
import jax.numpy as jnp
from jax import lax
from jax.sharding import PartitionSpec as P

HEADS = 32
FF = 8192
IMAGE = 64
GROUPS = 4

f32 = jnp.float32
bf16 = jnp.bfloat16
norm_eps = 1e-05


def pick(table, index):
    return lax.dynamic_index_in_dim(jnp.asarray(table, jnp.int32), index, keepdims=False)


def put(buffer, block, index):
    return lax.dynamic_update_slice(buffer, block[None], (index,) + (0,) * block.ndim)


def put_all(buffer, blocks, index_of, k):
    for label in range(blocks.shape[0]):
        buffer = put(buffer, blocks[label], index_of(k, label))
    return buffer


def block_at(array, index, axis=0):
    return lax.dynamic_index_in_dim(array, index, axis, keepdims=False)


class Ring:
    def __init__(self, members, here, of_group):
        self.size = len(members[0])
        self.sorted_members = [sorted(ring) for ring in members]
        device_count = sum(len(ring) for ring in members)
        place = [0] * device_count
        for ring in members:
            for step, device in enumerate(ring):
                place[device] = step
        self.position = pick(place, here)
        self.labels = [of_group(device) for device in members[0]]
        self.forward = [
            (ring[i], ring[(i + 1) % self.size]) for ring in members for i in range(self.size)
        ]
        self.backward = [(b, a) for a, b in self.forward]

    def label(self, offset):
        return pick(self.labels, (self.position + offset) % self.size)

    def send(self, block, way):
        return lax.ppermute(block, "fsdp", self.forward if way > 0 else self.backward)

    def gather_native(self, chunk):
        return lax.all_gather(chunk, "fsdp", axis=0, axis_index_groups=self.sorted_members)

    def scatter_native(self, part):
        return lax.psum_scatter(
            part,
            "fsdp",
            scatter_dimension=0,
            axis_index_groups=self.sorted_members,
            tiled=False,
        ).astype(f32)

    def gather(self, chunks, buffers, index_of=lambda k, label: label):
        if self.size > 4 * GROUPS:
            gathered = [self.gather_native(c) for c in chunks]
            return [put_all(b, g, index_of, k) for k, (b, g) in enumerate(zip(buffers, gathered))]
        half = self.size // 2
        buffers = [put(b, c, index_of(k, self.label(0))) for k, (b, c) in enumerate(zip(buffers, chunks))]
        onward = list(chunks)
        backward = list(chunks)
        for step in range(1, half):
            for k in range(len(chunks)):
                onward[k] = self.send(onward[k], 1)
                backward[k] = self.send(backward[k], -1)
                buffers[k] = put(buffers[k], onward[k], index_of(k, self.label(-step)))
                buffers[k] = put(buffers[k], backward[k], index_of(k, self.label(step)))
        for k in range(len(chunks)):
            cut = chunks[k].shape[0] // 2
            last = jnp.concatenate(
                [self.send(onward[k][:cut], 1), self.send(backward[k][cut:], -1)], axis=0
            )
            buffers[k] = put(buffers[k], last, index_of(k, self.label(half)))
        return buffers

    def scatter(self, parts):
        if self.size > 4 * GROUPS:
            return [self.scatter_native(part) for part in parts]
        half = self.size // 2
        onward, backward = [], []
        for part in parts:
            far = block_at(part, self.label(half))
            cut = part.shape[1] // 2
            onward.append(self.send(far[:cut], 1))
            backward.append(self.send(far[cut:], -1))
        for step in range(half - 1, 0, -1):
            for k, part in enumerate(parts):
                ahead = block_at(part, self.label(step)).astype(f32)
                behind = block_at(part, self.label(-step)).astype(f32)
                if step == half - 1:
                    cut = part.shape[1] // 2
                    ahead = jnp.concatenate(
                        [ahead[:cut] + onward[k].astype(f32), ahead[cut:]], axis=0
                    )
                    behind = jnp.concatenate(
                        [behind[:cut], behind[cut:] + backward[k].astype(f32)], axis=0
                    )
                else:
                    ahead = ahead + onward[k].astype(f32)
                    behind = behind + backward[k].astype(f32)
                onward[k] = self.send(ahead.astype(part.dtype), 1)
                backward[k] = self.send(behind.astype(part.dtype), -1)
        sums = []
        for k, part in enumerate(parts):
            own = block_at(part, self.label(0)).astype(f32)
            if half == 1:
                sums.append(own + jnp.concatenate([onward[k], backward[k]], axis=0).astype(f32))
            else:
                sums.append(own + onward[k].astype(f32) + backward[k].astype(f32))
        return sums


def tp_send(block, mask):
    return lax.ppermute(block, "tp", [(i, i ^ mask) for i in range(4)])


def tp_sum(values):
    return values + tp_send(values, 1) + tp_send(values, 2) + tp_send(values, 3)


def tp_rows_gather(piece, buffer, rank):
    across = tp_send(piece, 2)
    buffer = put(buffer, piece, rank)
    buffer = put(buffer, tp_send(piece, 1), rank ^ 1)
    buffer = put(buffer, across, rank ^ 2)
    return put(buffer, tp_send(across, 1), rank ^ 3)


def rotation_tables(count, row_width):
    position = jnp.arange(count).astype(f32)[:, None]
    channel = jnp.arange(row_width // 2).astype(f32)[None, :]
    frequency = jnp.exp(-(2.0 * channel / row_width) * jnp.log(10000.0))
    angle = position * frequency
    zeta_base = (2.0 * channel + 0.4 * row_width) / (1.4 * row_width)
    growth = jnp.exp((position - count // 2) / 512.0 * jnp.log(zeta_base))
    return (jnp.cos(angle), jnp.sin(angle), growth)


def turn(values, cosine, sine_table, factor):
    paired = values.reshape(values.shape[:-1] + (values.shape[-1] // 2, 2))
    even_part = paired[..., 0]
    odd_part = paired[..., 1]
    cosine = cosine[:, None, :]
    sine_table = sine_table[:, None, :]
    factor = factor[:, None, :]
    new_even = (even_part * cosine - odd_part * sine_table) * factor
    new_odd = (odd_part * cosine + even_part * sine_table) * factor
    return jnp.stack([new_even, new_odd], axis=-1).reshape(values.shape)


def turn_back(values, cosine, sine_table, factor):
    paired = values.reshape(values.shape[:-1] + (values.shape[-1] // 2, 2))
    even_part = paired[..., 0] * factor[:, None, :]
    odd_part = paired[..., 1] * factor[:, None, :]
    cosine = cosine[:, None, :]
    sine_table = sine_table[:, None, :]
    new_even = even_part * cosine + odd_part * sine_table
    new_odd = odd_part * cosine - even_part * sine_table
    return jnp.stack([new_even, new_odd], axis=-1).reshape(values.shape)


def norm_stats(first_sum, square_sum, row_width):
    mean_value = first_sum / row_width
    variance = square_sum / row_width - mean_value * mean_value
    return mean_value, lax.rsqrt(variance + norm_eps)


def norm_rows(values, gain_vector, shift_vector):
    width = values.shape[-1]
    mean_value, inverse = norm_stats(
        jnp.sum(values, axis=-1, keepdims=True),
        jnp.sum(values * values, axis=-1, keepdims=True),
        width,
    )
    hat = (values - mean_value) * inverse
    return hat * gain_vector + shift_vector, hat, inverse


def norm_back_rows(scaled, hat, inverse):
    width = scaled.shape[-1]
    return inverse * (
        scaled
        - jnp.sum(scaled, axis=-1, keepdims=True) / width
        - hat * jnp.sum(scaled * hat, axis=-1, keepdims=True) / width
    )


def matmul(a, b, dims):
    return lax.dot_general(a, b, (dims, ((), ())), preferred_element_type=f32)


def per_device(
    tokens,
    cotangent,
    caption_lengths,
    w_qkv,
    head_biases,
    head_gain,
    w_out,
    model_gains,
    model_biases,
    w_fc1,
    w_fc2,
    ffn_gain,
    ffn_biases,
    *,
    fsdp_size,
):
    here = lax.axis_index("fsdp")
    rank = lax.axis_index("tp")
    core, side = rank % 2, rank // 2
    others = fsdp_size // GROUPS
    group, member = here // others, here % others
    ring = Ring(
        [list(range(0, fsdp_size, 2)) + list(range(fsdp_size - 1, 0, -2))], here, lambda f: f
    )
    member_ring = Ring(
        [[g * others + o for o in range(others)] for g in range(GROUPS)],
        here,
        lambda f: f % others,
    )

    def group_send(block, shift):
        return lax.ppermute(
            block,
            "fsdp",
            [
                (g * others + o, (g + shift) % GROUPS * others + o)
                for g in range(GROUPS)
                for o in range(others)
            ],
        )

    pair_count = caption_lengths.shape[0]
    row_count, model_width = tokens.shape
    slot_count = row_count // pair_count
    sub_rows = row_count // 4
    head_dim = model_width // HEADS
    local_width = w_qkv.shape[2]
    local_heads = local_width // head_dim
    block_rows = w_qkv.shape[0]
    hidden_width = FF
    local_hidden = w_fc1.shape[1] // GROUPS

    model_part = jnp.concatenate([model_gains, model_biases], axis=0)
    head_part = jnp.concatenate([head_biases, head_gain[None]], axis=0)
    unit_part = jnp.concatenate([ffn_biases, ffn_gain[None]], axis=0)
    packed = jnp.concatenate([model_part.reshape(-1), head_part.reshape(-1), unit_part.reshape(-1)])
    packed_size = packed.shape[0]
    packed = jnp.pad(packed, (0, -packed_size % 256)).reshape(2, -1)
    qkv_blocks = [w_qkv[:, c] for c in range(3)]

    def room(chunk):
        return jnp.zeros((fsdp_size,) + chunk.shape, chunk.dtype)

    first = [packed] + qkv_blocks
    vectors, *qkv_full = ring.gather(first, [room(c) for c in first])
    qkv_full = [w.reshape(model_width, local_width) for w in qkv_full]
    vectors = vectors.reshape(fsdp_size, -1)[:, :packed_size]
    sizes = [model_part.size, head_part.size, unit_part.size]
    model_vectors = (
        vectors[:, : sizes[0]].reshape((fsdp_size,) + model_part.shape).transpose(1, 0, 2)
    ).reshape(6, model_width).astype(f32)
    head_vectors = (
        vectors[:, sizes[0] : sizes[0] + sizes[1]]
        .reshape((fsdp_size,) + head_part.shape)
        .transpose(1, 0, 2)
    ).reshape(5, local_width).astype(f32)
    unit_all = vectors[:, sizes[0] + sizes[1] :].reshape((GROUPS, others) + unit_part.shape)
    unit_vectors = block_at(unit_all, group).transpose(1, 0, 2).reshape(3, local_hidden).astype(f32)

    (out_full,) = ring.gather([w_out.T], [room(w_out.T)])
    out_full = out_full.reshape(model_width, local_width)

    fc_full = []
    for weights in (w_fc2.T, w_fc1):
        pieces = weights.reshape(block_rows, GROUPS, local_hidden)
        chunks = [block_at(pieces, group, 1)]
        for shift in range(1, GROUPS):
            chunks.append(group_send(block_at(pieces, (group + shift) % GROUPS, 1), shift))
        buffer = jnp.zeros((fsdp_size, block_rows, local_hidden), bf16)
        for shift in range(GROUPS):
            (buffer,) = member_ring.gather(
                [chunks[shift]],
                [buffer],
                lambda k, label, s=shift: (group - s) % GROUPS * others + label,
            )
        fc_full.append(buffer.reshape(model_width, local_hidden))
    fc2_full, fc1_full = fc_full

    def rows_gather(piece):
        buffer = jnp.zeros((GROUPS * 4,) + piece.shape, piece.dtype)
        pieces = [piece] + [group_send(piece, shift) for shift in range(1, GROUPS)]
        for shift, block in enumerate(pieces):
            base = (group - shift) % GROUPS * 4
            across = tp_send(block, 2)
            buffer = put(buffer, block, base + rank)
            buffer = put(buffer, tp_send(block, 1), base + (rank ^ 1))
            buffer = put(buffer, across, base + (rank ^ 2))
            buffer = put(buffer, tp_send(across, 1), base + (rank ^ 3))
        return buffer.reshape(GROUPS * 4 * piece.shape[0], piece.shape[1])

    def rows_product(left, right, dims):
        by_rank = left.reshape(2, 2, sub_rows, left.shape[1])
        away = block_at(by_rank, 1 - core, 1).reshape(2 * sub_rows, -1)
        sent = tp_send(matmul(away, right, dims).astype(bf16), 1)
        kept = block_at(by_rank, core, 1).reshape(2 * sub_rows, -1)
        total = (matmul(kept, right, dims) + sent.astype(f32)).reshape(2, sub_rows, -1)
        crossing = tp_send(block_at(total, 1 - side).astype(bf16), 2)
        return block_at(total, side) + crossing.astype(f32)

    def group_product(left, right, dims):
        by_rank = left.reshape(GROUPS * 2, 2, sub_rows, left.shape[1])
        width = GROUPS * 2 * sub_rows
        away = block_at(by_rank, 1 - core, 1).reshape(width, -1)
        sent = tp_send(matmul(away, right, dims).astype(bf16), 1)
        kept = block_at(by_rank, core, 1).reshape(width, -1)
        total = (matmul(kept, right, dims) + sent.astype(f32)).reshape(GROUPS, 2, sub_rows, -1)
        pieces = []
        for shift in (2, 1, 3, 0):
            chunk = block_at(total, (group + shift) % GROUPS)
            crossing = tp_send(block_at(chunk, 1 - side).astype(bf16), 2)
            chunk = block_at(chunk, side) + crossing.astype(f32)
            if shift:
                chunk = group_send(chunk.astype(bf16), shift).astype(f32)
            pieces.append(chunk)
        return pieces[3] + pieces[0] + pieces[1] + pieces[2]

    def group_sum(values):
        values = tp_sum(values)
        return values + sum(group_send(values, shift) for shift in range(1, GROUPS))

    def my_rows(array):
        return lax.dynamic_slice_in_dim(array, rank * sub_rows, sub_rows, 0)

    slot_index = jnp.arange(slot_count)[None, :]
    key_valid = slot_index < IMAGE + caption_lengths[:, None]
    keep_rows = key_valid.reshape(row_count).astype(f32)[:, None]
    my_keep = my_rows(keep_rows)
    my_grad_out = my_rows(cotangent).astype(f32) * my_keep
    grad_out_all = rows_gather(my_grad_out.astype(bf16))

    cosine, sine_table, growth = rotation_tables(slot_count, head_dim)
    causal = jnp.arange(slot_count)[:, None] >= jnp.arange(slot_count)[None, :]
    allowed = causal[None, None] & key_valid[:, None, None, :]
    scale_value = 1.0 / math.sqrt(head_dim)
    normed_in, _, _ = norm_rows(tokens.astype(f32), model_vectors[0], model_vectors[2])
    normed_in_b = normed_in.astype(bf16)
    linear = [
        (matmul(normed_in_b, qkv_full[c], ((1,), (0,))) + head_vectors[c]).reshape(
            pair_count, slot_count, local_heads, head_dim
        )
        for c in range(3)
    ]
    queries = turn(linear[0], cosine, sine_table, growth).astype(bf16)
    keys_rot = turn(linear[1], cosine, sine_table, 1.0 / growth).astype(bf16)
    values_in = linear[2].astype(bf16)
    raw_scores = jnp.einsum("gqhe,gkhe->ghqk", queries, keys_rot, preferred_element_type=f32)
    scores = jnp.where(allowed, raw_scores * scale_value, -1e30)
    top_score = jnp.max(scores, axis=-1, keepdims=True)
    log_total = top_score + jnp.log(jnp.sum(jnp.exp(scores - top_score), axis=-1, keepdims=True))
    probs = jnp.exp(scores - log_total)
    heads_out = jnp.einsum(
        "ghqk,gkhe->gqhe", probs.astype(bf16), values_in, preferred_element_type=f32
    ).reshape(row_count, local_width)
    head_stats = tp_sum(
        jnp.stack([jnp.sum(heads_out, axis=-1), jnp.sum(heads_out * heads_out, axis=-1)])
    )
    mean_attn, inverse_attn = norm_stats(
        head_stats[0][:, None], head_stats[1][:, None], model_width
    )
    hat_attn = (heads_out - mean_attn) * inverse_attn
    post_attn_b = (hat_attn * head_vectors[4] + head_vectors[3]).astype(bf16)
    branch = rows_product(post_attn_b, out_full, ((1,), (1,)))
    middle = my_rows(tokens).astype(f32) + branch + model_vectors[4]
    normed_mid, hat_mid, inverse_mid = norm_rows(middle, model_vectors[1], model_vectors[3])

    normed_mid_all = rows_gather(normed_mid.astype(bf16))
    grad_post_ffn = matmul(grad_out_all, fc2_full, ((1,), (0,)))
    before = matmul(normed_mid_all, fc1_full, ((1,), (0,))) + unit_vectors[0]
    below = 0.5 * lax.erfc(-before * math.sqrt(0.5))
    active = before * below
    slope = below + before * (math.sqrt(0.5 / math.pi) * jnp.exp(-0.5 * before * before))
    scaled_ffn = grad_post_ffn * unit_vectors[2]
    sums = group_sum(
        jnp.stack(
            [
                jnp.sum(active, axis=-1),
                jnp.sum(active * active, axis=-1),
                jnp.sum(scaled_ffn, axis=-1),
                jnp.sum(scaled_ffn * active, axis=-1),
            ]
        )
    )[:, :, None]
    mean_ffn, inverse_ffn = norm_stats(sums[0], sums[1], hidden_width)
    hat_ffn = (active - mean_ffn) * inverse_ffn
    hat_sum = inverse_ffn * (sums[3] - mean_ffn * sums[2])
    grad_active = inverse_ffn * (
        scaled_ffn - sums[2] / hidden_width - hat_ffn * hat_sum / hidden_width
    )
    grad_before_b = (grad_active * slope).astype(bf16)
    grad_mid_normed = group_product(grad_before_b, fc1_full, ((1,), (1,)))
    grad_middle = my_grad_out + norm_back_rows(
        grad_mid_normed * model_vectors[1], hat_mid, inverse_mid
    )
    grad_middle_b = tp_rows_gather(
        grad_middle.astype(bf16), jnp.zeros((4, sub_rows, model_width), bf16), rank
    ).reshape(row_count, model_width)

    post_ffn_b = (hat_ffn * unit_vectors[2] + unit_vectors[1]).astype(bf16)
    second = group_product(post_ffn_b, fc2_full, ((1,), (1,)))
    out_rows = ((middle + second + model_vectors[5]) * my_keep).astype(bf16)
    layer_out = tp_rows_gather(
        out_rows, jnp.zeros((4, sub_rows, model_width), bf16), rank
    ).reshape(row_count, model_width)

    def fc_scatter(left, right):
        grad = matmul(left, right, ((0,), (0,))).astype(bf16)
        grad = grad.reshape(GROUPS, others, block_rows, local_hidden)
        buffer = jnp.zeros((GROUPS, block_rows, local_hidden), f32)
        for shift in (2, 1, 3, 0):
            (chunk,) = member_ring.scatter([block_at(grad, (group + shift) % GROUPS)])
            if shift:
                chunk = group_send(chunk.astype(bf16), shift).astype(f32)
            buffer = put(buffer, chunk, (group - shift) % GROUPS)
        return buffer.transpose(1, 0, 2).reshape(block_rows, GROUPS * local_hidden)

    grad_fc2_s = fc_scatter(grad_out_all, post_ffn_b).T
    grad_fc1_s = fc_scatter(normed_mid_all, grad_before_b)
    unit_grads = jnp.stack(
        [
            jnp.sum(grad_before_b.astype(f32), axis=0),
            jnp.sum(grad_post_ffn, axis=0),
            jnp.sum(grad_post_ffn * hat_ffn, axis=0),
        ]
    )

    grad_post_attn = matmul(grad_middle_b, out_full, ((1,), (0,)))
    grad_out_proj = matmul(grad_middle_b, post_attn_b, ((0,), (0,))).astype(bf16)
    (grad_out_s,) = ring.scatter([grad_out_proj.reshape(fsdp_size, block_rows, local_width)])
    scaled_attn = grad_post_attn * head_vectors[4]
    head_back = tp_sum(
        jnp.stack([jnp.sum(scaled_attn, axis=-1), jnp.sum(scaled_attn * hat_attn, axis=-1)])
    )[:, :, None]
    grad_heads_b = (
        (
            inverse_attn
            * (scaled_attn - head_back[0] / model_width - hat_attn * head_back[1] / model_width)
        )
        .astype(bf16)
        .reshape(pair_count, slot_count, local_heads, head_dim)
    )
    grad_probs = jnp.einsum("gqhe,gkhe->ghqk", grad_heads_b, values_in, preferred_element_type=f32)
    grad_values = jnp.einsum(
        "ghqk,gqhe->gkhe", probs.astype(bf16), grad_heads_b, preferred_element_type=f32
    )
    grad_scores = probs * (grad_probs - jnp.sum(probs * grad_probs, axis=-1, keepdims=True))
    grad_scores_b = (grad_scores * scale_value).astype(bf16)
    grad_queries = jnp.einsum(
        "ghqk,gkhe->gqhe", grad_scores_b, keys_rot, preferred_element_type=f32
    )
    grad_keys = jnp.einsum("ghqk,gqhe->gkhe", grad_scores_b, queries, preferred_element_type=f32)
    grad_linear = [
        part.reshape(row_count, local_width).astype(bf16)
        for part in (
            turn_back(grad_queries, cosine, sine_table, growth),
            turn_back(grad_keys, cosine, sine_table, 1.0 / growth),
            grad_values,
        )
    ]
    grad_qkv = [
        matmul(normed_in_b, part, ((0,), (0,)))
        .astype(bf16)
        .reshape(fsdp_size, block_rows, local_width)
        for part in grad_linear
    ]
    grad_qkv_s = jnp.stack(ring.scatter(grad_qkv), axis=1)
    grad_in_normed = rows_product(
        jnp.concatenate(grad_linear, axis=1),
        jnp.concatenate(qkv_full, axis=1),
        ((1,), (1,)),
    )
    _, hat_in, inverse_in = norm_rows(
        my_rows(tokens).astype(f32), model_vectors[0], model_vectors[2]
    )
    grad_token_rows = grad_middle + norm_back_rows(
        grad_in_normed * model_vectors[0], hat_in, inverse_in
    )
    grad_tokens = tp_rows_gather(
        grad_token_rows, jnp.zeros((4, sub_rows, model_width), f32), rank
    ).reshape(row_count, model_width)

    model_grads = jnp.stack(
        [
            jnp.sum(grad_in_normed * hat_in, axis=0),
            jnp.sum(grad_mid_normed * hat_mid, axis=0),
            jnp.sum(grad_in_normed, axis=0),
            jnp.sum(grad_mid_normed, axis=0),
            jnp.sum(grad_middle, axis=0),
            jnp.sum(my_grad_out, axis=0),
        ]
    )
    head_grads = jnp.stack(
        [jnp.sum(part.astype(f32), axis=0) for part in grad_linear]
        + [jnp.sum(grad_post_attn, axis=0), jnp.sum(grad_post_attn * hat_attn, axis=0)]
    )

    def by_block(vectors_in, blocks):
        return vectors_in.reshape(vectors_in.shape[0], blocks, -1).transpose(1, 0, 2)

    model_blocks = by_block(tp_sum(model_grads), fsdp_size).reshape(fsdp_size, -1)
    head_blocks = by_block(head_grads, fsdp_size).reshape(fsdp_size, -1)
    joined = jnp.concatenate([model_blocks, head_blocks], axis=1)
    joined_size = joined.shape[1]
    joined = jnp.pad(joined, ((0, 0), (0, -joined_size % 256))).reshape(fsdp_size, 2, -1)
    (joined_s,) = ring.scatter([joined])
    joined_s = joined_s.reshape(-1)
    model_s = joined_s[: model_blocks.shape[1]].reshape(6, -1)
    head_s = joined_s[model_blocks.shape[1] : joined_size].reshape(5, -1)
    unit_blocks = by_block(unit_grads, others).reshape(others, -1)
    unit_size = unit_blocks.shape[1]
    unit_blocks = jnp.pad(unit_blocks, ((0, 0), (0, -unit_size % 256))).reshape(others, 2, -1)
    (unit_s,) = member_ring.scatter([unit_blocks])
    unit_s = unit_s.reshape(-1)[:unit_size].reshape(3, -1)
    return (
        layer_out,
        grad_tokens,
        grad_qkv_s,
        head_s[:4],
        head_s[4],
        grad_out_s.T,
        model_s[:2],
        model_s[2:],
        grad_fc1_s,
        grad_fc2_s,
        unit_s[2],
        unit_s[:2],
    )


def solution(mesh):
    placed = (
        P("fsdp", None),
        P("fsdp", None),
        P("fsdp"),
        P("fsdp", None, "tp"),
        P(None, ("tp", "fsdp")),
        P(("tp", "fsdp")),
        P("tp", "fsdp"),
        P(None, "fsdp"),
        P(None, "fsdp"),
        P("fsdp", "tp"),
        P("tp", "fsdp"),
        P(("tp", "fsdp")),
        P(None, ("tp", "fsdp")),
    )
    return jax.shard_map(
        functools.partial(per_device, fsdp_size=mesh.shape["fsdp"]),
        mesh=mesh,
        in_specs=placed,
        out_specs=(
            P("fsdp", None),
            P("fsdp", None),
            P("fsdp", None, "tp"),
            P(None, ("tp", "fsdp")),
            P(("tp", "fsdp")),
            P("tp", "fsdp"),
            P(None, "fsdp"),
            P(None, "fsdp"),
            P("fsdp", "tp"),
            P("tp", "fsdp"),
            P(("tp", "fsdp")),
            P(None, ("tp", "fsdp")),
        ),
        check_vma=False,
    )
```

```python
import functools
import math

import jax
import jax.numpy as jnp
import numpy as np
from jax import lax
from jax.experimental import pallas as pl
from jax.experimental.pallas import tpu as pltpu
from jax.sharding import PartitionSpec as P

HEADS = 32
FF = 8192
IMAGE = 64
GROUPS = 4

f32 = jnp.float32
bf16 = jnp.bfloat16
norm_eps = 1e-05


def pick(table, index):
    return lax.dynamic_index_in_dim(jnp.asarray(table, jnp.int32), index, keepdims=False)


def row_at(table, index):
    return lax.dynamic_index_in_dim(jnp.asarray(table, jnp.int32), index, keepdims=False)


def put(buffer, block, index):
    return lax.dynamic_update_slice(buffer, block[None], (index,) + (0,) * block.ndim)


def block_at(array, index, axis=0):
    return lax.dynamic_index_in_dim(array, index, axis, keepdims=False)


def after(value, *tokens):
    return lax.optimization_barrier((value,) + tokens)[0]


class Ring:
    def __init__(self, size, here):
        self.size = size
        self.here = here
        self.native = size > 8
        self.order = list(range(0, size, 2)) + list(range(size - 1, 0, -2))
        self.position = pick([self.order.index(i) for i in range(size)], here)
        self.forward = [(self.order[i], self.order[(i + 1) % size]) for i in range(size)]
        self.backward = [(b, a) for a, b in self.forward]

    def label(self, offset):
        return pick(self.order, (self.position + offset) % self.size)

    def labels(self, offsets):
        place = [self.order.index(i) for i in range(self.size)]
        return row_at(
            [[self.order[(place[i] + k) % self.size] for k in offsets] for i in range(self.size)],
            self.here,
        )

    def send(self, block, way):
        return lax.ppermute(block, "fsdp", self.forward if way > 0 else self.backward)

    def gather_parts(self, block):
        half = self.size // 2
        parts = [(0, block)]
        onward = backward = block
        for step in range(1, half):
            onward = self.send(onward, 1)
            backward = self.send(backward, -1)
            onward, backward = lax.optimization_barrier((onward, backward))
            parts += [(-step, onward), (step, backward)]
        cut = block.shape[0] // 2
        return parts, [self.send(onward[:cut], 1), self.send(backward[cut:], -1)]

    def gather(self, block):
        if self.native:
            full = lax.all_gather(block, "fsdp", axis=0)
            wide = full.reshape((8, self.size // 8, 4, -1, block.shape[1]))
            wide = wide.transpose(0, 2, 1, 3, 4).reshape(8, -1, block.shape[1])
            cut = wide.shape[1] // 2
            blocks = [wide[k] for k in range(8)]
            return blocks[:4] + [blocks[4][:cut], blocks[4][cut:]] + blocks[5:]
        parts, halves = self.gather_parts(block)
        parts = dict((offset % 8, part) for offset, part in parts)
        return [parts[k] for k in range(4)] + halves + [parts[k] for k in range(5, 8)]

    def scatter(self, part, stages):
        if self.native:
            for stage in stages:
                stage(part)
            return lax.psum_scatter(part, "fsdp", scatter_dimension=0, tiled=False).astype(f32)
        half = self.size // 2
        cut = part[half][0].shape[0]
        onward = self.send(part[half][0], 1)
        backward = self.send(part[half][1], -1)
        tokens = stages[0](part[half][0])
        for step in range(half - 1, 0, -1):
            onward, backward = after((onward, backward), *tokens)
            ahead = part[step].astype(f32)
            behind = part[self.size - step].astype(f32)
            if step == half - 1:
                ahead = jnp.concatenate([ahead[:cut] + onward.astype(f32), ahead[cut:]], axis=0)
                behind = jnp.concatenate(
                    [behind[:cut], behind[cut:] + backward.astype(f32)], axis=0
                )
            else:
                ahead = ahead + onward.astype(f32)
                behind = behind + backward.astype(f32)
            ahead, behind = ahead.astype(bf16), behind.astype(bf16)
            onward = self.send(ahead, 1)
            backward = self.send(behind, -1)
            tokens = stages[half - step](ahead)
        return part[0].astype(f32) + onward.astype(f32) + backward.astype(f32)


def tp_send(block, mask):
    return lax.ppermute(block, "tp", [(i, i ^ mask) for i in range(4)])


def tp_sum(values):
    return values + tp_send(values, 1) + tp_send(values, 2) + tp_send(values, 3)


def tp_rows_gather(piece, core, side):
    across = tp_send(piece, 2)
    blocks = [piece, tp_send(piece, 1), across, tp_send(across, 1)]
    blocks = [jnp.where(core == 1, blocks[i ^ 1], blocks[i]) for i in range(4)]
    blocks = [jnp.where(side == 1, blocks[i ^ 2], blocks[i]) for i in range(4)]
    return jnp.concatenate(blocks, axis=0)


def rotation_tables(count, row_width):
    position = np.arange(count, dtype=np.float32)[:, None]
    lane = np.arange(2 * row_width)[None, :]
    channel = (lane % row_width // 2).astype(np.float32)
    frequency = np.exp(-(2.0 * channel / row_width) * np.log(np.float32(10000.0)))
    angle = (position * frequency).astype(np.float32)
    zeta_base = (2.0 * channel + 0.4 * row_width) / (1.4 * row_width)
    growth = np.exp((position - count // 2) / 512.0 * np.log(zeta_base))
    cosine = np.cos(angle)
    sine = np.sin(angle) * np.where(lane % 2 == 0, -1.0, 1.0)
    tables = [cosine * growth, sine * growth, cosine / growth, sine / growth]
    return jnp.asarray(np.stack(tables).astype(np.float32))


def swapped(values):
    width = values.shape[1]
    lane = lax.broadcasted_iota(jnp.int32, values.shape, 1)
    return jnp.where(lane % 2 == 0, pltpu.roll(values, width - 1, 1), pltpu.roll(values, 1, 1))


def scores_of(query, key, limit, scale_value):
    raw = matmul(query, key, ((1,), (1,))) * scale_value
    row = lax.broadcasted_iota(jnp.int32, raw.shape, 0)
    column = lax.broadcasted_iota(jnp.int32, raw.shape, 1)
    scores = jnp.where((column <= row) & (column < limit), raw, -1e30)
    top = jnp.max(scores, axis=-1, keepdims=True)
    grown = jnp.exp(scores - top)
    return grown * (1.0 / jnp.sum(grown, axis=-1, keepdims=True))


def in_head(values, head, head_dim):
    lane = lax.broadcasted_iota(jnp.int32, values.shape, 1)
    return jnp.where(lane // head_dim == head, values, jnp.zeros_like(values))


def block_columns(labels, k, depth):
    return pl.ds(pl.multiple_of(labels[k] * depth, depth), depth)


def row_parts(rank, rows):
    core = lax.rem(rank, 2)
    return [
        [pl.ds(pl.multiple_of((2 * side + place) * rows, rows), rows) for side in range(2)]
        for place in (1 - core, core)
    ]


def attention_forward(labels, limits, x, *refs, slots, head_dim, scale):
    blocks, (bias, tables, q_out, k_out, v_out, o_out, sums) = refs[:9], refs[9:]
    depth = x.shape[1] // 8
    pairs = x.shape[0] // slots
    width = 2 * head_dim
    turned = []
    for c in range(3):
        total = bias[c : c + 1, :]
        for k in range(8):
            if k == 4:
                part = blocks[4 + c // 2][c % 2 * depth : (c % 2 + 1) * depth, :]
            else:
                part = blocks[k + k // 5][c * depth : (c + 1) * depth, :]
            total = total + matmul(x[:, block_columns(labels, k, depth)], part, ((1,), (0,)))
        turned.append(total)
    first = jnp.zeros((x.shape[0], 1), f32)
    square = jnp.zeros((x.shape[0], 1), f32)
    for j in range(q_out.shape[1] // width):
        lanes = slice(j * width, (j + 1) * width)
        for p in range(pairs):
            rows = slice(p * slots, (p + 1) * slots)
            q = turned[0][rows, lanes]
            q = q * tables[0] + swapped(q) * tables[1]
            k = turned[1][rows, lanes]
            k = (k * tables[2] + swapped(k) * tables[3]).astype(bf16)
            v = turned[2][rows, lanes].astype(bf16)
            q_out[rows, lanes] = q.astype(bf16)
            k_out[rows, lanes] = k
            v_out[rows, lanes] = v
            mixed = []
            for head in range(2):
                probs = scores_of(in_head(q, head, head_dim).astype(bf16), k, limits[p], scale)
                mixed.append(matmul(probs.astype(bf16), v, ((1,), (0,))))
            lane = lax.broadcasted_iota(jnp.int32, mixed[0].shape, 1)
            o_out[rows, lanes] = jnp.where(lane < head_dim, mixed[0], mixed[1])
    mixed = o_out[...]
    lane = lax.broadcasted_iota(jnp.int32, sums.shape, 1)
    partial = jnp.where(lane == 0, jnp.sum(mixed, axis=-1, keepdims=True), 0.0) + jnp.where(
        lane == 1, jnp.sum(mixed * mixed, axis=-1, keepdims=True), 0.0
    )

    @pl.when(pl.program_id(0) == 0)
    def _():
        sums[...] = partial

    @pl.when(pl.program_id(0) > 0)
    def _():
        sums[...] += partial


def attention_backward(
    limits, grad, mixed, coefficients, gain, tables, q_in, k_in, v_in, gq_out, gk_out, gv_out, sums, *, slots, head_dim, scale
):
    pairs = grad.shape[0] // slots
    width = 2 * head_dim
    mean, inverse = coefficients[:, 0:1], coefficients[:, 1:2]
    first, second = coefficients[:, 2:3], coefficients[:, 3:4]
    row = lax.broadcasted_iota(jnp.int32, (8, width), 0)
    for j in range(grad.shape[1] // width):
        lanes = slice(j * width, (j + 1) * width)
        total = jnp.zeros((8, width), f32)
        for p in range(pairs):
            rows = slice(p * slots, (p + 1) * slots)
            g = grad[rows, lanes]
            hat = (mixed[rows, lanes] - mean[rows]) * inverse[rows]
            total += jnp.where(row == 3, jnp.sum(g, axis=0, keepdims=True), 0.0)
            total += jnp.where(row == 4, jnp.sum(g * hat, axis=0, keepdims=True), 0.0)
            g = inverse[rows] * (g * gain[4:5, lanes] - first[rows] - hat * second[rows])
            q, k, v = q_in[rows, lanes].astype(f32), k_in[rows, lanes].astype(f32), v_in[rows, lanes]
            gq = jnp.zeros((slots, width), f32)
            gk = jnp.zeros((slots, width), f32)
            gv = jnp.zeros((slots, width), f32)
            for head in range(2):
                q_head = in_head(q, head, head_dim).astype(bf16)
                k_head = in_head(k, head, head_dim).astype(bf16)
                g_head = in_head(g, head, head_dim).astype(bf16)
                probs = scores_of(q_head, k_head, limits[p], scale)
                grad_probs = matmul(g_head, v, ((1,), (1,)))
                gv += matmul(probs.astype(bf16), g_head, ((0,), (0,)))
                spread = jnp.sum(probs * grad_probs, axis=-1, keepdims=True)
                grad_scores = (probs * (grad_probs - spread) * scale).astype(bf16)
                gq += matmul(grad_scores, k_head, ((1,), (0,)))
                gk += matmul(grad_scores, q_head, ((0,), (0,)))
            gq = (gq * tables[0] - swapped(gq) * tables[1]).astype(bf16)
            gk = (gk * tables[2] - swapped(gk) * tables[3]).astype(bf16)
            gv = gv.astype(bf16)
            gq_out[rows, lanes] = gq
            gk_out[rows, lanes] = gk
            gv_out[rows, lanes] = gv
            for index, part in enumerate((gq, gk, gv)):
                total += jnp.where(
                    row == index, jnp.sum(part.astype(f32), axis=0, keepdims=True), 0.0
                )
        sums[:, lanes] = total


def output_product(labels, rank, mixed, coefficients, gains, *refs):
    blocks, (away_out, kept_out, post_out) = refs[:8], refs[8:]
    depth = away_out.shape[1] // 8
    rows = away_out.shape[0] // 2
    hat = (mixed[...] - coefficients[:, 0:1]) * coefficients[:, 1:2]
    post_out[...] = (hat * gains[4:5, :] + gains[3:4, :]).astype(bf16)
    for out, slices in zip((away_out, kept_out), row_parts(rank[0], rows)):
        left = jnp.concatenate([post_out[part, :] for part in slices], axis=0)
        for k in range(8):
            product = matmul(left, blocks[k][...], ((1,), (1,)))
            out[:, block_columns(labels, k, depth)] = product.astype(out.dtype)


def output_back(labels, grad, mixed, coefficients, gains, *refs):
    blocks, (out, sums) = refs[:8], refs[8:]
    depth = grad.shape[1] // 8
    total = jnp.zeros(out.shape, f32)
    for k in range(8):
        total = total + matmul(
            grad[:, block_columns(labels, k, depth)], blocks[k][...], ((1,), (0,))
        )
    out[...] = total
    scaled = total * gains[4:5, :]
    hat = (mixed[...] - coefficients[:, 0:1]) * coefficients[:, 1:2]
    lane = lax.broadcasted_iota(jnp.int32, sums.shape, 1)
    sums[...] = jnp.where(lane == 0, jnp.sum(scaled, axis=-1, keepdims=True), 0.0) + jnp.where(
        lane == 1, jnp.sum(scaled * hat, axis=-1, keepdims=True), 0.0
    )


def projection_gradient(labels, x, grad, gq, gk, gv, post, out):
    depth = x.shape[1]
    for c, part in enumerate((gq, gk, gv)):
        out[0, c * depth : (c + 1) * depth, :] = matmul(x[...], part[...], ((0,), (0,))).astype(bf16)
    out[0, 3 * depth :, :] = matmul(grad[...], post[...], ((0,), (0,))).astype(bf16)


def projection_gradient_far(labels, x, grad, gq, gk, gv, post, first_out, second_out):
    depth = x.shape[1]
    first_out[:depth, :] = matmul(x[...], gq[...], ((0,), (0,))).astype(bf16)
    first_out[depth:, :] = matmul(x[...], gk[...], ((0,), (0,))).astype(bf16)
    second_out[:depth, :] = matmul(x[...], gv[...], ((0,), (0,))).astype(bf16)
    second_out[depth:, :] = matmul(grad[...], post[...], ((0,), (0,))).astype(bf16)


def projection_back(labels, rank, gq, gk, gv, *refs):
    blocks, (away_out, kept_out) = refs[:9], refs[9:]
    depth = away_out.shape[1] // 8
    rows = away_out.shape[0] // 2
    for out, slices in zip((away_out, kept_out), row_parts(rank[0], rows)):
        left = [
            jnp.concatenate([grad[part, :] for part in slices], axis=0) for grad in (gq, gk, gv)
        ]
        for k in range(8):
            total = jnp.zeros((2 * rows, depth), f32)
            for c in range(3):
                if k == 4:
                    part = blocks[4 + c // 2][c % 2 * depth : (c % 2 + 1) * depth, :]
                else:
                    part = blocks[k + k // 5][c * depth : (c + 1) * depth, :]
                total = total + matmul(left[c], part, ((1,), (1,)))
            out[:, block_columns(labels, k, depth)] = total.astype(out.dtype)


def columns_of(rows):
    return jnp.transpose(jnp.concatenate([rows] * 16, axis=0))


def ffn_forward(labels, x, g, vectors, *refs):
    blocks, (active_out, slope_out, grad_out, sums) = refs[:8], refs[8:]
    depth = x.shape[1] // 8
    before = vectors[0:1, :]
    grad = jnp.zeros(grad_out.shape, f32)
    for k in range(8):
        lanes = block_columns(labels, k, depth)
        before = before + matmul(x[:, lanes], blocks[k][:depth, :], ((1,), (0,)))
        grad = grad + matmul(g[:, lanes], blocks[k][depth:, :], ((1,), (0,)))
    below = 0.5 + 0.5 * lax.erf(before * math.sqrt(0.5))
    active = before * below
    active_out[...] = active
    slope_out[...] = below + before * (math.sqrt(0.5 / math.pi) * jnp.exp(-0.5 * before * before))
    grad_out[...] = grad
    scaled = grad * vectors[2:3, :]
    lane = lax.broadcasted_iota(jnp.int32, (grad.shape[0], 128), 1)
    columns = jnp.zeros((grad.shape[0], 128), f32)
    for index, values in enumerate((active, active * active, scaled, scaled * active)):
        columns += jnp.where(lane == index, jnp.sum(values, axis=-1, keepdims=True), 0.0)
    sums[...] = jnp.transpose(columns)[:8, :]


def ffn_backward(labels, sums, active, slope, grad, vectors, *refs, width):
    blocks, (before_out, post_out, out, totals) = refs[:8], refs[8:]
    columns = columns_of(sums[...])
    mean = columns[:, 0:1] / width
    inverse = lax.rsqrt(columns[:, 1:2] / width - mean * mean + norm_eps)
    hat_sum = inverse * (columns[:, 3:4] - mean * columns[:, 2:3])
    hat = (active[...] - mean) * inverse
    gain = vectors[2:3, :]
    post_out[...] = (hat * gain + vectors[1:2, :]).astype(bf16)
    moved = grad[...] * gain - columns[:, 2:3] / width - hat * (hat_sum / width)
    grad_before = (inverse * moved * slope[...]).astype(bf16)
    before_out[...] = grad_before
    product_into(labels, grad_before, blocks, out)
    row = lax.broadcasted_iota(jnp.int32, totals.shape, 0)
    partial = jnp.zeros(totals.shape, f32)
    for index, values in enumerate((grad_before.astype(f32), grad[...], grad[...] * hat)):
        partial += jnp.where(row == index, jnp.sum(values, axis=0, keepdims=True), 0.0)

    @pl.when(pl.program_id(0) == 0)
    def _():
        totals[...] = partial

    @pl.when(pl.program_id(0) > 0)
    def _():
        totals[...] += partial


def product_into(labels, left, blocks, out):
    depth = out.shape[1] // 8
    for k in range(8):
        product = matmul(left, blocks[k][...], ((1,), (1,)))
        out[:, block_columns(labels, k, depth)] = product.astype(bf16)


def ffn_product(labels, left, *refs):
    product_into(labels, left[...], refs[:8], refs[8])


def ffn_gradient(labels, near_x, far_x, near_g, far_g, near_before, far_before, near_post, far_post, *outs):
    depth = near_x.shape[1]
    totals = []
    for c, (near, far, near_right, far_right) in enumerate(
        ((near_x, far_x, near_before, far_before), (near_g, far_g, near_post, far_post))
    ):
        total = matmul(near[...], near_right[...], ((0,), (0,)))
        total = total + matmul(far[...], far_right[...], ((0,), (0,)))
        totals.append(total.astype(bf16))
    for k, out in enumerate(outs):

        @pl.when(pl.program_id(0) == k)
        def _(out=out):
            for c, total in enumerate(totals):
                out[c * depth : (c + 1) * depth, :] = total


def ffn_placed(groups, *refs):
    blocks, (first_out, second_out) = refs[:4], refs[4:]
    depth, width = blocks[0].shape[0] // 2, blocks[0].shape[1]
    for k in range(4):
        place = pl.ds(pl.multiple_of(groups[k] * width, width), width)
        first_out[:, place] = blocks[k][:depth, :].astype(f32)
        second_out[place, :] = jnp.transpose(blocks[k][depth:, :].astype(f32))


def cost(flops, moved, exponentials=0):
    return pl.CostEstimate(flops=flops, bytes_accessed=moved, transcendentals=exponentials)


def norm_stats(first_sum, square_sum, row_width):
    mean_value = first_sum / row_width
    variance = square_sum / row_width - mean_value * mean_value
    return mean_value, lax.rsqrt(variance + norm_eps)


def norm_rows(values, gain_vector, shift_vector):
    width = values.shape[-1]
    mean_value, inverse = norm_stats(
        jnp.sum(values, axis=-1, keepdims=True),
        jnp.sum(values * values, axis=-1, keepdims=True),
        width,
    )
    hat = (values - mean_value) * inverse
    return hat * gain_vector + shift_vector, hat, inverse


def norm_back_rows(scaled, hat, inverse):
    width = scaled.shape[-1]
    return inverse * (
        scaled
        - jnp.sum(scaled, axis=-1, keepdims=True) / width
        - hat * jnp.sum(scaled * hat, axis=-1, keepdims=True) / width
    )


def matmul(a, b, dims):
    return lax.dot_general(a, b, (dims, ((), ())), preferred_element_type=f32)


def per_device(
    tokens,
    cotangent,
    caption_lengths,
    w_qkv,
    head_biases,
    head_gain,
    w_out,
    model_gains,
    model_biases,
    w_fc1,
    w_fc2,
    ffn_gain,
    ffn_biases,
    *,
    fsdp_size,
):
    here = lax.axis_index("fsdp")
    rank = lax.axis_index("tp")
    core, side = rank % 2, rank // 2
    others = fsdp_size // GROUPS
    group, member = here // others, here % others
    ring = Ring(fsdp_size, here)
    group_lists = [[g * others + o for g in range(GROUPS)] for o in range(others)]
    member_lists = [[g * others + o for o in range(others)] for g in range(GROUPS)]

    def group_send(block, shift):
        return lax.ppermute(
            block,
            "fsdp",
            [
                (g * others + o, (g + shift) % GROUPS * others + o)
                for g in range(GROUPS)
                for o in range(others)
            ],
        )

    def group_swap(blocks):
        return lax.all_to_all(blocks, "fsdp", 0, 0, axis_index_groups=group_lists)

    def pair_send(block):
        return lax.ppermute(block, "fsdp", [(f, f ^ 1) for f in range(fsdp_size)])

    def member_gather(blocks):
        if others == 2:
            theirs = pair_send(blocks)
            return jnp.stack(
                [jnp.where(member == 0, blocks, theirs), jnp.where(member == 0, theirs, blocks)],
                axis=1,
            )
        full = lax.all_gather(blocks, "fsdp", axis=0, axis_index_groups=member_lists)
        return jnp.moveaxis(full, 0, 1)

    def member_scatter(blocks):
        if others == 2:
            sent = pair_send(block_at(blocks, 1 - member, 1))
            return block_at(blocks, member, 1).astype(f32) + sent.astype(f32)
        return lax.psum_scatter(
            blocks, "fsdp", scatter_dimension=1, axis_index_groups=member_lists, tiled=False
        ).astype(f32)

    pair_count = caption_lengths.shape[0]
    row_count, model_width = tokens.shape
    slot_count = row_count // pair_count
    sub_rows = row_count // 4
    head_dim = model_width // HEADS
    local_width = w_qkv.shape[2]
    block_rows = w_qkv.shape[0]
    hidden_width = FF
    local_hidden = w_fc1.shape[1] // GROUPS

    model_part = jnp.concatenate([model_gains, model_biases], axis=0)
    head_part = jnp.concatenate([head_biases, head_gain[None]], axis=0)
    unit_part = jnp.concatenate([ffn_biases, ffn_gain[None]], axis=0)
    packed = jnp.concatenate([model_part.reshape(-1), head_part.reshape(-1), unit_part.reshape(-1)])
    vectors = lax.all_to_all(
        jnp.broadcast_to(packed[None], (fsdp_size, packed.shape[0])), "fsdp", 0, 0
    )
    sizes = [model_part.size, head_part.size, unit_part.size]
    model_vectors = (
        vectors[:, : sizes[0]].reshape((fsdp_size,) + model_part.shape).transpose(1, 0, 2)
    ).reshape(6, model_width).astype(f32)
    head_vectors = (
        vectors[:, sizes[0] : sizes[0] + sizes[1]]
        .reshape((fsdp_size,) + head_part.shape)
        .transpose(1, 0, 2)
    ).reshape(5, local_width).astype(f32)
    unit_all = vectors[:, sizes[0] + sizes[1] :].reshape((GROUPS, others) + unit_part.shape)
    unit_vectors = block_at(unit_all, group).transpose(1, 0, 2).reshape(3, local_hidden).astype(f32)

    def rows_gather(piece, *tokens):
        pieces = [piece] + [group_send(piece, shift) for shift in range(1, GROUPS)]
        across = [tp_send(piece, 2)]
        pieces[1] = after(pieces[1], across[0])
        across += [tp_send(part, 2) for part in pieces[1:]]
        near = after(jnp.concatenate(pieces + across, axis=0), *tokens)
        return near, tp_send(near, 1)

    def core_sum(away, kept):
        return (kept + tp_send(away, 1).astype(f32)).reshape(2, sub_rows, -1)

    def side_sum(total):
        crossing = tp_send(block_at(total, 1 - side).astype(bf16), 2)
        return block_at(total, side) + crossing.astype(f32)

    def group_core(far, near):
        total = near.astype(f32) + tp_send(far, 1).astype(f32)
        return total.reshape(2, GROUPS, sub_rows, -1)

    def group_shares(total):
        return total[0] + tp_send(total[1].astype(bf16), 2).astype(f32)

    def group_shares_piped(total):
        return {k: total[0, k] + tp_send(total[1, k].astype(bf16), 2).astype(f32) for k in (2, 1, 3, 0)}

    def group_total(shares):
        sent = [group_send(shares[k].astype(bf16), -k).astype(f32) for k in (2, 1, 3)]
        return shares[0], sent

    def group_sum(values):
        def swap(array, width):
            pieces = [array[:, i : i + width] for i in range(0, array.shape[1], width)]
            pieces = [pieces[i ^ 1] for i in range(len(pieces))]
            return jnp.concatenate(pieces, axis=1)

        half_rows = 2 * GROUPS * sub_rows
        flip_core = tp_send(values, 1)
        flip_side = tp_send(values, 2)
        flip_both = tp_send(values, 3)
        values = values + swap(flip_core + swap(flip_both, half_rows // 2), half_rows)
        values = values + swap(flip_side, half_rows // 2)
        total = values
        for shift in range(1, GROUPS):
            part = group_send(values, shift).reshape(8, 4, GROUPS * sub_rows)
            cut = (GROUPS - shift) * sub_rows
            part = jnp.concatenate([part[:, :, cut:], part[:, :, :cut]], axis=2)
            total = total + part.reshape(8, -1)
        return total

    def my_rows(array):
        return lax.dynamic_slice_in_dim(array, rank * sub_rows, sub_rows, 0)

    slot_index = jnp.arange(slot_count)[None, :]
    key_valid = slot_index < IMAGE + caption_lengths[:, None]
    keep_rows = key_valid.reshape(row_count).astype(f32)[:, None]
    my_keep = my_rows(keep_rows)
    my_grad_out = my_rows(cotangent).astype(f32) * my_keep
    depth = model_width // 8
    own_block = jnp.concatenate([w_qkv[:, c] for c in range(3)] + [w_out.T], axis=0)
    blocks = ring.gather(own_block)
    labels = jnp.arange(8, dtype=jnp.int32) if ring.native else ring.labels(range(8))

    fc_pieces = jnp.concatenate(
        [w.reshape(block_rows, GROUPS, local_hidden) for w in (w_fc1, w_fc2.T)], axis=0
    )
    fc_pieces = after(fc_pieces.transpose(1, 0, 2), blocks[3])
    fc_mine = [block_at(fc_pieces, group)]
    for shift in (1, 3, 2):
        fc_mine.append(group_send(block_at(fc_pieces, (group + shift) % GROUPS), shift))
    fc_received = list(fc_mine)
    if others == 2:
        fc_theirs = [pair_send(part) for part in fc_mine]
        fc_labels = row_at(
            [
                [(f // 2 - k) % GROUPS * 2 + f % 2 for k in (0, 1, 3, 2)]
                + [(f // 2 - k) % GROUPS * 2 + 1 - f % 2 for k in (0, 1, 3, 2)]
                for f in range(fsdp_size)
            ],
            here,
        )
    else:
        full = jnp.zeros(fc_pieces.shape, bf16)
        for shift, part in zip((0, 1, 3, 2), fc_mine):
            full = put(full, part, (group - shift) % GROUPS)
        full = lax.all_gather(full, "fsdp", axis=0, axis_index_groups=member_lists)
        full = full.reshape(others, GROUPS, 2, block_rows, local_hidden).transpose(2, 1, 0, 3, 4)
        full = full.reshape(2, 8, depth, local_hidden).transpose(1, 0, 2, 3)
        full = full.reshape(8, 2 * depth, local_hidden)
        fc_mine, fc_theirs = [full[k] for k in range(4)], [full[k] for k in range(4, 8)]
        fc_labels = jnp.arange(8)
    fc_labels = fc_labels.astype(jnp.int32)
    fc_blocks = fc_mine + fc_theirs
    cotangent_rows = after(my_grad_out.astype(bf16), fc_received[3])
    cotangent_rows = [cotangent_rows] + [
        group_send(cotangent_rows, shift) for shift in range(1, GROUPS)
    ]

    tables = rotation_tables(slot_count, head_dim)
    limits = IMAGE + caption_lengths
    scale_value = 1.0 / math.sqrt(head_dim)
    normed_in, _, _ = norm_rows(tokens.astype(f32), model_vectors[0], model_vectors[2])
    normed_in_b = normed_in.astype(bf16)
    part_width = 4 * head_dim
    parts = local_width // part_width
    scalars = pl.BlockSpec(memory_space=pltpu.SMEM)

    def whole(shape, first=0):
        return pl.BlockSpec(shape, lambda j: (first,) + (0,) * (len(shape) - 1))

    def columns(rows):
        return pl.BlockSpec((rows, part_width), lambda j: (0, j))

    def projection_specs(width, index_map):
        full = pl.BlockSpec((3 * depth, width), index_map)
        return [full] * 4 + [pl.BlockSpec((2 * depth, width), index_map)] * 2 + [full] * 3

    out_row = whole((depth, local_width), 3)
    out_specs = [out_row] * 4 + [whole((depth, local_width), 1)] + [out_row] * 3
    out_blocks = blocks[:4] + blocks[5:]
    rank_array = rank.astype(jnp.int32)[None]
    big = pltpu.CompilerParams(vmem_limit_bytes=58 << 20)
    queries, keys_rot, values_in, heads_out, head_sums = pl.pallas_call(
        functools.partial(
            attention_forward, slots=slot_count, head_dim=head_dim, scale=scale_value
        ),
        grid=(parts,),
        in_specs=[scalars, scalars, whole((row_count, model_width))]
        + projection_specs(part_width, lambda j: (0, j))
        + [columns(5), whole((4, slot_count, 2 * head_dim))],
        out_specs=[columns(row_count)] * 4 + [whole((row_count, 128))],
        out_shape=[jax.ShapeDtypeStruct((row_count, local_width), bf16)] * 3
        + [
            jax.ShapeDtypeStruct((row_count, local_width), f32),
            jax.ShapeDtypeStruct((row_count, 128), f32),
        ],
        compiler_params=big,
        cost_estimate=cost(2 * row_count * model_width * 3 * local_width, 12 << 20, 1 << 20),
        name="attention_forward",
    )(labels, limits, normed_in_b, *blocks, head_vectors, tables)
    head_stats = tp_sum(head_sums[:, :2].T)
    mean_attn, inverse_attn = norm_stats(
        head_stats[0][:, None], head_stats[1][:, None], model_width
    )
    coefficients = jnp.concatenate([mean_attn, inverse_attn], axis=1)
    halves = [
        jax.ShapeDtypeStruct((2 * sub_rows, model_width), bf16),
        jax.ShapeDtypeStruct((2 * sub_rows, model_width), f32),
    ]
    half_specs = [whole((2 * sub_rows, model_width))] * 2
    away, kept, post_attn_b = pl.pallas_call(
        output_product,
        grid=(1,),
        in_specs=[
            scalars,
            scalars,
            whole((row_count, local_width)),
            whole((row_count, 2)),
            whole((5, local_width)),
        ]
        + out_specs,
        out_specs=half_specs + [whole((row_count, local_width))],
        out_shape=halves + [jax.ShapeDtypeStruct((row_count, local_width), bf16)],
        compiler_params=big,
        cost_estimate=cost(2 * row_count * model_width * local_width, 5 << 20),
        name="output_product",
    )(labels, rank_array, after(heads_out, *fc_received[1:], fc_theirs[0]), coefficients, head_vectors, *out_blocks)
    branch = side_sum(core_sum(away, kept))
    middle = my_rows(tokens).astype(f32) + branch + model_vectors[4]
    normed_mid, hat_mid, inverse_mid = norm_rows(middle, model_vectors[1], model_vectors[3])

    cotangent_near = after(jnp.concatenate(cotangent_rows, axis=0), branch)
    cotangent_near = jnp.concatenate([cotangent_near, tp_send(cotangent_near, 2)], axis=0)
    grad_out_all = (cotangent_near, tp_send(cotangent_near, 1))
    normed_mid_all = rows_gather(
        after(normed_mid.astype(bf16), *cotangent_rows), *fc_theirs[1:]
    )
    half_rows = 2 * GROUPS * sub_rows
    step_rows = half_rows // 2

    def rows(width):
        return pl.BlockSpec((step_rows, width), lambda j: (j, 0))

    fc_half = [[whole((depth, local_hidden), start)] * 8 for start in range(2)]
    half_shape = jax.ShapeDtypeStruct((half_rows, local_hidden), f32)
    half_shape_b = jax.ShapeDtypeStruct((half_rows, local_hidden), bf16)
    product_shape = jax.ShapeDtypeStruct((half_rows, model_width), bf16)

    def forward_half(x, g):
        return pl.pallas_call(
            ffn_forward,
            grid=(2,),
            in_specs=[scalars, rows(model_width), rows(model_width), whole((3, local_hidden))]
            + [whole((2 * depth, local_hidden))] * 8,
            out_specs=[rows(local_hidden)] * 3 + [pl.BlockSpec((8, step_rows), lambda j: (0, j))],
            out_shape=[half_shape] * 3 + [jax.ShapeDtypeStruct((8, half_rows), f32)],
            compiler_params=big,
            cost_estimate=cost(4 * half_rows * model_width * local_hidden, 10 << 20, 1 << 20),
            name="ffn_forward",
        )(fc_labels, x, g, unit_vectors, *fc_blocks)

    *hidden_near, sums_near = forward_half(normed_mid_all[0], grad_out_all[0])
    *hidden_far, sums_far = forward_half(normed_mid_all[1], grad_out_all[1])
    sums = group_sum(jnp.concatenate([sums_near, sums_far], axis=1))

    def backward_half(index, hidden):
        return pl.pallas_call(
            functools.partial(ffn_backward, width=hidden_width),
            grid=(2,),
            in_specs=[scalars, pl.BlockSpec((8, step_rows), lambda j: (0, j + 2 * index))]
            + [rows(local_hidden)] * 3
            + [whole((3, local_hidden))]
            + fc_half[0],
            out_specs=[rows(local_hidden)] * 2 + [rows(model_width), whole((8, local_hidden))],
            out_shape=[half_shape_b] * 2
            + [product_shape, jax.ShapeDtypeStruct((8, local_hidden), f32)],
            compiler_params=big,
            cost_estimate=cost(2 * half_rows * model_width * local_hidden, 8 << 20),
            name="ffn_backward",
        )(fc_labels, sums, *hidden, unit_vectors, *fc_blocks)

    before_far, post_far, mid_far, totals_far = backward_half(1, hidden_far)
    before_near, post_near, mid_near, totals_near = backward_half(0, hidden_near)

    def second_half(post):
        return pl.pallas_call(
            ffn_product,
            grid=(2,),
            in_specs=[scalars, rows(local_hidden)] + fc_half[1],
            out_specs=rows(model_width),
            out_shape=product_shape,
            compiler_params=big,
            cost_estimate=cost(2 * half_rows * model_width * local_hidden, 5 << 20),
            name="ffn_product",
        )(fc_labels, post, *fc_blocks)

    mid_total = group_core(mid_far, mid_near)
    shares = group_shares_piped(mid_total)
    unit_s = member_scatter((totals_near + totals_far)[:3].reshape(3, others, -1))

    fc_order = (2, 1, 3, 0)

    def fc_gradient(order, token):
        return pl.pallas_call(
            ffn_gradient,
            grid_spec=pltpu.PrefetchScalarGridSpec(
                num_scalar_prefetch=1,
                grid=(4,),
                in_specs=[pl.BlockSpec((half_rows, depth), lambda j, label: (0, label[j]))] * 4
                + [pl.BlockSpec((half_rows, local_hidden), lambda j, label: (0, 0))] * 4,
                out_specs=[pl.BlockSpec((2 * depth, local_hidden), lambda j, label: (0, 0))] * 4,
            ),
            out_shape=[jax.ShapeDtypeStruct((2 * depth, local_hidden), bf16)] * 4,
            compiler_params=big,
            cost_estimate=cost(4 * half_rows * model_width * local_hidden, 9 << 20),
            name="ffn_gradient",
        )(
            order.astype(jnp.int32),
            *normed_mid_all,
            *grad_out_all,
            before_near,
            before_far,
            *after((post_near, post_far), token),
        )

    if others == 2:
        ahead = [[(f // 2 + k) % GROUPS * 2 for k in fc_order] for f in range(fsdp_size)]
        away_labels = row_at([[a + 1 - f % 2 for a in row] for f, row in enumerate(ahead)], here)
        kept_labels = row_at([[a + f % 2 for a in row] for f, row in enumerate(ahead)], here)
        fc_away = fc_gradient(away_labels, mid_total)
        fc_kept = fc_gradient(kept_labels, shares[2])
        fc_sent = [pair_send(part) for part in fc_away]
        fc_summed = [
            (kept.astype(f32) + sent.astype(f32)).astype(bf16)
            for kept, sent in zip(fc_kept, fc_sent)
        ]
    else:
        fc_away = fc_gradient(jnp.arange(4), mid_total)
        fc_kept = fc_gradient(jnp.arange(4, 8), shares[2])
        fc_grads = jnp.stack(fc_away + fc_kept)
        fc_grads = fc_grads.reshape(8, 2, depth, local_hidden).transpose(1, 0, 2, 3)
        fc_grads = fc_grads.reshape(2, GROUPS, others, block_rows, local_hidden)
        fc_grads = fc_grads.transpose(1, 2, 0, 3, 4).reshape(GROUPS, others, -1, local_hidden)
        fc_grads = member_scatter(fc_grads).astype(bf16)
        fc_summed = [block_at(fc_grads, (group + shift) % GROUPS) for shift in fc_order]
        fc_sent = fc_summed

    shares[1], shares[3] = after((shares[1], shares[3]), *fc_away)
    own, sent = group_total(shares)
    own = after(own, fc_kept[0], *fc_sent[:3], unit_s)
    grad_mid_normed = own + sent[0] + sent[1] + sent[2]
    grad_middle = my_grad_out + norm_back_rows(
        grad_mid_normed * model_vectors[1], hat_mid, inverse_mid
    )
    grad_middle_b = tp_rows_gather(grad_middle.astype(bf16), core, side)
    fc_spread = [group_send(part, k) if k else part for k, part in zip(fc_order, fc_summed)]

    grad_post_attn, back_sums = pl.pallas_call(
        output_back,
        grid=(1,),
        in_specs=[
            scalars,
            whole((row_count, model_width)),
            whole((row_count, local_width)),
            whole((row_count, 2)),
            whole((5, local_width)),
        ]
        + out_specs,
        out_specs=[whole((row_count, local_width)), whole((row_count, 128))],
        out_shape=[
            jax.ShapeDtypeStruct((row_count, local_width), f32),
            jax.ShapeDtypeStruct((row_count, 128), f32),
        ],
        compiler_params=big,
        cost_estimate=cost(2 * row_count * model_width * local_width, 5 << 20),
        name="output_back",
    )(labels, after(grad_middle_b, fc_sent[3]), heads_out, coefficients, head_vectors, *out_blocks)
    head_back = tp_sum(back_sums[:, :2].T)[:, :, None]
    coefficients = jnp.concatenate(
        [coefficients, head_back[0] / model_width, head_back[1] / model_width], axis=1
    )
    *grad_linear, head_sums_back = pl.pallas_call(
        functools.partial(
            attention_backward, slots=slot_count, head_dim=head_dim, scale=scale_value
        ),
        grid=(parts,),
        in_specs=[
            scalars,
            columns(row_count),
            columns(row_count),
            whole((row_count, 4)),
            columns(5),
            whole((4, slot_count, 2 * head_dim)),
            columns(row_count),
            columns(row_count),
            columns(row_count),
        ],
        out_specs=[columns(row_count)] * 3 + [columns(8)],
        out_shape=[jax.ShapeDtypeStruct((row_count, local_width), bf16)] * 3
        + [jax.ShapeDtypeStruct((8, local_width), f32)],
        compiler_params=pltpu.CompilerParams(vmem_limit_bytes=40 << 20),
        cost_estimate=cost(10 * row_count * slot_count * 2 * local_width, 4 << 20, 1 << 20),
        name="attention_backward",
    )(
        limits,
        after(grad_post_attn, fc_spread[0]),
        heads_out,
        coefficients,
        head_vectors,
        tables,
        queries,
        keys_rot,
        values_in,
    )
    def weight_gradients(kernel, count, order, out_specs, out_shape):
        return pl.pallas_call(
            kernel,
            grid_spec=pltpu.PrefetchScalarGridSpec(
                num_scalar_prefetch=1,
                grid=(count,),
                in_specs=[pl.BlockSpec((row_count, depth), lambda j, label: (0, label[j]))] * 2
                + [pl.BlockSpec((row_count, local_width), lambda j, label: (0, 0))] * 4,
                out_specs=out_specs,
            ),
            out_shape=out_shape,
            compiler_params=big,
            cost_estimate=cost(count * row_count * depth * 8 * local_width, count << 20),
            name=kernel.__name__,
        )(order, normed_in_b, grad_middle_b, *grad_linear, post_attn_b)

    far_grads = weight_gradients(
        projection_gradient_far,
        1,
        labels[4:5],
        [pl.BlockSpec((2 * depth, local_width), lambda j, label: (0, 0))] * 2,
        [jax.ShapeDtypeStruct((2 * depth, local_width), bf16)] * 2,
    )
    order = [0, 3, 5, 2, 6, 1, 7]
    weight_grads = weight_gradients(
        projection_gradient,
        7,
        jnp.asarray(order, jnp.int32) if ring.native else ring.labels(order),
        pl.BlockSpec((1, 4 * depth, local_width), lambda j, label: (j, 0, 0)),
        jax.ShapeDtypeStruct((7, 4 * depth, local_width), bf16),
    )
    weight_grads = dict((k, weight_grads[j]) for j, k in enumerate(order))
    weight_grads[4] = far_grads
    if ring.native:
        weight_grads[4] = jnp.concatenate(far_grads, axis=0)
        weight_grads = jnp.stack([weight_grads[k] for k in range(8)])
        weight_grads = weight_grads.reshape(8, 4, fsdp_size // 8, block_rows, local_width)
        weight_grads = weight_grads.transpose(0, 2, 1, 3, 4).reshape(fsdp_size, -1, local_width)
    placed_rows = (block_rows, GROUPS * local_hidden)
    def place_ffn(token):
        return pl.pallas_call(
            ffn_placed,
            grid=(1,),
            in_specs=[scalars] + [whole((2 * block_rows, local_hidden))] * 4,
            out_specs=[whole(placed_rows), whole(placed_rows[::-1])],
            out_shape=[
                jax.ShapeDtypeStruct(placed_rows, f32),
                jax.ShapeDtypeStruct(placed_rows[::-1], f32),
            ],
            compiler_params=big,
            cost_estimate=cost(0, 6 << 20),
            name="ffn_placed",
        )(
            row_at([[(f // others - k) % GROUPS for k in fc_order] for f in range(fsdp_size)], here),
            *after(tuple(fc_spread), token),
        )

    results = {}

    def while_half(token):
        results["parts"] = [second_half(after(post, token)) for post in (post_far, post_near)]
        return fc_spread + results["parts"]

    def while_first(token):
        back_away, back_kept = pl.pallas_call(
            projection_back,
            grid=(1,),
            in_specs=[scalars, scalars]
            + [whole((row_count, local_width))] * 3
            + projection_specs(local_width, lambda j: (0, 0)),
            out_specs=half_specs,
            out_shape=halves,
            compiler_params=big,
            cost_estimate=cost(2 * row_count * model_width * 3 * local_width, 10 << 20),
            name="projection_back",
        )(labels, rank_array, *after(tuple(grad_linear), token), *blocks)
        results["back"] = back_away, back_kept
        results["core"] = group_core(*after(tuple(results["parts"]), token))
        return back_away, back_kept, results["core"]

    def while_second(token):
        grad_in_normed = side_sum(core_sum(*after(results["back"], token)))
        _, hat_in, inverse_in = norm_rows(
            my_rows(tokens).astype(f32), model_vectors[0], model_vectors[2]
        )
        grad_token_rows = grad_middle + norm_back_rows(
            grad_in_normed * model_vectors[0], hat_in, inverse_in
        )
        results["model"] = tp_sum(
            jnp.stack(
                [
                    jnp.sum(grad_in_normed * hat_in, axis=0),
                    jnp.sum(grad_mid_normed * hat_mid, axis=0),
                    jnp.sum(grad_in_normed, axis=0),
                    jnp.sum(grad_mid_normed, axis=0),
                    jnp.sum(grad_middle, axis=0),
                    jnp.sum(my_grad_out, axis=0),
                ]
            )
        )
        results["shares"] = group_shares(after(results["core"], token))
        results["tokens"] = grad_token_rows
        results["placed"] = place_ffn(token)
        return [results["model"], results["tokens"], results["shares"]] + list(results["placed"])

    def by_block(vectors_in, blocks_in):
        return vectors_in.reshape(vectors_in.shape[0], blocks_in, -1).transpose(1, 0, 2)

    def while_third(token):
        model_grads, token_rows, shares = after(
            (results["model"], results["tokens"], results["shares"]), token
        )
        model_blocks = by_block(model_grads, fsdp_size).reshape(fsdp_size, -1)
        head_blocks = by_block(head_sums_back[:5], fsdp_size).reshape(fsdp_size, -1)
        joined = jnp.concatenate([model_blocks, head_blocks], axis=1)
        joined_s = jnp.sum(lax.all_to_all(joined, "fsdp", 0, 0), axis=0)
        results["model_s"] = joined_s[: model_blocks.shape[1]].reshape(6, -1)
        results["head_s"] = joined_s[model_blocks.shape[1] :].reshape(5, -1)
        results["grad_tokens"] = tp_rows_gather(token_rows, core, side)
        own, sent = group_total(shares)
        own = after(own, joined_s, results["grad_tokens"])
        second = own + sent[0] + sent[1] + sent[2]
        out_rows = ((middle + second + model_vectors[5]) * my_keep).astype(bf16)
        results["layer_out"] = tp_rows_gather(out_rows, core, side)
        return ()

    weights_s = ring.scatter(weight_grads, [while_half, while_first, while_second, while_third])
    weights_s = weights_s.reshape(4, block_rows, local_width)
    grad_qkv_s = weights_s[:3].transpose(1, 0, 2)
    grad_out_s = weights_s[3]
    return (
        results["layer_out"],
        results["grad_tokens"],
        grad_qkv_s,
        results["head_s"][:4],
        results["head_s"][4],
        grad_out_s.T,
        results["model_s"][:2],
        results["model_s"][2:],
        *results["placed"],
        unit_s[2],
        unit_s[:2],
    )


def solution(mesh):
    placed = (
        P("fsdp", None),
        P("fsdp", None),
        P("fsdp"),
        P("fsdp", None, "tp"),
        P(None, ("tp", "fsdp")),
        P(("tp", "fsdp")),
        P("tp", "fsdp"),
        P(None, "fsdp"),
        P(None, "fsdp"),
        P("fsdp", "tp"),
        P("tp", "fsdp"),
        P(("tp", "fsdp")),
        P(None, ("tp", "fsdp")),
    )
    return jax.shard_map(
        functools.partial(per_device, fsdp_size=mesh.shape["fsdp"]),
        mesh=mesh,
        in_specs=placed,
        out_specs=(
            P("fsdp", None),
            P("fsdp", None),
            P("fsdp", None, "tp"),
            P(None, ("tp", "fsdp")),
            P(("tp", "fsdp")),
            P("tp", "fsdp"),
            P(None, "fsdp"),
            P(None, "fsdp"),
            P("fsdp", "tp"),
            P("tp", "fsdp"),
            P(("tp", "fsdp")),
            P(None, ("tp", "fsdp")),
        ),
        check_vma=False,
    )
```

```python
import functools
import math

import jax
import jax.numpy as jnp
import numpy as np
from jax import lax
from jax.experimental import pallas as pl
from jax.experimental.pallas import tpu as pltpu
from jax.sharding import PartitionSpec as P

HEADS = 32
FF = 8192
IMAGE = 64
GROUPS = 4

f32 = jnp.float32
bf16 = jnp.bfloat16
norm_eps = 1e-05


def pick(table, index):
    return lax.dynamic_index_in_dim(jnp.asarray(table, jnp.int32), index, keepdims=False)


def row_at(table, index):
    return lax.dynamic_index_in_dim(jnp.asarray(table, jnp.int32), index, keepdims=False)


def put(buffer, block, index):
    return lax.dynamic_update_slice(buffer, block[None], (index,) + (0,) * block.ndim)


def block_at(array, index, axis=0):
    return lax.dynamic_index_in_dim(array, index, axis, keepdims=False)


def after(value, *tokens):
    return lax.optimization_barrier((value,) + tokens)[0]


class Ring:
    def __init__(self, size, here):
        self.size = size
        self.here = here
        self.native = size > 8
        self.order = list(range(0, size, 2)) + list(range(size - 1, 0, -2))
        self.position = pick([self.order.index(i) for i in range(size)], here)
        self.forward = [(self.order[i], self.order[(i + 1) % size]) for i in range(size)]
        self.backward = [(b, a) for a, b in self.forward]

    def label(self, offset):
        return pick(self.order, (self.position + offset) % self.size)

    def labels(self, offsets):
        place = [self.order.index(i) for i in range(self.size)]
        return row_at(
            [[self.order[(place[i] + k) % self.size] for k in offsets] for i in range(self.size)],
            self.here,
        )

    def send(self, block, way):
        return lax.ppermute(block, "fsdp", self.forward if way > 0 else self.backward)

    def gather_parts(self, block):
        half = self.size // 2
        parts = [(0, block)]
        onward = backward = block
        for step in range(1, half):
            onward = self.send(onward, 1)
            backward = self.send(backward, -1)
            onward, backward = lax.optimization_barrier((onward, backward))
            parts += [(-step, onward), (step, backward)]
        cut = block.shape[0] // 2
        return parts, [self.send(onward[:cut], 1), self.send(backward[cut:], -1)]

    def gather(self, block):
        if self.native:
            full = lax.all_gather(block, "fsdp", axis=0)
            wide = full.reshape((8, self.size // 8, 4, -1, block.shape[1]))
            wide = wide.transpose(0, 2, 1, 3, 4).reshape(8, -1, block.shape[1])
            cut = wide.shape[1] // 2
            blocks = [wide[k] for k in range(8)]
            return blocks[:4] + [blocks[4][:cut], blocks[4][cut:]] + blocks[5:]
        parts, halves = self.gather_parts(block)
        parts = dict((offset % 8, part) for offset, part in parts)
        return [parts[k] for k in range(4)] + halves + [parts[k] for k in range(5, 8)]

    def scatter(self, part, stages):
        if self.native:
            for stage in stages:
                stage(part)
            return lax.psum_scatter(part, "fsdp", scatter_dimension=0, tiled=False).astype(f32)
        half = self.size // 2
        cut = part[half][0].shape[0]
        onward = self.send(part[half][0], 1)
        backward = self.send(part[half][1], -1)
        tokens = stages[0](part[half][0])
        for step in range(half - 1, 0, -1):
            onward, backward = after((onward, backward), *tokens)
            ahead = part[step].astype(f32)
            behind = part[self.size - step].astype(f32)
            if step == half - 1:
                ahead = jnp.concatenate([ahead[:cut] + onward.astype(f32), ahead[cut:]], axis=0)
                behind = jnp.concatenate(
                    [behind[:cut], behind[cut:] + backward.astype(f32)], axis=0
                )
            else:
                ahead = ahead + onward.astype(f32)
                behind = behind + backward.astype(f32)
            ahead, behind = ahead.astype(bf16), behind.astype(bf16)
            onward = self.send(ahead, 1)
            backward = self.send(behind, -1)
            tokens = stages[half - step](ahead)
        return part[0].astype(f32) + onward.astype(f32) + backward.astype(f32)


def tp_send(block, mask):
    return lax.ppermute(block, "tp", [(i, i ^ mask) for i in range(4)])


def tp_sum(values):
    return values + tp_send(values, 1) + tp_send(values, 2) + tp_send(values, 3)


def tp_rows_gather(piece, core, side):
    across = tp_send(piece, 2)
    blocks = [piece, tp_send(piece, 1), across, tp_send(across, 1)]
    blocks = [jnp.where(core == 1, blocks[i ^ 1], blocks[i]) for i in range(4)]
    blocks = [jnp.where(side == 1, blocks[i ^ 2], blocks[i]) for i in range(4)]
    return jnp.concatenate(blocks, axis=0)


def rotation_tables(count, row_width):
    position = np.arange(count, dtype=np.float32)[:, None]
    lane = np.arange(2 * row_width)[None, :]
    channel = (lane % row_width // 2).astype(np.float32)
    frequency = np.exp(-(2.0 * channel / row_width) * np.log(np.float32(10000.0)))
    angle = (position * frequency).astype(np.float32)
    zeta_base = (2.0 * channel + 0.4 * row_width) / (1.4 * row_width)
    growth = np.exp((position - count // 2) / 512.0 * np.log(zeta_base))
    cosine = np.cos(angle)
    sine = np.sin(angle) * np.where(lane % 2 == 0, -1.0, 1.0)
    tables = [cosine * growth, sine * growth, cosine / growth, sine / growth]
    return jnp.asarray(np.stack(tables).astype(np.float32))


def swapped(values):
    width = values.shape[1]
    lane = lax.broadcasted_iota(jnp.int32, values.shape, 1)
    return jnp.where(lane % 2 == 0, pltpu.roll(values, width - 1, 1), pltpu.roll(values, 1, 1))


def scores_of(query, key, limit, scale_value):
    raw = matmul(query, key, ((1,), (1,))) * scale_value
    row = lax.broadcasted_iota(jnp.int32, raw.shape, 0)
    column = lax.broadcasted_iota(jnp.int32, raw.shape, 1)
    scores = jnp.where((column <= row) & (column < limit), raw, -1e30)
    top = jnp.max(scores, axis=-1, keepdims=True)
    grown = jnp.exp(scores - top)
    return grown * (1.0 / jnp.sum(grown, axis=-1, keepdims=True))


def in_head(values, head, head_dim):
    lane = lax.broadcasted_iota(jnp.int32, values.shape, 1)
    return jnp.where(lane // head_dim == head, values, jnp.zeros_like(values))


def block_columns(labels, k, depth):
    return pl.ds(pl.multiple_of(labels[k] * depth, depth), depth)


def row_parts(rank, rows):
    core = lax.rem(rank, 2)
    return [
        [pl.ds(pl.multiple_of((2 * side + place) * rows, rows), rows) for side in range(2)]
        for place in (1 - core, core)
    ]


def attention_forward(labels, limits, x, *refs, slots, head_dim, scale):
    blocks, (bias, tables, q_out, k_out, v_out, o_out, sums) = refs[:9], refs[9:]
    depth = x.shape[1] // 8
    pairs = x.shape[0] // slots
    width = 2 * head_dim
    turned = []
    for c in range(3):
        total = bias[c : c + 1, :]
        for k in range(8):
            if k == 4:
                part = blocks[4 + c // 2][c % 2 * depth : (c % 2 + 1) * depth, :]
            else:
                part = blocks[k + k // 5][c * depth : (c + 1) * depth, :]
            total = total + matmul(x[:, block_columns(labels, k, depth)], part, ((1,), (0,)))
        turned.append(total)
    first = jnp.zeros((x.shape[0], 1), f32)
    square = jnp.zeros((x.shape[0], 1), f32)
    for j in range(q_out.shape[1] // width):
        lanes = slice(j * width, (j + 1) * width)
        for p in range(pairs):
            rows = slice(p * slots, (p + 1) * slots)
            q = turned[0][rows, lanes]
            q = q * tables[0] + swapped(q) * tables[1]
            k = turned[1][rows, lanes]
            k = (k * tables[2] + swapped(k) * tables[3]).astype(bf16)
            v = turned[2][rows, lanes].astype(bf16)
            q_out[rows, lanes] = q.astype(bf16)
            k_out[rows, lanes] = k
            v_out[rows, lanes] = v
            mixed = []
            for head in range(2):
                probs = scores_of(in_head(q, head, head_dim).astype(bf16), k, limits[p], scale)
                mixed.append(matmul(probs.astype(bf16), v, ((1,), (0,))))
            lane = lax.broadcasted_iota(jnp.int32, mixed[0].shape, 1)
            o_out[rows, lanes] = jnp.where(lane < head_dim, mixed[0], mixed[1])
    mixed = o_out[...]
    lane = lax.broadcasted_iota(jnp.int32, sums.shape, 1)
    partial = jnp.where(lane == 0, jnp.sum(mixed, axis=-1, keepdims=True), 0.0) + jnp.where(
        lane == 1, jnp.sum(mixed * mixed, axis=-1, keepdims=True), 0.0
    )

    @pl.when(pl.program_id(0) == 0)
    def _():
        sums[...] = partial

    @pl.when(pl.program_id(0) > 0)
    def _():
        sums[...] += partial


def attention_backward(
    limits, grad, mixed, coefficients, gain, tables, q_in, k_in, v_in, gq_out, gk_out, gv_out, sums, *, slots, head_dim, scale
):
    pairs = grad.shape[0] // slots
    width = 2 * head_dim
    mean, inverse = coefficients[:, 0:1], coefficients[:, 1:2]
    first, second = coefficients[:, 2:3], coefficients[:, 3:4]
    row = lax.broadcasted_iota(jnp.int32, (8, width), 0)
    for j in range(grad.shape[1] // width):
        lanes = slice(j * width, (j + 1) * width)
        total = jnp.zeros((8, width), f32)
        for p in range(pairs):
            rows = slice(p * slots, (p + 1) * slots)
            g = grad[rows, lanes]
            hat = (mixed[rows, lanes] - mean[rows]) * inverse[rows]
            total += jnp.where(row == 3, jnp.sum(g, axis=0, keepdims=True), 0.0)
            total += jnp.where(row == 4, jnp.sum(g * hat, axis=0, keepdims=True), 0.0)
            g = inverse[rows] * (g * gain[4:5, lanes] - first[rows] - hat * second[rows])
            q, k, v = q_in[rows, lanes].astype(f32), k_in[rows, lanes].astype(f32), v_in[rows, lanes]
            gq = jnp.zeros((slots, width), f32)
            gk = jnp.zeros((slots, width), f32)
            gv = jnp.zeros((slots, width), f32)
            for head in range(2):
                q_head = in_head(q, head, head_dim).astype(bf16)
                k_head = in_head(k, head, head_dim).astype(bf16)
                g_head = in_head(g, head, head_dim).astype(bf16)
                probs = scores_of(q_head, k_head, limits[p], scale)
                grad_probs = matmul(g_head, v, ((1,), (1,)))
                gv += matmul(probs.astype(bf16), g_head, ((0,), (0,)))
                spread = jnp.sum(probs * grad_probs, axis=-1, keepdims=True)
                grad_scores = (probs * (grad_probs - spread) * scale).astype(bf16)
                gq += matmul(grad_scores, k_head, ((1,), (0,)))
                gk += matmul(grad_scores, q_head, ((0,), (0,)))
            gq = (gq * tables[0] - swapped(gq) * tables[1]).astype(bf16)
            gk = (gk * tables[2] - swapped(gk) * tables[3]).astype(bf16)
            gv = gv.astype(bf16)
            gq_out[rows, lanes] = gq
            gk_out[rows, lanes] = gk
            gv_out[rows, lanes] = gv
            for index, part in enumerate((gq, gk, gv)):
                total += jnp.where(
                    row == index, jnp.sum(part.astype(f32), axis=0, keepdims=True), 0.0
                )
        sums[:, lanes] = total


def output_product(labels, rank, mixed, coefficients, gains, *refs):
    blocks, (away_out, kept_out, post_out) = refs[:8], refs[8:]
    depth = away_out.shape[1] // 8
    rows = away_out.shape[0] // 2
    hat = (mixed[...] - coefficients[:, 0:1]) * coefficients[:, 1:2]
    post_out[...] = (hat * gains[4:5, :] + gains[3:4, :]).astype(bf16)
    for out, slices in zip((away_out, kept_out), row_parts(rank[0], rows)):
        left = jnp.concatenate([post_out[part, :] for part in slices], axis=0)
        for k in range(8):
            product = matmul(left, blocks[k][...], ((1,), (1,)))
            out[:, block_columns(labels, k, depth)] = product.astype(out.dtype)


def output_back(labels, grad, mixed, coefficients, gains, *refs):
    blocks, (out, sums) = refs[:8], refs[8:]
    depth = grad.shape[1] // 8
    total = jnp.zeros(out.shape, f32)
    for k in range(8):
        total = total + matmul(
            grad[:, block_columns(labels, k, depth)], blocks[k][...], ((1,), (0,))
        )
    out[...] = total
    scaled = total * gains[4:5, :]
    hat = (mixed[...] - coefficients[:, 0:1]) * coefficients[:, 1:2]
    lane = lax.broadcasted_iota(jnp.int32, sums.shape, 1)
    sums[...] = jnp.where(lane == 0, jnp.sum(scaled, axis=-1, keepdims=True), 0.0) + jnp.where(
        lane == 1, jnp.sum(scaled * hat, axis=-1, keepdims=True), 0.0
    )


def projection_gradient(labels, x, grad, gq, gk, gv, post, out):
    depth = x.shape[1]
    for c, part in enumerate((gq, gk, gv)):
        out[0, c * depth : (c + 1) * depth, :] = matmul(x[...], part[...], ((0,), (0,))).astype(bf16)
    out[0, 3 * depth :, :] = matmul(grad[...], post[...], ((0,), (0,))).astype(bf16)


def projection_gradient_far(labels, x, grad, gq, gk, gv, post, first_out, second_out):
    depth = x.shape[1]
    first_out[:depth, :] = matmul(x[...], gq[...], ((0,), (0,))).astype(bf16)
    first_out[depth:, :] = matmul(x[...], gk[...], ((0,), (0,))).astype(bf16)
    second_out[:depth, :] = matmul(x[...], gv[...], ((0,), (0,))).astype(bf16)
    second_out[depth:, :] = matmul(grad[...], post[...], ((0,), (0,))).astype(bf16)


def projection_back(labels, rank, gq, gk, gv, *refs):
    blocks, (away_out, kept_out) = refs[:9], refs[9:]
    depth = away_out.shape[1] // 8
    rows = away_out.shape[0] // 2
    for out, slices in zip((away_out, kept_out), row_parts(rank[0], rows)):
        left = [
            jnp.concatenate([grad[part, :] for part in slices], axis=0) for grad in (gq, gk, gv)
        ]
        for k in range(8):
            total = jnp.zeros((2 * rows, depth), f32)
            for c in range(3):
                if k == 4:
                    part = blocks[4 + c // 2][c % 2 * depth : (c % 2 + 1) * depth, :]
                else:
                    part = blocks[k + k // 5][c * depth : (c + 1) * depth, :]
                total = total + matmul(left[c], part, ((1,), (1,)))
            out[:, block_columns(labels, k, depth)] = total.astype(out.dtype)


def columns_of(rows):
    return jnp.transpose(jnp.concatenate([rows] * 16, axis=0))


def ffn_forward(labels, x, g, vectors, *refs):
    blocks, (active_out, slope_out, grad_out, sums) = refs[:8], refs[8:]
    depth = x.shape[1] // 8
    before = vectors[0:1, :]
    grad = jnp.zeros(grad_out.shape, f32)
    for k in range(8):
        lanes = block_columns(labels, k, depth)
        before = before + matmul(x[:, lanes], blocks[k][:depth, :], ((1,), (0,)))
        grad = grad + matmul(g[:, lanes], blocks[k][depth:, :], ((1,), (0,)))
    below = 0.5 + 0.5 * lax.erf(before * math.sqrt(0.5))
    active = before * below
    active_out[...] = active
    slope_out[...] = below + before * (math.sqrt(0.5 / math.pi) * jnp.exp(-0.5 * before * before))
    grad_out[...] = grad
    scaled = grad * vectors[2:3, :]
    lane = lax.broadcasted_iota(jnp.int32, (grad.shape[0], 128), 1)
    columns = jnp.zeros((grad.shape[0], 128), f32)
    for index, values in enumerate((active, active * active, scaled, scaled * active)):
        columns += jnp.where(lane == index, jnp.sum(values, axis=-1, keepdims=True), 0.0)
    sums[...] = jnp.transpose(columns)[:8, :]


def ffn_backward(labels, sums, active, slope, grad, vectors, *refs, width):
    blocks, (before_out, post_out, out, totals) = refs[:8], refs[8:]
    columns = columns_of(sums[...])
    mean = columns[:, 0:1] / width
    inverse = lax.rsqrt(columns[:, 1:2] / width - mean * mean + norm_eps)
    hat_sum = inverse * (columns[:, 3:4] - mean * columns[:, 2:3])
    hat = (active[...] - mean) * inverse
    gain = vectors[2:3, :]
    post_out[...] = (hat * gain + vectors[1:2, :]).astype(bf16)
    moved = grad[...] * gain - columns[:, 2:3] / width - hat * (hat_sum / width)
    grad_before = (inverse * moved * slope[...]).astype(bf16)
    before_out[...] = grad_before
    product_into(labels, grad_before, blocks, out)
    row = lax.broadcasted_iota(jnp.int32, totals.shape, 0)
    partial = jnp.zeros(totals.shape, f32)
    for index, values in enumerate((grad_before.astype(f32), grad[...], grad[...] * hat)):
        partial += jnp.where(row == index, jnp.sum(values, axis=0, keepdims=True), 0.0)

    @pl.when(pl.program_id(0) == 0)
    def _():
        totals[...] = partial

    @pl.when(pl.program_id(0) > 0)
    def _():
        totals[...] += partial


def product_into(labels, left, blocks, out):
    depth = out.shape[1] // 8
    for k in range(8):
        product = matmul(left, blocks[k][...], ((1,), (1,)))
        out[:, block_columns(labels, k, depth)] = product.astype(bf16)


def ffn_product(labels, left, *refs):
    product_into(labels, left[...], refs[:8], refs[8])


def ffn_gradient(labels, near_x, far_x, near_g, far_g, near_before, far_before, near_post, far_post, *outs):
    depth = near_x.shape[1]
    totals = []
    for c, (near, far, near_right, far_right) in enumerate(
        ((near_x, far_x, near_before, far_before), (near_g, far_g, near_post, far_post))
    ):
        total = matmul(near[...], near_right[...], ((0,), (0,)))
        total = total + matmul(far[...], far_right[...], ((0,), (0,)))
        totals.append(total.astype(bf16))
    for k, out in enumerate(outs):

        @pl.when(pl.program_id(0) == k)
        def _(out=out):
            for c, total in enumerate(totals):
                out[c * depth : (c + 1) * depth, :] = total


def ffn_placed(groups, *refs):
    blocks, (first_out, second_out) = refs[:4], refs[4:]
    depth, width = blocks[0].shape[0] // 2, blocks[0].shape[1]
    for k in range(4):
        place = pl.ds(pl.multiple_of(groups[k] * width, width), width)
        first_out[:, place] = blocks[k][:depth, :].astype(f32)
        second_out[place, :] = jnp.transpose(blocks[k][depth:, :].astype(f32))


def cost(flops, moved, exponentials=0):
    return pl.CostEstimate(flops=flops, bytes_accessed=moved, transcendentals=exponentials)


def norm_stats(first_sum, square_sum, row_width):
    mean_value = first_sum / row_width
    variance = square_sum / row_width - mean_value * mean_value
    return mean_value, lax.rsqrt(variance + norm_eps)


def norm_rows(values, gain_vector, shift_vector):
    width = values.shape[-1]
    mean_value, inverse = norm_stats(
        jnp.sum(values, axis=-1, keepdims=True),
        jnp.sum(values * values, axis=-1, keepdims=True),
        width,
    )
    hat = (values - mean_value) * inverse
    return hat * gain_vector + shift_vector, hat, inverse


def norm_back_rows(scaled, hat, inverse):
    width = scaled.shape[-1]
    return inverse * (
        scaled
        - jnp.sum(scaled, axis=-1, keepdims=True) / width
        - hat * jnp.sum(scaled * hat, axis=-1, keepdims=True) / width
    )


def matmul(a, b, dims):
    return lax.dot_general(a, b, (dims, ((), ())), preferred_element_type=f32)


def per_device(
    tokens,
    cotangent,
    caption_lengths,
    w_qkv,
    head_biases,
    head_gain,
    w_out,
    model_gains,
    model_biases,
    w_fc1,
    w_fc2,
    ffn_gain,
    ffn_biases,
    *,
    fsdp_size,
):
    here = lax.axis_index("fsdp")
    rank = lax.axis_index("tp")
    core, side = rank % 2, rank // 2
    others = fsdp_size // GROUPS
    group, member = here // others, here % others
    ring = Ring(fsdp_size, here)
    group_lists = [[g * others + o for g in range(GROUPS)] for o in range(others)]
    member_lists = [[g * others + o for o in range(others)] for g in range(GROUPS)]

    def group_send(block, shift):
        return lax.ppermute(
            block,
            "fsdp",
            [
                (g * others + o, (g + shift) % GROUPS * others + o)
                for g in range(GROUPS)
                for o in range(others)
            ],
        )

    def group_swap(blocks):
        return lax.all_to_all(blocks, "fsdp", 0, 0, axis_index_groups=group_lists)

    def pair_send(block):
        return lax.ppermute(block, "fsdp", [(f, f ^ 1) for f in range(fsdp_size)])

    def member_gather(blocks):
        if others == 2:
            theirs = pair_send(blocks)
            return jnp.stack(
                [jnp.where(member == 0, blocks, theirs), jnp.where(member == 0, theirs, blocks)],
                axis=1,
            )
        full = lax.all_gather(blocks, "fsdp", axis=0, axis_index_groups=member_lists)
        return jnp.moveaxis(full, 0, 1)

    def member_scatter(blocks):
        if others == 2:
            sent = pair_send(block_at(blocks, 1 - member, 1))
            return block_at(blocks, member, 1).astype(f32) + sent.astype(f32)
        return lax.psum_scatter(
            blocks, "fsdp", scatter_dimension=1, axis_index_groups=member_lists, tiled=False
        ).astype(f32)

    pair_count = caption_lengths.shape[0]
    row_count, model_width = tokens.shape
    slot_count = row_count // pair_count
    sub_rows = row_count // 4
    head_dim = model_width // HEADS
    local_width = w_qkv.shape[2]
    block_rows = w_qkv.shape[0]
    hidden_width = FF
    local_hidden = w_fc1.shape[1] // GROUPS

    model_part = jnp.concatenate([model_gains, model_biases], axis=0)
    head_part = jnp.concatenate([head_biases, head_gain[None]], axis=0)
    unit_part = jnp.concatenate([ffn_biases, ffn_gain[None]], axis=0)
    packed = jnp.concatenate([model_part.reshape(-1), head_part.reshape(-1), unit_part.reshape(-1)])
    vectors = lax.all_to_all(
        jnp.broadcast_to(packed[None], (fsdp_size, packed.shape[0])), "fsdp", 0, 0
    )
    sizes = [model_part.size, head_part.size, unit_part.size]
    model_vectors = (
        vectors[:, : sizes[0]].reshape((fsdp_size,) + model_part.shape).transpose(1, 0, 2)
    ).reshape(6, model_width).astype(f32)
    head_vectors = (
        vectors[:, sizes[0] : sizes[0] + sizes[1]]
        .reshape((fsdp_size,) + head_part.shape)
        .transpose(1, 0, 2)
    ).reshape(5, local_width).astype(f32)
    unit_all = vectors[:, sizes[0] + sizes[1] :].reshape((GROUPS, others) + unit_part.shape)
    unit_vectors = block_at(unit_all, group).transpose(1, 0, 2).reshape(3, local_hidden).astype(f32)

    def rows_gather(piece, *tokens):
        pieces = [piece] + [group_send(piece, shift) for shift in range(1, GROUPS)]
        across = [tp_send(piece, 2)]
        pieces[1] = after(pieces[1], across[0])
        across += [tp_send(part, 2) for part in pieces[1:]]
        near = after(jnp.concatenate(pieces + across, axis=0), *tokens)
        return near, tp_send(near, 1)

    def core_sum(away, kept):
        return (kept + tp_send(away, 1).astype(f32)).reshape(2, sub_rows, -1)

    def side_sum(total):
        crossing = tp_send(block_at(total, 1 - side).astype(bf16), 2)
        return block_at(total, side) + crossing.astype(f32)

    def group_core(far, near):
        total = near.astype(f32) + tp_send(far, 1).astype(f32)
        return total.reshape(2, GROUPS, sub_rows, -1)

    def group_shares(total):
        return total[0] + tp_send(total[1].astype(bf16), 2).astype(f32)

    def group_shares_piped(total):
        return {k: total[0, k] + tp_send(total[1, k].astype(bf16), 2).astype(f32) for k in (2, 1, 3, 0)}

    def group_total(shares):
        sent = [group_send(shares[k].astype(bf16), -k).astype(f32) for k in (2, 1, 3)]
        return shares[0], sent

    def group_sum(values):
        def swap(array, width):
            pieces = [array[:, i : i + width] for i in range(0, array.shape[1], width)]
            pieces = [pieces[i ^ 1] for i in range(len(pieces))]
            return jnp.concatenate(pieces, axis=1)

        half_rows = 2 * GROUPS * sub_rows
        flip_core = tp_send(values, 1)
        flip_side = tp_send(values, 2)
        flip_both = tp_send(values, 3)
        values = values + swap(flip_core + swap(flip_both, half_rows // 2), half_rows)
        values = values + swap(flip_side, half_rows // 2)
        total = values
        for shift in range(1, GROUPS):
            part = group_send(values, shift).reshape(8, 4, GROUPS * sub_rows)
            cut = (GROUPS - shift) * sub_rows
            part = jnp.concatenate([part[:, :, cut:], part[:, :, :cut]], axis=2)
            total = total + part.reshape(8, -1)
        return total

    def my_rows(array):
        return lax.dynamic_slice_in_dim(array, rank * sub_rows, sub_rows, 0)

    slot_index = jnp.arange(slot_count)[None, :]
    key_valid = slot_index < IMAGE + caption_lengths[:, None]
    keep_rows = key_valid.reshape(row_count).astype(f32)[:, None]
    my_keep = my_rows(keep_rows)
    my_grad_out = my_rows(cotangent).astype(f32) * my_keep
    depth = model_width // 8
    own_block = jnp.concatenate([w_qkv[:, c] for c in range(3)] + [w_out.T], axis=0)
    blocks = ring.gather(own_block)
    labels = jnp.arange(8, dtype=jnp.int32) if ring.native else ring.labels(range(8))

    fc_pieces = jnp.concatenate(
        [w.reshape(block_rows, GROUPS, local_hidden) for w in (w_fc1, w_fc2.T)], axis=0
    )
    fc_pieces = after(fc_pieces.transpose(1, 0, 2), blocks[3])
    fc_mine = [block_at(fc_pieces, group)]
    for shift in (1, 3, 2):
        fc_mine.append(group_send(block_at(fc_pieces, (group + shift) % GROUPS), shift))
    fc_received = list(fc_mine)
    if others == 2:
        fc_theirs = [pair_send(part) for part in fc_mine]
        fc_labels = row_at(
            [
                [(f // 2 - k) % GROUPS * 2 + f % 2 for k in (0, 1, 3, 2)]
                + [(f // 2 - k) % GROUPS * 2 + 1 - f % 2 for k in (0, 1, 3, 2)]
                for f in range(fsdp_size)
            ],
            here,
        )
    else:
        full = jnp.zeros(fc_pieces.shape, bf16)
        for shift, part in zip((0, 1, 3, 2), fc_mine):
            full = put(full, part, (group - shift) % GROUPS)
        full = lax.all_gather(full, "fsdp", axis=0, axis_index_groups=member_lists)
        full = full.reshape(others, GROUPS, 2, block_rows, local_hidden).transpose(2, 1, 0, 3, 4)
        full = full.reshape(2, 8, depth, local_hidden).transpose(1, 0, 2, 3)
        full = full.reshape(8, 2 * depth, local_hidden)
        fc_mine, fc_theirs = [full[k] for k in range(4)], [full[k] for k in range(4, 8)]
        fc_labels = jnp.arange(8)
    fc_labels = fc_labels.astype(jnp.int32)
    fc_blocks = fc_mine + fc_theirs
    cotangent_rows = after(my_grad_out.astype(bf16), fc_received[3])
    cotangent_rows = [cotangent_rows] + [
        group_send(cotangent_rows, shift) for shift in range(1, GROUPS)
    ]

    tables = rotation_tables(slot_count, head_dim)
    limits = IMAGE + caption_lengths
    scale_value = 1.0 / math.sqrt(head_dim)
    normed_in, _, _ = norm_rows(tokens.astype(f32), model_vectors[0], model_vectors[2])
    normed_in_b = normed_in.astype(bf16)
    part_width = 4 * head_dim
    parts = local_width // part_width
    scalars = pl.BlockSpec(memory_space=pltpu.SMEM)

    def whole(shape, first=0):
        return pl.BlockSpec(shape, lambda j: (first,) + (0,) * (len(shape) - 1))

    def columns(rows):
        return pl.BlockSpec((rows, part_width), lambda j: (0, j))

    def projection_specs(width, index_map):
        full = pl.BlockSpec((3 * depth, width), index_map)
        return [full] * 4 + [pl.BlockSpec((2 * depth, width), index_map)] * 2 + [full] * 3

    out_row = whole((depth, local_width), 3)
    out_specs = [out_row] * 4 + [whole((depth, local_width), 1)] + [out_row] * 3
    out_blocks = blocks[:4] + blocks[5:]
    rank_array = rank.astype(jnp.int32)[None]
    big = pltpu.CompilerParams(vmem_limit_bytes=58 << 20)
    queries, keys_rot, values_in, heads_out, head_sums = pl.pallas_call(
        functools.partial(
            attention_forward, slots=slot_count, head_dim=head_dim, scale=scale_value
        ),
        grid=(parts,),
        in_specs=[scalars, scalars, whole((row_count, model_width))]
        + projection_specs(part_width, lambda j: (0, j))
        + [columns(5), whole((4, slot_count, 2 * head_dim))],
        out_specs=[columns(row_count)] * 4 + [whole((row_count, 128))],
        out_shape=[jax.ShapeDtypeStruct((row_count, local_width), bf16)] * 3
        + [
            jax.ShapeDtypeStruct((row_count, local_width), f32),
            jax.ShapeDtypeStruct((row_count, 128), f32),
        ],
        compiler_params=big,
        cost_estimate=cost(2 * row_count * model_width * 3 * local_width, 12 << 20, 1 << 20),
        name="attention_forward",
    )(labels, limits, normed_in_b, *blocks, head_vectors, tables)
    head_stats = tp_sum(head_sums[:, :2].T)
    mean_attn, inverse_attn = norm_stats(
        head_stats[0][:, None], head_stats[1][:, None], model_width
    )
    coefficients = jnp.concatenate([mean_attn, inverse_attn], axis=1)
    halves = [
        jax.ShapeDtypeStruct((2 * sub_rows, model_width), bf16),
        jax.ShapeDtypeStruct((2 * sub_rows, model_width), f32),
    ]
    half_specs = [whole((2 * sub_rows, model_width))] * 2
    away, kept, post_attn_b = pl.pallas_call(
        output_product,
        grid=(1,),
        in_specs=[
            scalars,
            scalars,
            whole((row_count, local_width)),
            whole((row_count, 2)),
            whole((5, local_width)),
        ]
        + out_specs,
        out_specs=half_specs + [whole((row_count, local_width))],
        out_shape=halves + [jax.ShapeDtypeStruct((row_count, local_width), bf16)],
        compiler_params=big,
        cost_estimate=cost(2 * row_count * model_width * local_width, 5 << 20),
        name="output_product",
    )(labels, rank_array, after(heads_out, *fc_received[1:3], fc_theirs[0]), coefficients, head_vectors, *out_blocks)
    branch = side_sum(after(core_sum(away, kept), fc_received[3]))
    middle = my_rows(tokens).astype(f32) + branch + model_vectors[4]
    normed_mid, hat_mid, inverse_mid = norm_rows(middle, model_vectors[1], model_vectors[3])

    cotangent_near = after(jnp.concatenate(cotangent_rows, axis=0), fc_received[3])
    cotangent_near = jnp.concatenate([cotangent_near, tp_send(cotangent_near, 2)], axis=0)
    grad_out_all = (cotangent_near, tp_send(cotangent_near, 1))
    normed_mid_all = rows_gather(
        after(normed_mid.astype(bf16), *cotangent_rows), *fc_theirs[1:]
    )
    half_rows = 2 * GROUPS * sub_rows
    step_rows = half_rows // 2

    def rows(width):
        return pl.BlockSpec((step_rows, width), lambda j: (j, 0))

    fc_half = [[whole((depth, local_hidden), start)] * 8 for start in range(2)]
    half_shape = jax.ShapeDtypeStruct((half_rows, local_hidden), f32)
    half_shape_b = jax.ShapeDtypeStruct((half_rows, local_hidden), bf16)
    product_shape = jax.ShapeDtypeStruct((half_rows, model_width), bf16)

    def forward_half(x, g):
        return pl.pallas_call(
            ffn_forward,
            grid=(2,),
            in_specs=[scalars, rows(model_width), rows(model_width), whole((3, local_hidden))]
            + [whole((2 * depth, local_hidden))] * 8,
            out_specs=[rows(local_hidden)] * 3 + [pl.BlockSpec((8, step_rows), lambda j: (0, j))],
            out_shape=[half_shape] * 3 + [jax.ShapeDtypeStruct((8, half_rows), f32)],
            compiler_params=big,
            cost_estimate=cost(4 * half_rows * model_width * local_hidden, 10 << 20, 1 << 20),
            name="ffn_forward",
        )(fc_labels, x, g, unit_vectors, *fc_blocks)

    *hidden_near, sums_near = forward_half(normed_mid_all[0], grad_out_all[0])
    *hidden_far, sums_far = forward_half(normed_mid_all[1], grad_out_all[1])
    sums = group_sum(jnp.concatenate([sums_near, sums_far], axis=1))

    def backward_half(index, hidden):
        return pl.pallas_call(
            functools.partial(ffn_backward, width=hidden_width),
            grid=(2,),
            in_specs=[scalars, pl.BlockSpec((8, step_rows), lambda j: (0, j + 2 * index))]
            + [rows(local_hidden)] * 3
            + [whole((3, local_hidden))]
            + fc_half[0],
            out_specs=[rows(local_hidden)] * 2 + [rows(model_width), whole((8, local_hidden))],
            out_shape=[half_shape_b] * 2
            + [product_shape, jax.ShapeDtypeStruct((8, local_hidden), f32)],
            compiler_params=big,
            cost_estimate=cost(2 * half_rows * model_width * local_hidden, 8 << 20),
            name="ffn_backward",
        )(fc_labels, sums, *hidden, unit_vectors, *fc_blocks)

    before_far, post_far, mid_far, totals_far = backward_half(1, hidden_far)
    before_near, post_near, mid_near, totals_near = backward_half(0, hidden_near)

    def second_half(post):
        return pl.pallas_call(
            ffn_product,
            grid=(2,),
            in_specs=[scalars, rows(local_hidden)] + fc_half[1],
            out_specs=rows(model_width),
            out_shape=product_shape,
            compiler_params=big,
            cost_estimate=cost(2 * half_rows * model_width * local_hidden, 5 << 20),
            name="ffn_product",
        )(fc_labels, post, *fc_blocks)

    mid_total = group_core(mid_far, mid_near)
    shares = group_shares_piped(mid_total)
    unit_s = member_scatter((totals_near + totals_far)[:3].reshape(3, others, -1))

    fc_order = (2, 1, 3, 0)

    def fc_gradient(order, token):
        return pl.pallas_call(
            ffn_gradient,
            grid_spec=pltpu.PrefetchScalarGridSpec(
                num_scalar_prefetch=1,
                grid=(4,),
                in_specs=[pl.BlockSpec((half_rows, depth), lambda j, label: (0, label[j]))] * 4
                + [pl.BlockSpec((half_rows, local_hidden), lambda j, label: (0, 0))] * 4,
                out_specs=[pl.BlockSpec((2 * depth, local_hidden), lambda j, label: (0, 0))] * 4,
            ),
            out_shape=[jax.ShapeDtypeStruct((2 * depth, local_hidden), bf16)] * 4,
            compiler_params=big,
            cost_estimate=cost(4 * half_rows * model_width * local_hidden, 9 << 20),
            name="ffn_gradient",
        )(
            order.astype(jnp.int32),
            *normed_mid_all,
            *grad_out_all,
            before_near,
            before_far,
            *after((post_near, post_far), token),
        )

    if others == 2:
        ahead = [[(f // 2 + k) % GROUPS * 2 for k in fc_order] for f in range(fsdp_size)]
        away_labels = row_at([[a + 1 - f % 2 for a in row] for f, row in enumerate(ahead)], here)
        kept_labels = row_at([[a + f % 2 for a in row] for f, row in enumerate(ahead)], here)
        fc_away = fc_gradient(away_labels, mid_total)
        fc_kept = fc_gradient(kept_labels, shares[2])
        fc_sent = [pair_send(part) for part in fc_away]
        fc_summed = [
            (kept.astype(f32) + sent.astype(f32)).astype(bf16)
            for kept, sent in zip(fc_kept, fc_sent)
        ]
    else:
        fc_away = fc_gradient(jnp.arange(4), mid_total)
        fc_kept = fc_gradient(jnp.arange(4, 8), shares[2])
        fc_grads = jnp.stack(fc_away + fc_kept)
        fc_grads = fc_grads.reshape(8, 2, depth, local_hidden).transpose(1, 0, 2, 3)
        fc_grads = fc_grads.reshape(2, GROUPS, others, block_rows, local_hidden)
        fc_grads = fc_grads.transpose(1, 2, 0, 3, 4).reshape(GROUPS, others, -1, local_hidden)
        fc_grads = member_scatter(fc_grads).astype(bf16)
        fc_summed = [block_at(fc_grads, (group + shift) % GROUPS) for shift in fc_order]
        fc_sent = fc_summed

    shares[1], shares[3] = after((shares[1], shares[3]), *fc_away)
    own, sent = group_total(shares)
    own = after(own, fc_kept[0], *fc_sent[:3], unit_s)
    grad_mid_normed = own + sent[0] + sent[1] + sent[2]
    grad_middle = my_grad_out + norm_back_rows(
        grad_mid_normed * model_vectors[1], hat_mid, inverse_mid
    )
    grad_middle_b = tp_rows_gather(grad_middle.astype(bf16), core, side)
    fc_spread = [group_send(part, k) if k else part for k, part in zip(fc_order, fc_summed)]

    grad_post_attn, back_sums = pl.pallas_call(
        output_back,
        grid=(1,),
        in_specs=[
            scalars,
            whole((row_count, model_width)),
            whole((row_count, local_width)),
            whole((row_count, 2)),
            whole((5, local_width)),
        ]
        + out_specs,
        out_specs=[whole((row_count, local_width)), whole((row_count, 128))],
        out_shape=[
            jax.ShapeDtypeStruct((row_count, local_width), f32),
            jax.ShapeDtypeStruct((row_count, 128), f32),
        ],
        compiler_params=big,
        cost_estimate=cost(2 * row_count * model_width * local_width, 5 << 20),
        name="output_back",
    )(labels, after(grad_middle_b, fc_sent[3]), heads_out, coefficients, head_vectors, *out_blocks)
    head_back = tp_sum(back_sums[:, :2].T)[:, :, None]
    coefficients = jnp.concatenate(
        [coefficients, head_back[0] / model_width, head_back[1] / model_width], axis=1
    )
    *grad_linear, head_sums_back = pl.pallas_call(
        functools.partial(
            attention_backward, slots=slot_count, head_dim=head_dim, scale=scale_value
        ),
        grid=(parts,),
        in_specs=[
            scalars,
            columns(row_count),
            columns(row_count),
            whole((row_count, 4)),
            columns(5),
            whole((4, slot_count, 2 * head_dim)),
            columns(row_count),
            columns(row_count),
            columns(row_count),
        ],
        out_specs=[columns(row_count)] * 3 + [columns(8)],
        out_shape=[jax.ShapeDtypeStruct((row_count, local_width), bf16)] * 3
        + [jax.ShapeDtypeStruct((8, local_width), f32)],
        compiler_params=pltpu.CompilerParams(vmem_limit_bytes=40 << 20),
        cost_estimate=cost(10 * row_count * slot_count * 2 * local_width, 4 << 20, 1 << 20),
        name="attention_backward",
    )(
        limits,
        grad_post_attn,
        heads_out,
        coefficients,
        head_vectors,
        tables,
        queries,
        keys_rot,
        values_in,
    )
    def weight_gradients(kernel, count, order, out_specs, out_shape):
        return pl.pallas_call(
            kernel,
            grid_spec=pltpu.PrefetchScalarGridSpec(
                num_scalar_prefetch=1,
                grid=(count,),
                in_specs=[pl.BlockSpec((row_count, depth), lambda j, label: (0, label[j]))] * 2
                + [pl.BlockSpec((row_count, local_width), lambda j, label: (0, 0))] * 4,
                out_specs=out_specs,
            ),
            out_shape=out_shape,
            compiler_params=big,
            cost_estimate=cost(count * row_count * depth * 8 * local_width, count << 20),
            name=kernel.__name__,
        )(order, normed_in_b, grad_middle_b, *grad_linear, post_attn_b)

    far_grads = weight_gradients(
        projection_gradient_far,
        1,
        labels[4:5],
        [pl.BlockSpec((2 * depth, local_width), lambda j, label: (0, 0))] * 2,
        [jax.ShapeDtypeStruct((2 * depth, local_width), bf16)] * 2,
    )
    order = [0, 3, 5, 2, 6, 1, 7]
    weight_grads = weight_gradients(
        projection_gradient,
        7,
        jnp.asarray(order, jnp.int32) if ring.native else ring.labels(order),
        pl.BlockSpec((1, 4 * depth, local_width), lambda j, label: (j, 0, 0)),
        jax.ShapeDtypeStruct((7, 4 * depth, local_width), bf16),
    )
    weight_grads = dict((k, weight_grads[j]) for j, k in enumerate(order))
    weight_grads[4] = far_grads
    if ring.native:
        weight_grads[4] = jnp.concatenate(far_grads, axis=0)
        weight_grads = jnp.stack([weight_grads[k] for k in range(8)])
        weight_grads = weight_grads.reshape(8, 4, fsdp_size // 8, block_rows, local_width)
        weight_grads = weight_grads.transpose(0, 2, 1, 3, 4).reshape(fsdp_size, -1, local_width)
    placed_rows = (block_rows, GROUPS * local_hidden)
    def place_ffn(token):
        return pl.pallas_call(
            ffn_placed,
            grid=(1,),
            in_specs=[scalars] + [whole((2 * block_rows, local_hidden))] * 4,
            out_specs=[whole(placed_rows), whole(placed_rows[::-1])],
            out_shape=[
                jax.ShapeDtypeStruct(placed_rows, f32),
                jax.ShapeDtypeStruct(placed_rows[::-1], f32),
            ],
            compiler_params=big,
            cost_estimate=cost(0, 6 << 20),
            name="ffn_placed",
        )(
            row_at([[(f // others - k) % GROUPS for k in fc_order] for f in range(fsdp_size)], here),
            *after(tuple(fc_spread), token),
        )

    results = {}

    def while_half(token):
        results["parts"] = [second_half(after(post, token)) for post in (post_far, post_near)]
        return fc_spread + results["parts"]

    def while_first(token):
        back_away, back_kept = pl.pallas_call(
            projection_back,
            grid=(1,),
            in_specs=[scalars, scalars]
            + [whole((row_count, local_width))] * 3
            + projection_specs(local_width, lambda j: (0, 0)),
            out_specs=half_specs,
            out_shape=halves,
            compiler_params=big,
            cost_estimate=cost(2 * row_count * model_width * 3 * local_width, 10 << 20),
            name="projection_back",
        )(labels, rank_array, *after(tuple(grad_linear), token), *blocks)
        results["back"] = back_away, back_kept
        results["core"] = group_core(*after(tuple(results["parts"]), token))
        return back_away, back_kept, results["core"]

    def while_second(token):
        grad_in_normed = side_sum(core_sum(*after(results["back"], token)))
        _, hat_in, inverse_in = norm_rows(
            my_rows(tokens).astype(f32), model_vectors[0], model_vectors[2]
        )
        grad_token_rows = grad_middle + norm_back_rows(
            grad_in_normed * model_vectors[0], hat_in, inverse_in
        )
        results["model"] = tp_sum(
            jnp.stack(
                [
                    jnp.sum(grad_in_normed * hat_in, axis=0),
                    jnp.sum(grad_mid_normed * hat_mid, axis=0),
                    jnp.sum(grad_in_normed, axis=0),
                    jnp.sum(grad_mid_normed, axis=0),
                    jnp.sum(grad_middle, axis=0),
                    jnp.sum(my_grad_out, axis=0),
                ]
            )
        )
        results["shares"] = group_shares(after(results["core"], token))
        results["tokens"] = grad_token_rows
        results["placed"] = place_ffn(token)
        return [results["model"], results["tokens"], results["shares"]] + list(results["placed"])

    def by_block(vectors_in, blocks_in):
        return vectors_in.reshape(vectors_in.shape[0], blocks_in, -1).transpose(1, 0, 2)

    def while_third(token):
        model_grads, token_rows, shares = after(
            (results["model"], results["tokens"], results["shares"]), token
        )
        model_blocks = by_block(model_grads, fsdp_size).reshape(fsdp_size, -1)
        head_blocks = by_block(head_sums_back[:5], fsdp_size).reshape(fsdp_size, -1)
        joined = jnp.concatenate([model_blocks, head_blocks], axis=1)
        joined_s = jnp.sum(lax.all_to_all(joined, "fsdp", 0, 0), axis=0)
        results["model_s"] = joined_s[: model_blocks.shape[1]].reshape(6, -1)
        results["head_s"] = joined_s[model_blocks.shape[1] :].reshape(5, -1)
        results["grad_tokens"] = tp_rows_gather(token_rows, core, side)
        own, sent = group_total(shares)
        own = after(own, joined_s, results["grad_tokens"])
        second = own + sent[0] + sent[1] + sent[2]
        out_rows = ((middle + second + model_vectors[5]) * my_keep).astype(bf16)
        results["layer_out"] = tp_rows_gather(out_rows, core, side)
        return ()

    weights_s = ring.scatter(weight_grads, [while_half, while_first, while_second, while_third])
    weights_s = weights_s.reshape(4, block_rows, local_width)
    grad_qkv_s = weights_s[:3].transpose(1, 0, 2)
    grad_out_s = weights_s[3]
    return (
        results["layer_out"],
        results["grad_tokens"],
        grad_qkv_s,
        results["head_s"][:4],
        results["head_s"][4],
        grad_out_s.T,
        results["model_s"][:2],
        results["model_s"][2:],
        *results["placed"],
        unit_s[2],
        unit_s[:2],
    )


def solution(mesh):
    placed = (
        P("fsdp", None),
        P("fsdp", None),
        P("fsdp"),
        P("fsdp", None, "tp"),
        P(None, ("tp", "fsdp")),
        P(("tp", "fsdp")),
        P("tp", "fsdp"),
        P(None, "fsdp"),
        P(None, "fsdp"),
        P("fsdp", "tp"),
        P("tp", "fsdp"),
        P(("tp", "fsdp")),
        P(None, ("tp", "fsdp")),
    )
    return jax.shard_map(
        functools.partial(per_device, fsdp_size=mesh.shape["fsdp"]),
        mesh=mesh,
        in_specs=placed,
        out_specs=(
            P("fsdp", None),
            P("fsdp", None),
            P("fsdp", None, "tp"),
            P(None, ("tp", "fsdp")),
            P(("tp", "fsdp")),
            P("tp", "fsdp"),
            P(None, "fsdp"),
            P(None, "fsdp"),
            P("fsdp", "tp"),
            P("tp", "fsdp"),
            P(("tp", "fsdp")),
            P(None, ("tp", "fsdp")),
        ),
        check_vma=False,
    )
```

```python
import functools
import math

import jax
import jax.numpy as jnp
import numpy as np
from jax import lax
from jax.experimental import pallas as pl
from jax.experimental.pallas import tpu as pltpu
from jax.sharding import PartitionSpec as P

HEADS = 32
FF = 8192
IMAGE = 64
GROUPS = 4

f32 = jnp.float32
bf16 = jnp.bfloat16
norm_eps = 1e-05


def pick(table, index):
    return lax.dynamic_index_in_dim(jnp.asarray(table, jnp.int32), index, keepdims=False)


def row_at(table, index):
    return lax.dynamic_index_in_dim(jnp.asarray(table, jnp.int32), index, keepdims=False)


def put(buffer, block, index):
    return lax.dynamic_update_slice(buffer, block[None], (index,) + (0,) * block.ndim)


def block_at(array, index, axis=0):
    return lax.dynamic_index_in_dim(array, index, axis, keepdims=False)


def after(value, *tokens):
    return lax.optimization_barrier((value,) + tokens)[0]


class Ring:
    def __init__(self, size, here):
        self.size = size
        self.here = here
        self.native = size > 8
        self.order = list(range(0, size, 2)) + list(range(size - 1, 0, -2))
        self.position = pick([self.order.index(i) for i in range(size)], here)
        self.forward = [(self.order[i], self.order[(i + 1) % size]) for i in range(size)]
        self.backward = [(b, a) for a, b in self.forward]

    def label(self, offset):
        return pick(self.order, (self.position + offset) % self.size)

    def labels(self, offsets):
        place = [self.order.index(i) for i in range(self.size)]
        return row_at(
            [[self.order[(place[i] + k) % self.size] for k in offsets] for i in range(self.size)],
            self.here,
        )

    def send(self, block, way):
        return lax.ppermute(block, "fsdp", self.forward if way > 0 else self.backward)

    def gather_parts(self, block):
        half = self.size // 2
        parts = [(0, block)]
        onward = backward = block
        for step in range(1, half):
            onward = self.send(onward, 1)
            backward = self.send(backward, -1)
            parts += [(-step, onward), (step, backward)]
        cut = block.shape[0] // 2
        return parts, [self.send(onward[:cut], 1), self.send(backward[cut:], -1)]

    def gather(self, block):
        if self.native:
            full = lax.all_gather(block, "fsdp", axis=0)
            wide = full.reshape((8, self.size // 8, 4, -1, block.shape[1]))
            wide = wide.transpose(0, 2, 1, 3, 4).reshape(8, -1, block.shape[1])
            cut = wide.shape[1] // 2
            blocks = [wide[k] for k in range(8)]
            return blocks[:4] + [blocks[4][:cut], blocks[4][cut:]] + blocks[5:]
        parts, halves = self.gather_parts(block)
        parts = dict((offset % 8, part) for offset, part in parts)
        return [parts[k] for k in range(4)] + halves + [parts[k] for k in range(5, 8)]

    def scatter(self, part, stages):
        if self.native:
            for stage in stages:
                stage(part)
            return lax.psum_scatter(part, "fsdp", scatter_dimension=0, tiled=False).astype(f32)
        half = self.size // 2
        cut = part[half][0].shape[0]
        onward = self.send(part[half][0], 1)
        backward = self.send(part[half][1], -1)
        tokens = stages[0](part[half][0])
        for step in range(half - 1, 0, -1):
            onward, backward = after((onward, backward), *tokens)
            ahead = part[step].astype(f32)
            behind = part[self.size - step].astype(f32)
            if step == half - 1:
                ahead = jnp.concatenate([ahead[:cut] + onward.astype(f32), ahead[cut:]], axis=0)
                behind = jnp.concatenate(
                    [behind[:cut], behind[cut:] + backward.astype(f32)], axis=0
                )
            else:
                ahead = ahead + onward.astype(f32)
                behind = behind + backward.astype(f32)
            ahead, behind = ahead.astype(bf16), behind.astype(bf16)
            onward = self.send(ahead, 1)
            backward = self.send(behind, -1)
            tokens = stages[half - step](ahead)
        return part[0].astype(f32) + onward.astype(f32) + backward.astype(f32)


def tp_send(block, mask):
    return lax.ppermute(block, "tp", [(i, i ^ mask) for i in range(4)])


def tp_sum(values):
    return values + tp_send(values, 1) + tp_send(values, 2) + tp_send(values, 3)


def tp_rows_gather(piece, core, side):
    across = tp_send(piece, 2)
    blocks = [piece, tp_send(piece, 1), across, tp_send(across, 1)]
    blocks = [jnp.where(core == 1, blocks[i ^ 1], blocks[i]) for i in range(4)]
    blocks = [jnp.where(side == 1, blocks[i ^ 2], blocks[i]) for i in range(4)]
    return jnp.concatenate(blocks, axis=0)


def rotation_tables(count, row_width):
    position = np.arange(count, dtype=np.float32)[:, None]
    lane = np.arange(2 * row_width)[None, :]
    channel = (lane % row_width // 2).astype(np.float32)
    frequency = np.exp(-(2.0 * channel / row_width) * np.log(np.float32(10000.0)))
    angle = (position * frequency).astype(np.float32)
    zeta_base = (2.0 * channel + 0.4 * row_width) / (1.4 * row_width)
    growth = np.exp((position - count // 2) / 512.0 * np.log(zeta_base))
    cosine = np.cos(angle)
    sine = np.sin(angle) * np.where(lane % 2 == 0, -1.0, 1.0)
    tables = [cosine * growth, sine * growth, cosine / growth, sine / growth]
    return jnp.asarray(np.stack(tables).astype(np.float32))


def swapped(values):
    width = values.shape[1]
    lane = lax.broadcasted_iota(jnp.int32, values.shape, 1)
    return jnp.where(lane % 2 == 0, pltpu.roll(values, width - 1, 1), pltpu.roll(values, 1, 1))


def scores_of(query, key, limit, scale_value):
    raw = matmul(query, key, ((1,), (1,))) * scale_value
    row = lax.broadcasted_iota(jnp.int32, raw.shape, 0)
    column = lax.broadcasted_iota(jnp.int32, raw.shape, 1)
    scores = jnp.where((column <= row) & (column < limit), raw, -1e30)
    top = jnp.max(scores, axis=-1, keepdims=True)
    grown = jnp.exp(scores - top)
    return grown * (1.0 / jnp.sum(grown, axis=-1, keepdims=True))


def in_head(values, head, head_dim):
    lane = lax.broadcasted_iota(jnp.int32, values.shape, 1)
    return jnp.where(lane // head_dim == head, values, jnp.zeros_like(values))


def block_columns(labels, k, depth):
    return pl.ds(pl.multiple_of(labels[k] * depth, depth), depth)


def row_parts(rank, rows):
    core = lax.rem(rank, 2)
    return [
        [pl.ds(pl.multiple_of((2 * side + place) * rows, rows), rows) for side in range(2)]
        for place in (1 - core, core)
    ]


def attention_forward(labels, limits, x, *refs, slots, head_dim, scale):
    blocks, (bias, tables, q_out, k_out, v_out, o_out, sums) = refs[:9], refs[9:]
    depth = x.shape[1] // 8
    pairs = x.shape[0] // slots
    width = 2 * head_dim
    turned = []
    for c in range(3):
        total = bias[c : c + 1, :]
        for k in range(8):
            if k == 4:
                part = blocks[4 + c // 2][c % 2 * depth : (c % 2 + 1) * depth, :]
            else:
                part = blocks[k + k // 5][c * depth : (c + 1) * depth, :]
            total = total + matmul(x[:, block_columns(labels, k, depth)], part, ((1,), (0,)))
        turned.append(total)
    first = jnp.zeros((x.shape[0], 1), f32)
    square = jnp.zeros((x.shape[0], 1), f32)
    for j in range(q_out.shape[1] // width):
        lanes = slice(j * width, (j + 1) * width)
        for p in range(pairs):
            rows = slice(p * slots, (p + 1) * slots)
            q = turned[0][rows, lanes]
            q = q * tables[0] + swapped(q) * tables[1]
            k = turned[1][rows, lanes]
            k = (k * tables[2] + swapped(k) * tables[3]).astype(bf16)
            v = turned[2][rows, lanes].astype(bf16)
            q_out[rows, lanes] = q.astype(bf16)
            k_out[rows, lanes] = k
            v_out[rows, lanes] = v
            mixed = []
            for head in range(2):
                probs = scores_of(in_head(q, head, head_dim).astype(bf16), k, limits[p], scale)
                mixed.append(matmul(probs.astype(bf16), v, ((1,), (0,))))
            lane = lax.broadcasted_iota(jnp.int32, mixed[0].shape, 1)
            o_out[rows, lanes] = jnp.where(lane < head_dim, mixed[0], mixed[1])
    mixed = o_out[...]
    lane = lax.broadcasted_iota(jnp.int32, sums.shape, 1)
    partial = jnp.where(lane == 0, jnp.sum(mixed, axis=-1, keepdims=True), 0.0) + jnp.where(
        lane == 1, jnp.sum(mixed * mixed, axis=-1, keepdims=True), 0.0
    )

    @pl.when(pl.program_id(0) == 0)
    def _():
        sums[...] = partial

    @pl.when(pl.program_id(0) > 0)
    def _():
        sums[...] += partial


def attention_backward(
    limits, grad, mixed, coefficients, gain, tables, q_in, k_in, v_in, gq_out, gk_out, gv_out, sums, *, slots, head_dim, scale
):
    pairs = grad.shape[0] // slots
    width = 2 * head_dim
    mean, inverse = coefficients[:, 0:1], coefficients[:, 1:2]
    first, second = coefficients[:, 2:3], coefficients[:, 3:4]
    row = lax.broadcasted_iota(jnp.int32, (8, width), 0)
    for j in range(grad.shape[1] // width):
        lanes = slice(j * width, (j + 1) * width)
        total = jnp.zeros((8, width), f32)
        for p in range(pairs):
            rows = slice(p * slots, (p + 1) * slots)
            g = grad[rows, lanes]
            hat = (mixed[rows, lanes] - mean[rows]) * inverse[rows]
            total += jnp.where(row == 3, jnp.sum(g, axis=0, keepdims=True), 0.0)
            total += jnp.where(row == 4, jnp.sum(g * hat, axis=0, keepdims=True), 0.0)
            g = inverse[rows] * (g * gain[4:5, lanes] - first[rows] - hat * second[rows])
            q, k, v = q_in[rows, lanes].astype(f32), k_in[rows, lanes].astype(f32), v_in[rows, lanes]
            gq = jnp.zeros((slots, width), f32)
            gk = jnp.zeros((slots, width), f32)
            gv = jnp.zeros((slots, width), f32)
            for head in range(2):
                q_head = in_head(q, head, head_dim).astype(bf16)
                k_head = in_head(k, head, head_dim).astype(bf16)
                g_head = in_head(g, head, head_dim).astype(bf16)
                probs = scores_of(q_head, k_head, limits[p], scale)
                grad_probs = matmul(g_head, v, ((1,), (1,)))
                gv += matmul(probs.astype(bf16), g_head, ((0,), (0,)))
                spread = jnp.sum(probs * grad_probs, axis=-1, keepdims=True)
                grad_scores = (probs * (grad_probs - spread) * scale).astype(bf16)
                gq += matmul(grad_scores, k_head, ((1,), (0,)))
                gk += matmul(grad_scores, q_head, ((0,), (0,)))
            gq = (gq * tables[0] - swapped(gq) * tables[1]).astype(bf16)
            gk = (gk * tables[2] - swapped(gk) * tables[3]).astype(bf16)
            gv = gv.astype(bf16)
            gq_out[rows, lanes] = gq
            gk_out[rows, lanes] = gk
            gv_out[rows, lanes] = gv
            for index, part in enumerate((gq, gk, gv)):
                total += jnp.where(
                    row == index, jnp.sum(part.astype(f32), axis=0, keepdims=True), 0.0
                )
        sums[:, lanes] = total


def output_product(labels, rank, mixed, coefficients, gains, *refs):
    blocks, (away_out, kept_out, post_out) = refs[:8], refs[8:]
    depth = away_out.shape[1] // 8
    rows = away_out.shape[0] // 2
    hat = (mixed[...] - coefficients[:, 0:1]) * coefficients[:, 1:2]
    post_out[...] = (hat * gains[4:5, :] + gains[3:4, :]).astype(bf16)
    for out, slices in zip((away_out, kept_out), row_parts(rank[0], rows)):
        left = jnp.concatenate([post_out[part, :] for part in slices], axis=0)
        for k in range(8):
            product = matmul(left, blocks[k][...], ((1,), (1,)))
            out[:, block_columns(labels, k, depth)] = product.astype(out.dtype)


def output_back(labels, grad, mixed, coefficients, gains, *refs):
    blocks, (out, sums) = refs[:8], refs[8:]
    depth = grad.shape[1] // 8
    total = jnp.zeros(out.shape, f32)
    for k in range(8):
        total = total + matmul(
            grad[:, block_columns(labels, k, depth)], blocks[k][...], ((1,), (0,))
        )
    out[...] = total
    scaled = total * gains[4:5, :]
    hat = (mixed[...] - coefficients[:, 0:1]) * coefficients[:, 1:2]
    lane = lax.broadcasted_iota(jnp.int32, sums.shape, 1)
    sums[...] = jnp.where(lane == 0, jnp.sum(scaled, axis=-1, keepdims=True), 0.0) + jnp.where(
        lane == 1, jnp.sum(scaled * hat, axis=-1, keepdims=True), 0.0
    )


def projection_gradient(labels, x, grad, gq, gk, gv, post, out):
    depth = x.shape[1]
    for c, part in enumerate((gq, gk, gv)):
        out[0, c * depth : (c + 1) * depth, :] = matmul(x[...], part[...], ((0,), (0,))).astype(bf16)
    out[0, 3 * depth :, :] = matmul(grad[...], post[...], ((0,), (0,))).astype(bf16)


def projection_gradient_far(labels, x, grad, gq, gk, gv, post, first_out, second_out):
    depth = x.shape[1]
    first_out[:depth, :] = matmul(x[...], gq[...], ((0,), (0,))).astype(bf16)
    first_out[depth:, :] = matmul(x[...], gk[...], ((0,), (0,))).astype(bf16)
    second_out[:depth, :] = matmul(x[...], gv[...], ((0,), (0,))).astype(bf16)
    second_out[depth:, :] = matmul(grad[...], post[...], ((0,), (0,))).astype(bf16)


def projection_back(labels, rank, gq, gk, gv, *refs):
    blocks, (away_out, kept_out) = refs[:9], refs[9:]
    depth = away_out.shape[1] // 8
    rows = away_out.shape[0] // 2
    for out, slices in zip((away_out, kept_out), row_parts(rank[0], rows)):
        left = [
            jnp.concatenate([grad[part, :] for part in slices], axis=0) for grad in (gq, gk, gv)
        ]
        for k in range(8):
            total = jnp.zeros((2 * rows, depth), f32)
            for c in range(3):
                if k == 4:
                    part = blocks[4 + c // 2][c % 2 * depth : (c % 2 + 1) * depth, :]
                else:
                    part = blocks[k + k // 5][c * depth : (c + 1) * depth, :]
                total = total + matmul(left[c], part, ((1,), (1,)))
            out[:, block_columns(labels, k, depth)] = total.astype(out.dtype)


def columns_of(rows):
    return jnp.transpose(jnp.concatenate([rows] * 16, axis=0))


def ffn_forward(labels, x, g, vectors, *refs):
    blocks, (active_out, slope_out, grad_out, sums) = refs[:8], refs[8:]
    depth = x.shape[1] // 8
    before = vectors[0:1, :]
    grad = jnp.zeros(grad_out.shape, f32)
    for k in range(8):
        lanes = block_columns(labels, k, depth)
        before = before + matmul(x[:, lanes], blocks[k][:depth, :], ((1,), (0,)))
        grad = grad + matmul(g[:, lanes], blocks[k][depth:, :], ((1,), (0,)))
    below = 0.5 + 0.5 * lax.erf(before * math.sqrt(0.5))
    active = before * below
    active_out[...] = active
    slope_out[...] = below + before * (math.sqrt(0.5 / math.pi) * jnp.exp(-0.5 * before * before))
    grad_out[...] = grad
    scaled = grad * vectors[2:3, :]
    lane = lax.broadcasted_iota(jnp.int32, (grad.shape[0], 128), 1)
    columns = jnp.zeros((grad.shape[0], 128), f32)
    for index, values in enumerate((active, active * active, scaled, scaled * active)):
        columns += jnp.where(lane == index, jnp.sum(values, axis=-1, keepdims=True), 0.0)
    sums[...] = jnp.transpose(columns)[:8, :]


def ffn_backward(labels, sums, active, slope, grad, vectors, *refs, width):
    blocks, (before_out, post_out, out, totals) = refs[:8], refs[8:]
    columns = columns_of(sums[...])
    mean = columns[:, 0:1] / width
    inverse = lax.rsqrt(columns[:, 1:2] / width - mean * mean + norm_eps)
    hat_sum = inverse * (columns[:, 3:4] - mean * columns[:, 2:3])
    hat = (active[...] - mean) * inverse
    gain = vectors[2:3, :]
    post_out[...] = (hat * gain + vectors[1:2, :]).astype(bf16)
    moved = grad[...] * gain - columns[:, 2:3] / width - hat * (hat_sum / width)
    grad_before = (inverse * moved * slope[...]).astype(bf16)
    before_out[...] = grad_before
    product_into(labels, grad_before, blocks, out)
    row = lax.broadcasted_iota(jnp.int32, totals.shape, 0)
    partial = jnp.zeros(totals.shape, f32)
    for index, values in enumerate((grad_before.astype(f32), grad[...], grad[...] * hat)):
        partial += jnp.where(row == index, jnp.sum(values, axis=0, keepdims=True), 0.0)

    @pl.when(pl.program_id(0) == 0)
    def _():
        totals[...] = partial

    @pl.when(pl.program_id(0) > 0)
    def _():
        totals[...] += partial


def product_into(labels, left, blocks, out):
    depth = out.shape[1] // 8
    for k in range(8):
        product = matmul(left, blocks[k][...], ((1,), (1,)))
        out[:, block_columns(labels, k, depth)] = product.astype(bf16)


def ffn_product(labels, left, *refs):
    product_into(labels, left[...], refs[:8], refs[8])


def ffn_gradient(labels, near_x, far_x, near_g, far_g, near_before, far_before, near_post, far_post, *outs):
    depth = near_x.shape[1]
    totals = []
    for c, (near, far, near_right, far_right) in enumerate(
        ((near_x, far_x, near_before, far_before), (near_g, far_g, near_post, far_post))
    ):
        total = matmul(near[...], near_right[...], ((0,), (0,)))
        total = total + matmul(far[...], far_right[...], ((0,), (0,)))
        totals.append(total.astype(bf16))
    for k, out in enumerate(outs):

        @pl.when(pl.program_id(0) == k)
        def _(out=out):
            for c, total in enumerate(totals):
                out[c * depth : (c + 1) * depth, :] = total


def ffn_placed(groups, *refs):
    blocks, (first_out, second_out) = refs[:4], refs[4:]
    depth, width = blocks[0].shape[0] // 2, blocks[0].shape[1]
    for k in range(4):
        place = pl.ds(pl.multiple_of(groups[k] * width, width), width)
        first_out[:, place] = blocks[k][:depth, :].astype(f32)
        second_out[place, :] = jnp.transpose(blocks[k][depth:, :].astype(f32))


def cost(flops, moved, exponentials=0):
    return pl.CostEstimate(flops=flops, bytes_accessed=moved, transcendentals=exponentials)


def norm_stats(first_sum, square_sum, row_width):
    mean_value = first_sum / row_width
    variance = square_sum / row_width - mean_value * mean_value
    return mean_value, lax.rsqrt(variance + norm_eps)


def norm_rows(values, gain_vector, shift_vector):
    width = values.shape[-1]
    mean_value, inverse = norm_stats(
        jnp.sum(values, axis=-1, keepdims=True),
        jnp.sum(values * values, axis=-1, keepdims=True),
        width,
    )
    hat = (values - mean_value) * inverse
    return hat * gain_vector + shift_vector, hat, inverse


def norm_back_rows(scaled, hat, inverse):
    width = scaled.shape[-1]
    return inverse * (
        scaled
        - jnp.sum(scaled, axis=-1, keepdims=True) / width
        - hat * jnp.sum(scaled * hat, axis=-1, keepdims=True) / width
    )


def matmul(a, b, dims):
    return lax.dot_general(a, b, (dims, ((), ())), preferred_element_type=f32)


def per_device(
    tokens,
    cotangent,
    caption_lengths,
    w_qkv,
    head_biases,
    head_gain,
    w_out,
    model_gains,
    model_biases,
    w_fc1,
    w_fc2,
    ffn_gain,
    ffn_biases,
    *,
    fsdp_size,
):
    here = lax.axis_index("fsdp")
    rank = lax.axis_index("tp")
    core, side = rank % 2, rank // 2
    others = fsdp_size // GROUPS
    group, member = here // others, here % others
    ring = Ring(fsdp_size, here)
    group_lists = [[g * others + o for g in range(GROUPS)] for o in range(others)]
    member_lists = [[g * others + o for o in range(others)] for g in range(GROUPS)]

    def group_send(block, shift):
        return lax.ppermute(
            block,
            "fsdp",
            [
                (g * others + o, (g + shift) % GROUPS * others + o)
                for g in range(GROUPS)
                for o in range(others)
            ],
        )

    def group_swap(blocks):
        return lax.all_to_all(blocks, "fsdp", 0, 0, axis_index_groups=group_lists)

    def pair_send(block):
        return lax.ppermute(block, "fsdp", [(f, f ^ 1) for f in range(fsdp_size)])

    def member_gather(blocks):
        if others == 2:
            theirs = pair_send(blocks)
            return jnp.stack(
                [jnp.where(member == 0, blocks, theirs), jnp.where(member == 0, theirs, blocks)],
                axis=1,
            )
        full = lax.all_gather(blocks, "fsdp", axis=0, axis_index_groups=member_lists)
        return jnp.moveaxis(full, 0, 1)

    def member_scatter(blocks):
        if others == 2:
            sent = pair_send(block_at(blocks, 1 - member, 1))
            return block_at(blocks, member, 1).astype(f32) + sent.astype(f32)
        return lax.psum_scatter(
            blocks, "fsdp", scatter_dimension=1, axis_index_groups=member_lists, tiled=False
        ).astype(f32)

    pair_count = caption_lengths.shape[0]
    row_count, model_width = tokens.shape
    slot_count = row_count // pair_count
    sub_rows = row_count // 4
    head_dim = model_width // HEADS
    local_width = w_qkv.shape[2]
    block_rows = w_qkv.shape[0]
    hidden_width = FF
    local_hidden = w_fc1.shape[1] // GROUPS

    model_part = jnp.concatenate([model_gains, model_biases], axis=0)
    head_part = jnp.concatenate([head_biases, head_gain[None]], axis=0)
    unit_part = jnp.concatenate([ffn_biases, ffn_gain[None]], axis=0)
    packed = jnp.concatenate([model_part.reshape(-1), head_part.reshape(-1), unit_part.reshape(-1)])
    vectors = lax.all_to_all(
        jnp.broadcast_to(packed[None], (fsdp_size, packed.shape[0])), "fsdp", 0, 0
    )
    sizes = [model_part.size, head_part.size, unit_part.size]
    model_vectors = (
        vectors[:, : sizes[0]].reshape((fsdp_size,) + model_part.shape).transpose(1, 0, 2)
    ).reshape(6, model_width).astype(f32)
    head_vectors = (
        vectors[:, sizes[0] : sizes[0] + sizes[1]]
        .reshape((fsdp_size,) + head_part.shape)
        .transpose(1, 0, 2)
    ).reshape(5, local_width).astype(f32)
    unit_all = vectors[:, sizes[0] + sizes[1] :].reshape((GROUPS, others) + unit_part.shape)
    unit_vectors = block_at(unit_all, group).transpose(1, 0, 2).reshape(3, local_hidden).astype(f32)

    def rows_gather(piece, *tokens):
        pieces = [piece] + [group_send(piece, shift) for shift in range(1, GROUPS)]
        across = [tp_send(piece, 2)]
        pieces[1] = after(pieces[1], across[0])
        across += [tp_send(part, 2) for part in pieces[1:]]
        near = after(jnp.concatenate(pieces + across, axis=0), *tokens)
        return near, tp_send(near, 1)

    def core_sum(away, kept):
        return (kept + tp_send(away, 1).astype(f32)).reshape(2, sub_rows, -1)

    def side_sum(total):
        crossing = tp_send(block_at(total, 1 - side).astype(bf16), 2)
        return block_at(total, side) + crossing.astype(f32)

    def group_core(far, near):
        total = near.astype(f32) + tp_send(far, 1).astype(f32)
        return total.reshape(2, GROUPS, sub_rows, -1)

    def group_shares(total):
        return total[0] + tp_send(total[1].astype(bf16), 2).astype(f32)

    def group_shares_piped(total):
        return {k: total[0, k] + tp_send(total[1, k].astype(bf16), 2).astype(f32) for k in (2, 1, 3, 0)}

    def group_total(shares):
        sent = [group_send(shares[k].astype(bf16), -k).astype(f32) for k in (1, 3, 2)]
        return shares[0], sent

    def group_sum(values):
        def swap(array, width):
            pieces = [array[:, i : i + width] for i in range(0, array.shape[1], width)]
            pieces = [pieces[i ^ 1] for i in range(len(pieces))]
            return jnp.concatenate(pieces, axis=1)

        half_rows = 2 * GROUPS * sub_rows
        flip_core = tp_send(values, 1)
        flip_side = tp_send(values, 2)
        flip_both = tp_send(values, 3)
        values = values + swap(flip_core + swap(flip_both, half_rows // 2), half_rows)
        values = values + swap(flip_side, half_rows // 2)
        total = values
        for shift in range(1, GROUPS):
            part = group_send(values, shift).reshape(8, 4, GROUPS * sub_rows)
            cut = (GROUPS - shift) * sub_rows
            part = jnp.concatenate([part[:, :, cut:], part[:, :, :cut]], axis=2)
            total = total + part.reshape(8, -1)
        return total

    def my_rows(array):
        return lax.dynamic_slice_in_dim(array, rank * sub_rows, sub_rows, 0)

    slot_index = jnp.arange(slot_count)[None, :]
    key_valid = slot_index < IMAGE + caption_lengths[:, None]
    keep_rows = key_valid.reshape(row_count).astype(f32)[:, None]
    my_keep = my_rows(keep_rows)
    my_grad_out = my_rows(cotangent).astype(f32) * my_keep
    depth = model_width // 8
    own_block = jnp.concatenate([w_qkv[:, c] for c in range(3)] + [w_out.T], axis=0)
    blocks = ring.gather(own_block)
    labels = jnp.arange(8, dtype=jnp.int32) if ring.native else ring.labels(range(8))

    fc_pieces = jnp.concatenate(
        [w.reshape(block_rows, GROUPS, local_hidden) for w in (w_fc1, w_fc2.T)], axis=0
    )
    fc_pieces = after(fc_pieces.transpose(1, 0, 2), blocks[3])
    fc_mine = [block_at(fc_pieces, group)]
    for shift in (1, 3, 2):
        fc_mine.append(group_send(block_at(fc_pieces, (group + shift) % GROUPS), shift))
    fc_received = list(fc_mine)
    if others == 2:
        fc_theirs = [pair_send(part) for part in fc_mine]
        fc_labels = row_at(
            [
                [(f // 2 - k) % GROUPS * 2 + f % 2 for k in (0, 1, 3, 2)]
                + [(f // 2 - k) % GROUPS * 2 + 1 - f % 2 for k in (0, 1, 3, 2)]
                for f in range(fsdp_size)
            ],
            here,
        )
    else:
        full = jnp.zeros(fc_pieces.shape, bf16)
        for shift, part in zip((0, 1, 3, 2), fc_mine):
            full = put(full, part, (group - shift) % GROUPS)
        full = lax.all_gather(full, "fsdp", axis=0, axis_index_groups=member_lists)
        full = full.reshape(others, GROUPS, 2, block_rows, local_hidden).transpose(2, 1, 0, 3, 4)
        full = full.reshape(2, 8, depth, local_hidden).transpose(1, 0, 2, 3)
        full = full.reshape(8, 2 * depth, local_hidden)
        fc_mine, fc_theirs = [full[k] for k in range(4)], [full[k] for k in range(4, 8)]
        fc_labels = jnp.arange(8)
    fc_labels = fc_labels.astype(jnp.int32)
    fc_blocks = fc_mine + fc_theirs
    cotangent_rows = after(my_grad_out.astype(bf16), fc_received[3])
    cotangent_rows = [cotangent_rows] + [
        group_send(cotangent_rows, shift) for shift in range(1, GROUPS)
    ]

    tables = rotation_tables(slot_count, head_dim)
    limits = IMAGE + caption_lengths
    scale_value = 1.0 / math.sqrt(head_dim)
    normed_in, _, _ = norm_rows(tokens.astype(f32), model_vectors[0], model_vectors[2])
    normed_in_b = normed_in.astype(bf16)
    part_width = 4 * head_dim
    parts = local_width // part_width
    scalars = pl.BlockSpec(memory_space=pltpu.SMEM)

    def whole(shape, first=0):
        return pl.BlockSpec(shape, lambda j: (first,) + (0,) * (len(shape) - 1))

    def columns(rows):
        return pl.BlockSpec((rows, part_width), lambda j: (0, j))

    def projection_specs(width, index_map):
        full = pl.BlockSpec((3 * depth, width), index_map)
        return [full] * 4 + [pl.BlockSpec((2 * depth, width), index_map)] * 2 + [full] * 3

    out_row = whole((depth, local_width), 3)
    out_specs = [out_row] * 4 + [whole((depth, local_width), 1)] + [out_row] * 3
    out_blocks = blocks[:4] + blocks[5:]
    rank_array = rank.astype(jnp.int32)[None]
    big = pltpu.CompilerParams(vmem_limit_bytes=58 << 20)
    queries, keys_rot, values_in, heads_out, head_sums = pl.pallas_call(
        functools.partial(
            attention_forward, slots=slot_count, head_dim=head_dim, scale=scale_value
        ),
        grid=(parts,),
        in_specs=[scalars, scalars, whole((row_count, model_width))]
        + projection_specs(part_width, lambda j: (0, j))
        + [columns(5), whole((4, slot_count, 2 * head_dim))],
        out_specs=[columns(row_count)] * 4 + [whole((row_count, 128))],
        out_shape=[jax.ShapeDtypeStruct((row_count, local_width), bf16)] * 3
        + [
            jax.ShapeDtypeStruct((row_count, local_width), f32),
            jax.ShapeDtypeStruct((row_count, 128), f32),
        ],
        compiler_params=big,
        cost_estimate=cost(2 * row_count * model_width * 3 * local_width, 12 << 20, 1 << 20),
        name="attention_forward",
    )(labels, limits, normed_in_b, *blocks, head_vectors, tables)
    head_stats = tp_sum(head_sums[:, :2].T)
    mean_attn, inverse_attn = norm_stats(
        head_stats[0][:, None], head_stats[1][:, None], model_width
    )
    coefficients = jnp.concatenate([mean_attn, inverse_attn], axis=1)
    halves = [
        jax.ShapeDtypeStruct((2 * sub_rows, model_width), bf16),
        jax.ShapeDtypeStruct((2 * sub_rows, model_width), f32),
    ]
    half_specs = [whole((2 * sub_rows, model_width))] * 2
    away, kept, post_attn_b = pl.pallas_call(
        output_product,
        grid=(1,),
        in_specs=[
            scalars,
            scalars,
            whole((row_count, local_width)),
            whole((row_count, 2)),
            whole((5, local_width)),
        ]
        + out_specs,
        out_specs=half_specs + [whole((row_count, local_width))],
        out_shape=halves + [jax.ShapeDtypeStruct((row_count, local_width), bf16)],
        compiler_params=big,
        cost_estimate=cost(2 * row_count * model_width * local_width, 5 << 20),
        name="output_product",
    )(labels, rank_array, after(heads_out, *fc_received[1:3], fc_theirs[0]), coefficients, head_vectors, *out_blocks)
    branch = side_sum(after(core_sum(away, kept), fc_received[3]))
    middle = my_rows(tokens).astype(f32) + branch + model_vectors[4]
    normed_mid, hat_mid, inverse_mid = norm_rows(middle, model_vectors[1], model_vectors[3])

    cotangent_near = after(jnp.concatenate(cotangent_rows, axis=0), fc_received[3])
    cotangent_near = jnp.concatenate([cotangent_near, tp_send(cotangent_near, 2)], axis=0)
    grad_out_all = (cotangent_near, tp_send(cotangent_near, 1))
    normed_mid_all = rows_gather(
        after(normed_mid.astype(bf16), *cotangent_rows), *fc_theirs[1:]
    )
    half_rows = 2 * GROUPS * sub_rows
    step_rows = half_rows // 2

    def rows(width):
        return pl.BlockSpec((step_rows, width), lambda j: (j, 0))

    fc_half = [[whole((depth, local_hidden), start)] * 8 for start in range(2)]
    half_shape = jax.ShapeDtypeStruct((half_rows, local_hidden), f32)
    half_shape_b = jax.ShapeDtypeStruct((half_rows, local_hidden), bf16)
    product_shape = jax.ShapeDtypeStruct((half_rows, model_width), bf16)

    def forward_half(x, g):
        return pl.pallas_call(
            ffn_forward,
            grid=(2,),
            in_specs=[scalars, rows(model_width), rows(model_width), whole((3, local_hidden))]
            + [whole((2 * depth, local_hidden))] * 8,
            out_specs=[rows(local_hidden)] * 3 + [pl.BlockSpec((8, step_rows), lambda j: (0, j))],
            out_shape=[half_shape] * 3 + [jax.ShapeDtypeStruct((8, half_rows), f32)],
            compiler_params=big,
            cost_estimate=cost(4 * half_rows * model_width * local_hidden, 10 << 20, 1 << 20),
            name="ffn_forward",
        )(fc_labels, x, g, unit_vectors, *fc_blocks)

    *hidden_near, sums_near = forward_half(normed_mid_all[0], grad_out_all[0])
    *hidden_far, sums_far = forward_half(normed_mid_all[1], grad_out_all[1])
    sums = group_sum(jnp.concatenate([sums_near, sums_far], axis=1))

    def backward_half(index, hidden):
        return pl.pallas_call(
            functools.partial(ffn_backward, width=hidden_width),
            grid=(2,),
            in_specs=[scalars, pl.BlockSpec((8, step_rows), lambda j: (0, j + 2 * index))]
            + [rows(local_hidden)] * 3
            + [whole((3, local_hidden))]
            + fc_half[0],
            out_specs=[rows(local_hidden)] * 2 + [rows(model_width), whole((8, local_hidden))],
            out_shape=[half_shape_b] * 2
            + [product_shape, jax.ShapeDtypeStruct((8, local_hidden), f32)],
            compiler_params=big,
            cost_estimate=cost(2 * half_rows * model_width * local_hidden, 8 << 20),
            name="ffn_backward",
        )(fc_labels, sums, *hidden, unit_vectors, *fc_blocks)

    before_far, post_far, mid_far, totals_far = backward_half(1, hidden_far)
    before_near, post_near, mid_near, totals_near = backward_half(0, hidden_near)

    def second_half(post):
        return pl.pallas_call(
            ffn_product,
            grid=(2,),
            in_specs=[scalars, rows(local_hidden)] + fc_half[1],
            out_specs=rows(model_width),
            out_shape=product_shape,
            compiler_params=big,
            cost_estimate=cost(2 * half_rows * model_width * local_hidden, 5 << 20),
            name="ffn_product",
        )(fc_labels, post, *fc_blocks)

    mid_total = group_core(mid_far, mid_near)
    shares = group_shares_piped(mid_total)
    unit_s = member_scatter((totals_near + totals_far)[:3].reshape(3, others, -1))

    fc_order = (2, 1, 3, 0)

    def fc_gradient(order, token):
        return pl.pallas_call(
            ffn_gradient,
            grid_spec=pltpu.PrefetchScalarGridSpec(
                num_scalar_prefetch=1,
                grid=(4,),
                in_specs=[pl.BlockSpec((half_rows, depth), lambda j, label: (0, label[j]))] * 4
                + [pl.BlockSpec((half_rows, local_hidden), lambda j, label: (0, 0))] * 4,
                out_specs=[pl.BlockSpec((2 * depth, local_hidden), lambda j, label: (0, 0))] * 4,
            ),
            out_shape=[jax.ShapeDtypeStruct((2 * depth, local_hidden), bf16)] * 4,
            compiler_params=big,
            cost_estimate=cost(4 * half_rows * model_width * local_hidden, 9 << 20),
            name="ffn_gradient",
        )(
            order.astype(jnp.int32),
            *normed_mid_all,
            *grad_out_all,
            before_near,
            before_far,
            *after((post_near, post_far), token),
        )

    if others == 2:
        ahead = [[(f // 2 + k) % GROUPS * 2 for k in fc_order] for f in range(fsdp_size)]
        away_labels = row_at([[a + 1 - f % 2 for a in row] for f, row in enumerate(ahead)], here)
        kept_labels = row_at([[a + f % 2 for a in row] for f, row in enumerate(ahead)], here)
        fc_away = fc_gradient(away_labels, mid_total)
        fc_kept = fc_gradient(kept_labels, shares[2])
        fc_sent = [pair_send(part) for part in fc_away]
        fc_summed = [
            (kept.astype(f32) + sent.astype(f32)).astype(bf16)
            for kept, sent in zip(fc_kept, fc_sent)
        ]
    else:
        fc_away = fc_gradient(jnp.arange(4), mid_total)
        fc_kept = fc_gradient(jnp.arange(4, 8), shares[2])
        fc_grads = jnp.stack(fc_away + fc_kept)
        fc_grads = fc_grads.reshape(8, 2, depth, local_hidden).transpose(1, 0, 2, 3)
        fc_grads = fc_grads.reshape(2, GROUPS, others, block_rows, local_hidden)
        fc_grads = fc_grads.transpose(1, 2, 0, 3, 4).reshape(GROUPS, others, -1, local_hidden)
        fc_grads = member_scatter(fc_grads).astype(bf16)
        fc_summed = [block_at(fc_grads, (group + shift) % GROUPS) for shift in fc_order]
        fc_sent = fc_summed

    shares[1], shares[3] = after((shares[1], shares[3]), *fc_away)
    own, sent = group_total(shares)
    own = after(own, fc_kept[0], *fc_sent[:3], unit_s)
    grad_mid_normed = own + sent[0] + sent[1] + sent[2]
    grad_middle = my_grad_out + norm_back_rows(
        grad_mid_normed * model_vectors[1], hat_mid, inverse_mid
    )
    grad_middle_b = tp_rows_gather(grad_middle.astype(bf16), core, side)
    fc_spread = [group_send(part, k) if k else part for k, part in zip(fc_order, fc_summed)]

    grad_post_attn, back_sums = pl.pallas_call(
        output_back,
        grid=(1,),
        in_specs=[
            scalars,
            whole((row_count, model_width)),
            whole((row_count, local_width)),
            whole((row_count, 2)),
            whole((5, local_width)),
        ]
        + out_specs,
        out_specs=[whole((row_count, local_width)), whole((row_count, 128))],
        out_shape=[
            jax.ShapeDtypeStruct((row_count, local_width), f32),
            jax.ShapeDtypeStruct((row_count, 128), f32),
        ],
        compiler_params=big,
        cost_estimate=cost(2 * row_count * model_width * local_width, 5 << 20),
        name="output_back",
    )(labels, after(grad_middle_b, fc_sent[3]), heads_out, coefficients, head_vectors, *out_blocks)
    head_back = tp_sum(back_sums[:, :2].T)[:, :, None]
    coefficients = jnp.concatenate(
        [coefficients, head_back[0] / model_width, head_back[1] / model_width], axis=1
    )
    *grad_linear, head_sums_back = pl.pallas_call(
        functools.partial(
            attention_backward, slots=slot_count, head_dim=head_dim, scale=scale_value
        ),
        grid=(parts,),
        in_specs=[
            scalars,
            columns(row_count),
            columns(row_count),
            whole((row_count, 4)),
            columns(5),
            whole((4, slot_count, 2 * head_dim)),
            columns(row_count),
            columns(row_count),
            columns(row_count),
        ],
        out_specs=[columns(row_count)] * 3 + [columns(8)],
        out_shape=[jax.ShapeDtypeStruct((row_count, local_width), bf16)] * 3
        + [jax.ShapeDtypeStruct((8, local_width), f32)],
        compiler_params=pltpu.CompilerParams(vmem_limit_bytes=40 << 20),
        cost_estimate=cost(10 * row_count * slot_count * 2 * local_width, 4 << 20, 1 << 20),
        name="attention_backward",
    )(
        limits,
        grad_post_attn,
        heads_out,
        coefficients,
        head_vectors,
        tables,
        queries,
        keys_rot,
        values_in,
    )
    def weight_gradients(kernel, count, order, out_specs, out_shape):
        return pl.pallas_call(
            kernel,
            grid_spec=pltpu.PrefetchScalarGridSpec(
                num_scalar_prefetch=1,
                grid=(count,),
                in_specs=[pl.BlockSpec((row_count, depth), lambda j, label: (0, label[j]))] * 2
                + [pl.BlockSpec((row_count, local_width), lambda j, label: (0, 0))] * 4,
                out_specs=out_specs,
            ),
            out_shape=out_shape,
            compiler_params=big,
            cost_estimate=cost(count * row_count * depth * 8 * local_width, count << 20),
            name=kernel.__name__,
        )(order, normed_in_b, grad_middle_b, *grad_linear, post_attn_b)

    far_grads = weight_gradients(
        projection_gradient_far,
        1,
        labels[4:5],
        [pl.BlockSpec((2 * depth, local_width), lambda j, label: (0, 0))] * 2,
        [jax.ShapeDtypeStruct((2 * depth, local_width), bf16)] * 2,
    )
    order = [0, 3, 5, 2, 6, 1, 7]
    weight_grads = weight_gradients(
        projection_gradient,
        7,
        jnp.asarray(order, jnp.int32) if ring.native else ring.labels(order),
        pl.BlockSpec((1, 4 * depth, local_width), lambda j, label: (j, 0, 0)),
        jax.ShapeDtypeStruct((7, 4 * depth, local_width), bf16),
    )
    weight_grads = dict((k, weight_grads[j]) for j, k in enumerate(order))
    weight_grads[4] = far_grads
    if ring.native:
        weight_grads[4] = jnp.concatenate(far_grads, axis=0)
        weight_grads = jnp.stack([weight_grads[k] for k in range(8)])
        weight_grads = weight_grads.reshape(8, 4, fsdp_size // 8, block_rows, local_width)
        weight_grads = weight_grads.transpose(0, 2, 1, 3, 4).reshape(fsdp_size, -1, local_width)
    placed_rows = (block_rows, GROUPS * local_hidden)
    def place_ffn(token):
        return pl.pallas_call(
            ffn_placed,
            grid=(1,),
            in_specs=[scalars] + [whole((2 * block_rows, local_hidden))] * 4,
            out_specs=[whole(placed_rows), whole(placed_rows[::-1])],
            out_shape=[
                jax.ShapeDtypeStruct(placed_rows, f32),
                jax.ShapeDtypeStruct(placed_rows[::-1], f32),
            ],
            compiler_params=big,
            cost_estimate=cost(0, 6 << 20),
            name="ffn_placed",
        )(
            row_at([[(f // others - k) % GROUPS for k in fc_order] for f in range(fsdp_size)], here),
            *after(tuple(fc_spread), token),
        )

    results = {}

    def while_half(token):
        results["parts"] = [second_half(after(post, token)) for post in (post_far, post_near)]
        return fc_spread + results["parts"]

    def while_first(token):
        back_away, back_kept = pl.pallas_call(
            projection_back,
            grid=(1,),
            in_specs=[scalars, scalars]
            + [whole((row_count, local_width))] * 3
            + projection_specs(local_width, lambda j: (0, 0)),
            out_specs=half_specs,
            out_shape=halves,
            compiler_params=big,
            cost_estimate=cost(2 * row_count * model_width * 3 * local_width, 10 << 20),
            name="projection_back",
        )(labels, rank_array, *after(tuple(grad_linear), token), *blocks)
        results["back"] = back_away, back_kept
        results["core"] = group_core(*after(tuple(results["parts"]), token))
        return back_away, back_kept, results["core"]

    def by_block(vectors_in, blocks_in):
        return vectors_in.reshape(vectors_in.shape[0], blocks_in, -1).transpose(1, 0, 2)

    def while_second(token):
        grad_in_normed = side_sum(core_sum(*after(results["back"], token)))
        _, hat_in, inverse_in = norm_rows(
            my_rows(tokens).astype(f32), model_vectors[0], model_vectors[2]
        )
        grad_token_rows = grad_middle + norm_back_rows(
            grad_in_normed * model_vectors[0], hat_in, inverse_in
        )
        model_grads = (
            jnp.stack(
                [
                    jnp.sum(grad_in_normed * hat_in, axis=0),
                    jnp.sum(grad_mid_normed * hat_mid, axis=0),
                    jnp.sum(grad_in_normed, axis=0),
                    jnp.sum(grad_mid_normed, axis=0),
                    jnp.sum(grad_middle, axis=0),
                    jnp.sum(my_grad_out, axis=0),
                ]
            )
        )
        results["shares"] = group_shares(after(results["core"], token))
        results["tokens"] = grad_token_rows
        model_blocks = by_block(model_grads, fsdp_size).reshape(fsdp_size, -1)
        head_blocks = by_block(head_sums_back[:5], fsdp_size).reshape(fsdp_size, -1)
        joined = jnp.concatenate([model_blocks, head_blocks], axis=1)
        results["joined"] = jnp.sum(lax.all_to_all(joined, "fsdp", 0, 0), axis=0)
        results["placed"] = place_ffn(token)
        return [results["joined"], results["tokens"], results["shares"]] + list(results["placed"])

    def while_third(token):
        joined_s, token_rows, shares = after(
            (results["joined"], results["tokens"], results["shares"]), token
        )
        model_size = 6 * model_width // fsdp_size
        results["model_s"] = tp_sum(joined_s[None, :model_size]).reshape(6, -1)
        results["head_s"] = joined_s[model_size:].reshape(5, -1)
        results["grad_tokens"] = tp_rows_gather(token_rows, core, side)
        own, sent = group_total(shares)
        second = own + sent[0] + sent[1] + sent[2]
        out_rows = ((middle + second + model_vectors[5]) * my_keep).astype(bf16)
        results["layer_out"] = tp_rows_gather(out_rows, core, side)
        return ()

    weights_s = ring.scatter(weight_grads, [while_half, while_first, while_second, while_third])
    weights_s = weights_s.reshape(4, block_rows, local_width)
    grad_qkv_s = weights_s[:3].transpose(1, 0, 2)
    grad_out_s = weights_s[3]
    return (
        results["layer_out"],
        results["grad_tokens"],
        grad_qkv_s,
        results["head_s"][:4],
        results["head_s"][4],
        grad_out_s.T,
        results["model_s"][:2],
        results["model_s"][2:],
        *results["placed"],
        unit_s[2],
        unit_s[:2],
    )


def solution(mesh):
    placed = (
        P("fsdp", None),
        P("fsdp", None),
        P("fsdp"),
        P("fsdp", None, "tp"),
        P(None, ("tp", "fsdp")),
        P(("tp", "fsdp")),
        P("tp", "fsdp"),
        P(None, "fsdp"),
        P(None, "fsdp"),
        P("fsdp", "tp"),
        P("tp", "fsdp"),
        P(("tp", "fsdp")),
        P(None, ("tp", "fsdp")),
    )
    return jax.shard_map(
        functools.partial(per_device, fsdp_size=mesh.shape["fsdp"]),
        mesh=mesh,
        in_specs=placed,
        out_specs=(
            P("fsdp", None),
            P("fsdp", None),
            P("fsdp", None, "tp"),
            P(None, ("tp", "fsdp")),
            P(("tp", "fsdp")),
            P("tp", "fsdp"),
            P(None, "fsdp"),
            P(None, "fsdp"),
            P("fsdp", "tp"),
            P("tp", "fsdp"),
            P(("tp", "fsdp")),
            P(None, ("tp", "fsdp")),
        ),
        check_vma=False,
    )
```

```python
import functools
import math

import jax
import jax.numpy as jnp
import numpy as np
from jax import lax
from jax.experimental import pallas as pl
from jax.experimental.pallas import tpu as pltpu
from jax.sharding import PartitionSpec as P

HEADS = 32
FF = 8192
IMAGE = 64
GROUPS = 4

f32 = jnp.float32
bf16 = jnp.bfloat16
norm_eps = 1e-05


def pick(table, index):
    return lax.dynamic_index_in_dim(jnp.asarray(table, jnp.int32), index, keepdims=False)


def row_at(table, index):
    return lax.dynamic_index_in_dim(jnp.asarray(table, jnp.int32), index, keepdims=False)


def put(buffer, block, index):
    return lax.dynamic_update_slice(buffer, block[None], (index,) + (0,) * block.ndim)


def block_at(array, index, axis=0):
    return lax.dynamic_index_in_dim(array, index, axis, keepdims=False)


def after(value, *tokens):
    return lax.optimization_barrier((value,) + tokens)[0]


class Ring:
    def __init__(self, size, here):
        self.size = size
        self.here = here
        self.native = size > 8
        self.order = list(range(0, size, 2)) + list(range(size - 1, 0, -2))
        self.position = pick([self.order.index(i) for i in range(size)], here)
        self.forward = [(self.order[i], self.order[(i + 1) % size]) for i in range(size)]
        self.backward = [(b, a) for a, b in self.forward]

    def label(self, offset):
        return pick(self.order, (self.position + offset) % self.size)

    def labels(self, offsets):
        place = [self.order.index(i) for i in range(self.size)]
        return row_at(
            [[self.order[(place[i] + k) % self.size] for k in offsets] for i in range(self.size)],
            self.here,
        )

    def send(self, block, way):
        return lax.ppermute(block, "fsdp", self.forward if way > 0 else self.backward)

    def gather_parts(self, block):
        half = self.size // 2
        parts = [(0, block)]
        onward = backward = block
        for step in range(1, half):
            onward = self.send(onward, 1)
            backward = self.send(backward, -1)
            parts += [(-step, onward), (step, backward)]
        cut = block.shape[0] // 2
        return parts, [self.send(onward[:cut], 1), self.send(backward[cut:], -1)]

    def gather(self, block):
        if self.native:
            full = lax.all_gather(block, "fsdp", axis=0)
            wide = full.reshape((8, self.size // 8, 4, -1, block.shape[1]))
            wide = wide.transpose(0, 2, 1, 3, 4).reshape(8, -1, block.shape[1])
            cut = wide.shape[1] // 2
            blocks = [wide[k] for k in range(8)]
            return blocks[:4] + [blocks[4][:cut], blocks[4][cut:]] + blocks[5:]
        parts, halves = self.gather_parts(block)
        parts = dict((offset % 8, part) for offset, part in parts)
        return [parts[k] for k in range(4)] + halves + [parts[k] for k in range(5, 8)]

    def scatter(self, part, stages):
        if self.native:
            for stage in stages:
                stage(part)
            return lax.psum_scatter(part, "fsdp", scatter_dimension=0, tiled=False).astype(f32)
        half = self.size // 2
        cut = part[half][0].shape[0]
        onward = self.send(part[half][0], 1)
        backward = self.send(part[half][1], -1)
        tokens = stages[0](part[half][0])
        for step in range(half - 1, 0, -1):
            onward, backward = after((onward, backward), *tokens)
            ahead = part[step].astype(f32)
            behind = part[self.size - step].astype(f32)
            if step == half - 1:
                ahead = jnp.concatenate([ahead[:cut] + onward.astype(f32), ahead[cut:]], axis=0)
                behind = jnp.concatenate(
                    [behind[:cut], behind[cut:] + backward.astype(f32)], axis=0
                )
            else:
                ahead = ahead + onward.astype(f32)
                behind = behind + backward.astype(f32)
            ahead, behind = ahead.astype(bf16), behind.astype(bf16)
            onward = self.send(ahead, 1)
            backward = self.send(behind, -1)
            tokens = stages[half - step](ahead)
        return part[0].astype(f32) + onward.astype(f32) + backward.astype(f32)


def tp_send(block, mask):
    return lax.ppermute(block, "tp", [(i, i ^ mask) for i in range(4)])


def tp_sum(values):
    return values + tp_send(values, 1) + tp_send(values, 2) + tp_send(values, 3)


def tp_rows_gather(piece, core, side):
    across = tp_send(piece, 2)
    blocks = [piece, tp_send(piece, 1), across, tp_send(across, 1)]
    blocks = [jnp.where(core == 1, blocks[i ^ 1], blocks[i]) for i in range(4)]
    blocks = [jnp.where(side == 1, blocks[i ^ 2], blocks[i]) for i in range(4)]
    return jnp.concatenate(blocks, axis=0)


def rotation_tables(count, row_width):
    position = np.arange(count, dtype=np.float32)[:, None]
    lane = np.arange(row_width)[None, :]
    channel = (lane % row_width // 2).astype(np.float32)
    frequency = np.exp(-(2.0 * channel / row_width) * np.log(np.float32(10000.0)))
    angle = (position * frequency).astype(np.float32)
    zeta_base = (2.0 * channel + 0.4 * row_width) / (1.4 * row_width)
    growth = np.exp((position - count // 2) / 512.0 * np.log(zeta_base))
    cosine = np.cos(angle)
    sine = np.sin(angle) * np.where(lane % 2 == 0, -1.0, 1.0)
    tables = [cosine * growth, sine * growth, cosine / growth, sine / growth]
    one_head = lax.optimization_barrier(jnp.asarray(np.stack(tables).astype(np.float32)))
    return jnp.concatenate([one_head, one_head], axis=2)


def swapped(values):
    width = values.shape[1]
    lane = lax.broadcasted_iota(jnp.int32, values.shape, 1)
    return jnp.where(lane % 2 == 0, pltpu.roll(values, width - 1, 1), pltpu.roll(values, 1, 1))


def scores_of(query, key, limit, scale_value):
    raw = matmul(query, key, ((1,), (1,))) * scale_value
    row = lax.broadcasted_iota(jnp.int32, raw.shape, 0)
    column = lax.broadcasted_iota(jnp.int32, raw.shape, 1)
    scores = jnp.where((column <= row) & (column < limit), raw, -1e30)
    top = jnp.max(scores, axis=-1, keepdims=True)
    grown = jnp.exp(scores - top)
    return grown * (1.0 / jnp.sum(grown, axis=-1, keepdims=True))


def in_head(values, head, head_dim):
    lane = lax.broadcasted_iota(jnp.int32, values.shape, 1)
    return jnp.where(lane // head_dim == head, values, jnp.zeros_like(values))


def block_columns(labels, k, depth):
    return pl.ds(pl.multiple_of(labels[k] * depth, depth), depth)


def row_parts(rank, rows):
    core = lax.rem(rank, 2)
    return [
        [pl.ds(pl.multiple_of((2 * side + place) * rows, rows), rows) for side in range(2)]
        for place in (1 - core, core)
    ]


def attention_forward(labels, limits, x, *refs, slots, head_dim, scale):
    blocks, (bias, tables, q_out, k_out, v_out, o_out, sums) = refs[:9], refs[9:]
    depth = x.shape[1] // 8
    pairs = x.shape[0] // slots
    width = 2 * head_dim
    turned = []
    for c in range(3):
        total = bias[c : c + 1, :]
        for k in range(8):
            if k == 4:
                part = blocks[4 + c // 2][c % 2 * depth : (c % 2 + 1) * depth, :]
            else:
                part = blocks[k + k // 5][c * depth : (c + 1) * depth, :]
            total = total + matmul(x[:, block_columns(labels, k, depth)], part, ((1,), (0,)))
        turned.append(total)
    first = jnp.zeros((x.shape[0], 1), f32)
    square = jnp.zeros((x.shape[0], 1), f32)
    for j in range(q_out.shape[1] // width):
        lanes = slice(j * width, (j + 1) * width)
        for p in range(pairs):
            rows = slice(p * slots, (p + 1) * slots)
            q = turned[0][rows, lanes]
            q = q * tables[0] + swapped(q) * tables[1]
            k = turned[1][rows, lanes]
            k = (k * tables[2] + swapped(k) * tables[3]).astype(bf16)
            v = turned[2][rows, lanes].astype(bf16)
            q_out[rows, lanes] = q.astype(bf16)
            k_out[rows, lanes] = k
            v_out[rows, lanes] = v
            mixed = []
            for head in range(2):
                probs = scores_of(in_head(q, head, head_dim).astype(bf16), k, limits[p], scale)
                mixed.append(matmul(probs.astype(bf16), v, ((1,), (0,))))
            lane = lax.broadcasted_iota(jnp.int32, mixed[0].shape, 1)
            o_out[rows, lanes] = jnp.where(lane < head_dim, mixed[0], mixed[1])
    mixed = o_out[...]
    lane = lax.broadcasted_iota(jnp.int32, sums.shape, 1)
    partial = jnp.where(lane == 0, jnp.sum(mixed, axis=-1, keepdims=True), 0.0) + jnp.where(
        lane == 1, jnp.sum(mixed * mixed, axis=-1, keepdims=True), 0.0
    )

    @pl.when(pl.program_id(0) == 0)
    def _():
        sums[...] = partial

    @pl.when(pl.program_id(0) > 0)
    def _():
        sums[...] += partial


def attention_backward(
    limits, grad, mixed, coefficients, gain, tables, q_in, k_in, v_in, gq_out, gk_out, gv_out, sums, *, slots, head_dim, scale
):
    pairs = grad.shape[0] // slots
    width = 2 * head_dim
    mean, inverse = coefficients[:, 0:1], coefficients[:, 1:2]
    first, second = coefficients[:, 2:3], coefficients[:, 3:4]
    row = lax.broadcasted_iota(jnp.int32, (8, width), 0)
    for j in range(grad.shape[1] // width):
        lanes = slice(j * width, (j + 1) * width)
        total = jnp.zeros((8, width), f32)
        for p in range(pairs):
            rows = slice(p * slots, (p + 1) * slots)
            g = grad[rows, lanes]
            hat = (mixed[rows, lanes] - mean[rows]) * inverse[rows]
            total += jnp.where(row == 3, jnp.sum(g, axis=0, keepdims=True), 0.0)
            total += jnp.where(row == 4, jnp.sum(g * hat, axis=0, keepdims=True), 0.0)
            g = inverse[rows] * (g * gain[4:5, lanes] - first[rows] - hat * second[rows])
            q, k, v = q_in[rows, lanes].astype(f32), k_in[rows, lanes].astype(f32), v_in[rows, lanes]
            gq = jnp.zeros((slots, width), f32)
            gk = jnp.zeros((slots, width), f32)
            gv = jnp.zeros((slots, width), f32)
            for head in range(2):
                q_head = in_head(q, head, head_dim).astype(bf16)
                k_head = in_head(k, head, head_dim).astype(bf16)
                g_head = in_head(g, head, head_dim).astype(bf16)
                probs = scores_of(q_head, k_head, limits[p], scale)
                grad_probs = matmul(g_head, v, ((1,), (1,)))
                gv += matmul(probs.astype(bf16), g_head, ((0,), (0,)))
                spread = jnp.sum(probs * grad_probs, axis=-1, keepdims=True)
                grad_scores = (probs * (grad_probs - spread) * scale).astype(bf16)
                gq += matmul(grad_scores, k_head, ((1,), (0,)))
                gk += matmul(grad_scores, q_head, ((0,), (0,)))
            gq = (gq * tables[0] - swapped(gq) * tables[1]).astype(bf16)
            gk = (gk * tables[2] - swapped(gk) * tables[3]).astype(bf16)
            gv = gv.astype(bf16)
            gq_out[rows, lanes] = gq
            gk_out[rows, lanes] = gk
            gv_out[rows, lanes] = gv
            for index, part in enumerate((gq, gk, gv)):
                total += jnp.where(
                    row == index, jnp.sum(part.astype(f32), axis=0, keepdims=True), 0.0
                )
        sums[:, lanes] = total


def output_product(labels, rank, mixed, coefficients, gains, *refs):
    blocks, (away_out, kept_out, post_out) = refs[:8], refs[8:]
    depth = away_out.shape[1] // 8
    rows = away_out.shape[0] // 2
    hat = (mixed[...] - coefficients[:, 0:1]) * coefficients[:, 1:2]
    post_out[...] = (hat * gains[4:5, :] + gains[3:4, :]).astype(bf16)
    for out, slices in zip((away_out, kept_out), row_parts(rank[0], rows)):
        left = jnp.concatenate([post_out[part, :] for part in slices], axis=0)
        for k in range(8):
            product = matmul(left, blocks[k][...], ((1,), (1,)))
            out[:, block_columns(labels, k, depth)] = product.astype(out.dtype)


def output_back(labels, grad, mixed, coefficients, gains, *refs):
    blocks, (out, sums) = refs[:8], refs[8:]
    depth = grad.shape[1] // 8
    total = jnp.zeros(out.shape, f32)
    for k in range(8):
        total = total + matmul(
            grad[:, block_columns(labels, k, depth)], blocks[k][...], ((1,), (0,))
        )
    out[...] = total
    scaled = total * gains[4:5, :]
    hat = (mixed[...] - coefficients[:, 0:1]) * coefficients[:, 1:2]
    lane = lax.broadcasted_iota(jnp.int32, sums.shape, 1)
    sums[...] = jnp.where(lane == 0, jnp.sum(scaled, axis=-1, keepdims=True), 0.0) + jnp.where(
        lane == 1, jnp.sum(scaled * hat, axis=-1, keepdims=True), 0.0
    )


def projection_gradient(labels, x, grad, gq, gk, gv, post, out):
    depth = x.shape[1]
    for c, part in enumerate((gq, gk, gv)):
        out[0, c * depth : (c + 1) * depth, :] = matmul(x[...], part[...], ((0,), (0,))).astype(bf16)
    out[0, 3 * depth :, :] = matmul(grad[...], post[...], ((0,), (0,))).astype(bf16)


def projection_gradient_far(labels, x, grad, gq, gk, gv, post, first_out, second_out):
    depth = x.shape[1]
    first_out[:depth, :] = matmul(x[...], gq[...], ((0,), (0,))).astype(bf16)
    first_out[depth:, :] = matmul(x[...], gk[...], ((0,), (0,))).astype(bf16)
    second_out[:depth, :] = matmul(x[...], gv[...], ((0,), (0,))).astype(bf16)
    second_out[depth:, :] = matmul(grad[...], post[...], ((0,), (0,))).astype(bf16)


def projection_back(labels, rank, gq, gk, gv, *refs):
    blocks, (away_out, kept_out) = refs[:9], refs[9:]
    depth = away_out.shape[1] // 8
    rows = away_out.shape[0] // 2
    for out, slices in zip((away_out, kept_out), row_parts(rank[0], rows)):
        left = [
            jnp.concatenate([grad[part, :] for part in slices], axis=0) for grad in (gq, gk, gv)
        ]
        for k in range(8):
            total = jnp.zeros((2 * rows, depth), f32)
            for c in range(3):
                if k == 4:
                    part = blocks[4 + c // 2][c % 2 * depth : (c % 2 + 1) * depth, :]
                else:
                    part = blocks[k + k // 5][c * depth : (c + 1) * depth, :]
                total = total + matmul(left[c], part, ((1,), (1,)))
            out[:, block_columns(labels, k, depth)] = total.astype(out.dtype)


def columns_of(rows):
    return jnp.transpose(jnp.concatenate([rows] * 16, axis=0))


def ffn_forward(labels, x, g, vectors, *refs):
    blocks, (active_out, slope_out, grad_out, sums) = refs[:8], refs[8:]
    depth = x.shape[1] // 8
    before = vectors[0:1, :]
    grad = jnp.zeros(grad_out.shape, f32)
    for k in range(8):
        lanes = block_columns(labels, k, depth)
        before = before + matmul(x[:, lanes], blocks[k][:depth, :], ((1,), (0,)))
        grad = grad + matmul(g[:, lanes], blocks[k][depth:, :], ((1,), (0,)))
    below = 0.5 + 0.5 * lax.erf(before * math.sqrt(0.5))
    active = before * below
    active_out[...] = active
    slope_out[...] = below + before * (math.sqrt(0.5 / math.pi) * jnp.exp(-0.5 * before * before))
    grad_out[...] = grad
    scaled = grad * vectors[2:3, :]
    lane = lax.broadcasted_iota(jnp.int32, (grad.shape[0], 128), 1)
    columns = jnp.zeros((grad.shape[0], 128), f32)
    for index, values in enumerate((active, active * active, scaled, scaled * active)):
        columns += jnp.where(lane == index, jnp.sum(values, axis=-1, keepdims=True), 0.0)
    sums[...] = jnp.transpose(columns)[:8, :]


def ffn_backward(labels, sums, active, slope, grad, vectors, *refs, width):
    blocks, (before_out, post_out, out, totals) = refs[:8], refs[8:]
    columns = columns_of(sums[...])
    mean = columns[:, 0:1] / width
    inverse = lax.rsqrt(columns[:, 1:2] / width - mean * mean + norm_eps)
    hat_sum = inverse * (columns[:, 3:4] - mean * columns[:, 2:3])
    hat = (active[...] - mean) * inverse
    gain = vectors[2:3, :]
    post_out[...] = (hat * gain + vectors[1:2, :]).astype(bf16)
    moved = grad[...] * gain - columns[:, 2:3] / width - hat * (hat_sum / width)
    grad_before = (inverse * moved * slope[...]).astype(bf16)
    before_out[...] = grad_before
    product_into(labels, grad_before, blocks, out)
    row = lax.broadcasted_iota(jnp.int32, totals.shape, 0)
    partial = jnp.zeros(totals.shape, f32)
    for index, values in enumerate((grad_before.astype(f32), grad[...], grad[...] * hat)):
        partial += jnp.where(row == index, jnp.sum(values, axis=0, keepdims=True), 0.0)

    @pl.when(pl.program_id(0) == 0)
    def _():
        totals[...] = partial

    @pl.when(pl.program_id(0) > 0)
    def _():
        totals[...] += partial


def product_into(labels, left, blocks, out):
    depth = out.shape[1] // 8
    for k in range(8):
        product = matmul(left, blocks[k][...], ((1,), (1,)))
        out[:, block_columns(labels, k, depth)] = product.astype(bf16)


def ffn_product(labels, left, *refs):
    product_into(labels, left[...], refs[:8], refs[8])


def ffn_gradient(labels, near_x, far_x, near_g, far_g, near_before, far_before, near_post, far_post, *outs):
    depth = near_x.shape[1]
    totals = []
    for c, (near, far, near_right, far_right) in enumerate(
        ((near_x, far_x, near_before, far_before), (near_g, far_g, near_post, far_post))
    ):
        total = matmul(near[...], near_right[...], ((0,), (0,)))
        total = total + matmul(far[...], far_right[...], ((0,), (0,)))
        totals.append(total.astype(bf16))
    for k, out in enumerate(outs):

        @pl.when(pl.program_id(0) == k)
        def _(out=out):
            for c, total in enumerate(totals):
                out[c * depth : (c + 1) * depth, :] = total


def ffn_placed(groups, *refs):
    blocks, (first_out, second_out) = refs[:4], refs[4:]
    depth, width = blocks[0].shape[0] // 2, blocks[0].shape[1]
    for k in range(4):
        place = pl.ds(pl.multiple_of(groups[k] * width, width), width)
        first_out[:, place] = blocks[k][:depth, :].astype(f32)
        second_out[place, :] = jnp.transpose(blocks[k][depth:, :].astype(f32))


def cost(flops, moved, exponentials=0):
    return pl.CostEstimate(flops=flops, bytes_accessed=moved, transcendentals=exponentials)


def norm_stats(first_sum, square_sum, row_width):
    mean_value = first_sum / row_width
    variance = square_sum / row_width - mean_value * mean_value
    return mean_value, lax.rsqrt(variance + norm_eps)


def norm_rows(values, gain_vector, shift_vector):
    width = values.shape[-1]
    mean_value, inverse = norm_stats(
        jnp.sum(values, axis=-1, keepdims=True),
        jnp.sum(values * values, axis=-1, keepdims=True),
        width,
    )
    hat = (values - mean_value) * inverse
    return hat * gain_vector + shift_vector, hat, inverse


def norm_back_rows(scaled, hat, inverse):
    width = scaled.shape[-1]
    return inverse * (
        scaled
        - jnp.sum(scaled, axis=-1, keepdims=True) / width
        - hat * jnp.sum(scaled * hat, axis=-1, keepdims=True) / width
    )


def matmul(a, b, dims):
    return lax.dot_general(a, b, (dims, ((), ())), preferred_element_type=f32)


def per_device(
    tokens,
    cotangent,
    caption_lengths,
    w_qkv,
    head_biases,
    head_gain,
    w_out,
    model_gains,
    model_biases,
    w_fc1,
    w_fc2,
    ffn_gain,
    ffn_biases,
    *,
    fsdp_size,
):
    here = lax.axis_index("fsdp")
    rank = lax.axis_index("tp")
    core, side = rank % 2, rank // 2
    others = fsdp_size // GROUPS
    group, member = here // others, here % others
    ring = Ring(fsdp_size, here)
    group_lists = [[g * others + o for g in range(GROUPS)] for o in range(others)]
    member_lists = [[g * others + o for o in range(others)] for g in range(GROUPS)]

    def group_send(block, shift):
        return lax.ppermute(
            block,
            "fsdp",
            [
                (g * others + o, (g + shift) % GROUPS * others + o)
                for g in range(GROUPS)
                for o in range(others)
            ],
        )

    def group_swap(blocks):
        return lax.all_to_all(blocks, "fsdp", 0, 0, axis_index_groups=group_lists)

    def pair_send(block):
        return lax.ppermute(block, "fsdp", [(f, f ^ 1) for f in range(fsdp_size)])

    def member_gather(blocks):
        if others == 2:
            theirs = pair_send(blocks)
            return jnp.stack(
                [jnp.where(member == 0, blocks, theirs), jnp.where(member == 0, theirs, blocks)],
                axis=1,
            )
        full = lax.all_gather(blocks, "fsdp", axis=0, axis_index_groups=member_lists)
        return jnp.moveaxis(full, 0, 1)

    def member_scatter(blocks):
        if others == 2:
            sent = pair_send(block_at(blocks, 1 - member, 1))
            return block_at(blocks, member, 1).astype(f32) + sent.astype(f32)
        return lax.psum_scatter(
            blocks, "fsdp", scatter_dimension=1, axis_index_groups=member_lists, tiled=False
        ).astype(f32)

    pair_count = caption_lengths.shape[0]
    row_count, model_width = tokens.shape
    slot_count = row_count // pair_count
    sub_rows = row_count // 4
    head_dim = model_width // HEADS
    local_width = w_qkv.shape[2]
    block_rows = w_qkv.shape[0]
    hidden_width = FF
    local_hidden = w_fc1.shape[1] // GROUPS

    model_part = jnp.concatenate([model_gains, model_biases], axis=0)
    head_part = jnp.concatenate([head_biases, head_gain[None]], axis=0)
    unit_part = jnp.concatenate([ffn_biases, ffn_gain[None]], axis=0)
    packed = jnp.concatenate([model_part.reshape(-1), head_part.reshape(-1), unit_part.reshape(-1)])
    vectors = lax.all_to_all(
        jnp.broadcast_to(packed[None], (fsdp_size, packed.shape[0])), "fsdp", 0, 0
    )
    sizes = [model_part.size, head_part.size, unit_part.size]
    model_vectors = (
        vectors[:, : sizes[0]].reshape((fsdp_size,) + model_part.shape).transpose(1, 0, 2)
    ).reshape(6, model_width).astype(f32)
    head_vectors = (
        vectors[:, sizes[0] : sizes[0] + sizes[1]]
        .reshape((fsdp_size,) + head_part.shape)
        .transpose(1, 0, 2)
    ).reshape(5, local_width).astype(f32)
    unit_all = vectors[:, sizes[0] + sizes[1] :].reshape((GROUPS, others) + unit_part.shape)
    unit_vectors = block_at(unit_all, group).transpose(1, 0, 2).reshape(3, local_hidden).astype(f32)

    def rows_gather(piece, *tokens):
        pieces = [piece] + [group_send(piece, shift) for shift in range(1, GROUPS)]
        across = [tp_send(piece, 2)]
        pieces[1] = after(pieces[1], across[0])
        across += [tp_send(part, 2) for part in pieces[1:]]
        near = after(jnp.concatenate(pieces + across, axis=0), *tokens)
        return near, tp_send(near, 1)

    def core_sum(away, kept):
        return (kept + tp_send(away, 1).astype(f32)).reshape(2, sub_rows, -1)

    def side_sum(total):
        crossing = tp_send(block_at(total, 1 - side).astype(bf16), 2)
        return block_at(total, side) + crossing.astype(f32)

    def group_core(far, near):
        total = near.astype(f32) + tp_send(far, 1).astype(f32)
        return total.reshape(2, GROUPS, sub_rows, -1)

    def group_shares(total):
        return total[0] + tp_send(total[1].astype(bf16), 2).astype(f32)

    def group_shares_piped(total):
        return {k: total[0, k] + tp_send(total[1, k].astype(bf16), 2).astype(f32) for k in (2, 1, 3, 0)}

    def group_total(shares):
        sent = [group_send(shares[k].astype(bf16), -k).astype(f32) for k in (1, 3, 2)]
        return shares[0], sent

    def group_sum(values):
        def swap(array, width):
            pieces = [array[:, i : i + width] for i in range(0, array.shape[1], width)]
            pieces = [pieces[i ^ 1] for i in range(len(pieces))]
            return jnp.concatenate(pieces, axis=1)

        half_rows = 2 * GROUPS * sub_rows
        flip_core = tp_send(values, 1)
        flip_side = tp_send(values, 2)
        flip_both = tp_send(values, 3)
        values = values + swap(flip_core + swap(flip_both, half_rows // 2), half_rows)
        values = values + swap(flip_side, half_rows // 2)
        total = values
        for shift in range(1, GROUPS):
            part = group_send(values, shift).reshape(8, 4, GROUPS * sub_rows)
            cut = (GROUPS - shift) * sub_rows
            part = jnp.concatenate([part[:, :, cut:], part[:, :, :cut]], axis=2)
            total = total + part.reshape(8, -1)
        return total

    def my_rows(array):
        return lax.dynamic_slice_in_dim(array, rank * sub_rows, sub_rows, 0)

    slot_index = jnp.arange(slot_count)[None, :]
    key_valid = slot_index < IMAGE + caption_lengths[:, None]
    keep_rows = key_valid.reshape(row_count).astype(f32)[:, None]
    my_keep = my_rows(keep_rows)
    my_grad_out = my_rows(cotangent).astype(f32) * my_keep
    depth = model_width // 8
    own_block = jnp.concatenate([w_qkv[:, c] for c in range(3)] + [w_out.T], axis=0)
    blocks = ring.gather(own_block)
    labels = jnp.arange(8, dtype=jnp.int32) if ring.native else ring.labels(range(8))

    fc_pieces = jnp.concatenate(
        [w.reshape(block_rows, GROUPS, local_hidden) for w in (w_fc1, w_fc2.T)], axis=0
    )
    fc_pieces = after(fc_pieces.transpose(1, 0, 2), blocks[3])
    fc_mine = [block_at(fc_pieces, group)]
    for shift in (1, 3, 2):
        fc_mine.append(group_send(block_at(fc_pieces, (group + shift) % GROUPS), shift))
    fc_received = list(fc_mine)
    if others == 2:
        fc_theirs = [pair_send(part) for part in fc_mine]
        fc_labels = row_at(
            [
                [(f // 2 - k) % GROUPS * 2 + f % 2 for k in (0, 1, 3, 2)]
                + [(f // 2 - k) % GROUPS * 2 + 1 - f % 2 for k in (0, 1, 3, 2)]
                for f in range(fsdp_size)
            ],
            here,
        )
    else:
        full = jnp.zeros(fc_pieces.shape, bf16)
        for shift, part in zip((0, 1, 3, 2), fc_mine):
            full = put(full, part, (group - shift) % GROUPS)
        full = lax.all_gather(full, "fsdp", axis=0, axis_index_groups=member_lists)
        full = full.reshape(others, GROUPS, 2, block_rows, local_hidden).transpose(2, 1, 0, 3, 4)
        full = full.reshape(2, 8, depth, local_hidden).transpose(1, 0, 2, 3)
        full = full.reshape(8, 2 * depth, local_hidden)
        fc_mine, fc_theirs = [full[k] for k in range(4)], [full[k] for k in range(4, 8)]
        fc_labels = jnp.arange(8)
    fc_labels = fc_labels.astype(jnp.int32)
    fc_blocks = fc_mine + fc_theirs
    cotangent_rows = after(my_grad_out.astype(bf16), fc_received[3])
    cotangent_rows = [cotangent_rows] + [
        group_send(cotangent_rows, shift) for shift in range(1, GROUPS)
    ]

    tables = rotation_tables(slot_count, head_dim)
    limits = IMAGE + caption_lengths
    scale_value = 1.0 / math.sqrt(head_dim)
    normed_in, _, _ = norm_rows(tokens.astype(f32), model_vectors[0], model_vectors[2])
    normed_in_b = normed_in.astype(bf16)
    part_width = 4 * head_dim
    parts = local_width // part_width
    scalars = pl.BlockSpec(memory_space=pltpu.SMEM)

    def whole(shape, first=0):
        return pl.BlockSpec(shape, lambda j: (first,) + (0,) * (len(shape) - 1))

    def columns(rows):
        return pl.BlockSpec((rows, part_width), lambda j: (0, j))

    def projection_specs(width, index_map):
        full = pl.BlockSpec((3 * depth, width), index_map)
        return [full] * 4 + [pl.BlockSpec((2 * depth, width), index_map)] * 2 + [full] * 3

    out_row = whole((depth, local_width), 3)
    out_specs = [out_row] * 4 + [whole((depth, local_width), 1)] + [out_row] * 3
    out_blocks = blocks[:4] + blocks[5:]
    rank_array = rank.astype(jnp.int32)[None]
    big = pltpu.CompilerParams(vmem_limit_bytes=58 << 20)
    queries, keys_rot, values_in, heads_out, head_sums = pl.pallas_call(
        functools.partial(
            attention_forward, slots=slot_count, head_dim=head_dim, scale=scale_value
        ),
        grid=(parts,),
        in_specs=[scalars, scalars, whole((row_count, model_width))]
        + projection_specs(part_width, lambda j: (0, j))
        + [columns(5), whole((4, slot_count, 2 * head_dim))],
        out_specs=[columns(row_count)] * 4 + [whole((row_count, 128))],
        out_shape=[jax.ShapeDtypeStruct((row_count, local_width), bf16)] * 3
        + [
            jax.ShapeDtypeStruct((row_count, local_width), f32),
            jax.ShapeDtypeStruct((row_count, 128), f32),
        ],
        compiler_params=big,
        cost_estimate=cost(2 * row_count * model_width * 3 * local_width, 12 << 20, 1 << 20),
        name="attention_forward",
    )(labels, limits, normed_in_b, *blocks, head_vectors, tables)
    head_stats = tp_sum(head_sums[:, :2].T)
    mean_attn, inverse_attn = norm_stats(
        head_stats[0][:, None], head_stats[1][:, None], model_width
    )
    coefficients = jnp.concatenate([mean_attn, inverse_attn], axis=1)
    halves = [
        jax.ShapeDtypeStruct((2 * sub_rows, model_width), bf16),
        jax.ShapeDtypeStruct((2 * sub_rows, model_width), f32),
    ]
    half_specs = [whole((2 * sub_rows, model_width))] * 2
    away, kept, post_attn_b = pl.pallas_call(
        output_product,
        grid=(1,),
        in_specs=[
            scalars,
            scalars,
            whole((row_count, local_width)),
            whole((row_count, 2)),
            whole((5, local_width)),
        ]
        + out_specs,
        out_specs=half_specs + [whole((row_count, local_width))],
        out_shape=halves + [jax.ShapeDtypeStruct((row_count, local_width), bf16)],
        compiler_params=big,
        cost_estimate=cost(2 * row_count * model_width * local_width, 5 << 20),
        name="output_product",
    )(labels, rank_array, after(heads_out, *fc_received[1:3], fc_theirs[0]), coefficients, head_vectors, *out_blocks)
    branch = side_sum(after(core_sum(away, kept), fc_received[3]))
    middle = my_rows(tokens).astype(f32) + branch + model_vectors[4]
    normed_mid, hat_mid, inverse_mid = norm_rows(middle, model_vectors[1], model_vectors[3])

    cotangent_near = after(jnp.concatenate(cotangent_rows, axis=0), fc_received[3])
    cotangent_near = jnp.concatenate([cotangent_near, tp_send(cotangent_near, 2)], axis=0)
    grad_out_all = (cotangent_near, tp_send(cotangent_near, 1))
    normed_mid_all = rows_gather(
        after(normed_mid.astype(bf16), *cotangent_rows), *fc_theirs[1:]
    )
    half_rows = 2 * GROUPS * sub_rows
    step_rows = half_rows // 2

    def rows(width):
        return pl.BlockSpec((step_rows, width), lambda j: (j, 0))

    fc_half = [[whole((depth, local_hidden), start)] * 8 for start in range(2)]
    half_shape = jax.ShapeDtypeStruct((half_rows, local_hidden), f32)
    half_shape_b = jax.ShapeDtypeStruct((half_rows, local_hidden), bf16)
    product_shape = jax.ShapeDtypeStruct((half_rows, model_width), bf16)

    def forward_half(x, g):
        return pl.pallas_call(
            ffn_forward,
            grid=(2,),
            in_specs=[scalars, rows(model_width), rows(model_width), whole((3, local_hidden))]
            + [whole((2 * depth, local_hidden))] * 8,
            out_specs=[rows(local_hidden)] * 3 + [pl.BlockSpec((8, step_rows), lambda j: (0, j))],
            out_shape=[half_shape] * 3 + [jax.ShapeDtypeStruct((8, half_rows), f32)],
            compiler_params=big,
            cost_estimate=cost(4 * half_rows * model_width * local_hidden, 10 << 20, 1 << 20),
            name="ffn_forward",
        )(fc_labels, x, g, unit_vectors, *fc_blocks)

    *hidden_near, sums_near = forward_half(normed_mid_all[0], grad_out_all[0])
    *hidden_far, sums_far = forward_half(normed_mid_all[1], grad_out_all[1])
    sums = group_sum(jnp.concatenate([sums_near, sums_far], axis=1))

    def backward_half(index, hidden):
        return pl.pallas_call(
            functools.partial(ffn_backward, width=hidden_width),
            grid=(2,),
            in_specs=[scalars, pl.BlockSpec((8, step_rows), lambda j: (0, j + 2 * index))]
            + [rows(local_hidden)] * 3
            + [whole((3, local_hidden))]
            + fc_half[0],
            out_specs=[rows(local_hidden)] * 2 + [rows(model_width), whole((8, local_hidden))],
            out_shape=[half_shape_b] * 2
            + [product_shape, jax.ShapeDtypeStruct((8, local_hidden), f32)],
            compiler_params=big,
            cost_estimate=cost(2 * half_rows * model_width * local_hidden, 8 << 20),
            name="ffn_backward",
        )(fc_labels, sums, *hidden, unit_vectors, *fc_blocks)

    before_far, post_far, mid_far, totals_far = backward_half(1, hidden_far)
    before_near, post_near, mid_near, totals_near = backward_half(0, hidden_near)

    def second_half(post):
        return pl.pallas_call(
            ffn_product,
            grid=(2,),
            in_specs=[scalars, rows(local_hidden)] + fc_half[1],
            out_specs=rows(model_width),
            out_shape=product_shape,
            compiler_params=big,
            cost_estimate=cost(2 * half_rows * model_width * local_hidden, 5 << 20),
            name="ffn_product",
        )(fc_labels, post, *fc_blocks)

    mid_total = group_core(mid_far, mid_near)
    shares = group_shares_piped(mid_total)
    unit_s = member_scatter((totals_near + totals_far)[:3].reshape(3, others, -1))

    fc_order = (2, 1, 3, 0)

    def fc_gradient(order, token):
        return pl.pallas_call(
            ffn_gradient,
            grid_spec=pltpu.PrefetchScalarGridSpec(
                num_scalar_prefetch=1,
                grid=(4,),
                in_specs=[pl.BlockSpec((half_rows, depth), lambda j, label: (0, label[j]))] * 4
                + [pl.BlockSpec((half_rows, local_hidden), lambda j, label: (0, 0))] * 4,
                out_specs=[pl.BlockSpec((2 * depth, local_hidden), lambda j, label: (0, 0))] * 4,
            ),
            out_shape=[jax.ShapeDtypeStruct((2 * depth, local_hidden), bf16)] * 4,
            compiler_params=big,
            cost_estimate=cost(4 * half_rows * model_width * local_hidden, 9 << 20),
            name="ffn_gradient",
        )(
            order.astype(jnp.int32),
            *normed_mid_all,
            *grad_out_all,
            before_near,
            before_far,
            *after((post_near, post_far), token),
        )

    if others == 2:
        ahead = [[(f // 2 + k) % GROUPS * 2 for k in fc_order] for f in range(fsdp_size)]
        away_labels = row_at([[a + 1 - f % 2 for a in row] for f, row in enumerate(ahead)], here)
        kept_labels = row_at([[a + f % 2 for a in row] for f, row in enumerate(ahead)], here)
        fc_away = fc_gradient(away_labels, mid_total)
        fc_kept = fc_gradient(kept_labels, shares[2])
        fc_sent = [pair_send(part) for part in fc_away]
        fc_summed = [
            (kept.astype(f32) + sent.astype(f32)).astype(bf16)
            for kept, sent in zip(fc_kept, fc_sent)
        ]
    else:
        fc_away = fc_gradient(jnp.arange(4), mid_total)
        fc_kept = fc_gradient(jnp.arange(4, 8), shares[2])
        fc_grads = jnp.stack(fc_away + fc_kept)
        fc_grads = fc_grads.reshape(8, 2, depth, local_hidden).transpose(1, 0, 2, 3)
        fc_grads = fc_grads.reshape(2, GROUPS, others, block_rows, local_hidden)
        fc_grads = fc_grads.transpose(1, 2, 0, 3, 4).reshape(GROUPS, others, -1, local_hidden)
        fc_grads = member_scatter(fc_grads).astype(bf16)
        fc_summed = [block_at(fc_grads, (group + shift) % GROUPS) for shift in fc_order]
        fc_sent = fc_summed

    shares[1], shares[3] = after((shares[1], shares[3]), *fc_away)
    own, sent = group_total(shares)
    own = after(own, fc_kept[0], *fc_sent[:3], unit_s)
    grad_mid_normed = own + sent[0] + sent[1] + sent[2]
    grad_middle = my_grad_out + norm_back_rows(
        grad_mid_normed * model_vectors[1], hat_mid, inverse_mid
    )
    grad_middle_b = tp_rows_gather(grad_middle.astype(bf16), core, side)
    fc_spread = [group_send(part, k) if k else part for k, part in zip(fc_order, fc_summed)]

    grad_post_attn, back_sums = pl.pallas_call(
        output_back,
        grid=(1,),
        in_specs=[
            scalars,
            whole((row_count, model_width)),
            whole((row_count, local_width)),
            whole((row_count, 2)),
            whole((5, local_width)),
        ]
        + out_specs,
        out_specs=[whole((row_count, local_width)), whole((row_count, 128))],
        out_shape=[
            jax.ShapeDtypeStruct((row_count, local_width), f32),
            jax.ShapeDtypeStruct((row_count, 128), f32),
        ],
        compiler_params=big,
        cost_estimate=cost(2 * row_count * model_width * local_width, 5 << 20),
        name="output_back",
    )(labels, after(grad_middle_b, fc_sent[3]), heads_out, coefficients, head_vectors, *out_blocks)
    head_back = tp_sum(back_sums[:, :2].T)[:, :, None]
    coefficients = jnp.concatenate(
        [coefficients, head_back[0] / model_width, head_back[1] / model_width], axis=1
    )
    *grad_linear, head_sums_back = pl.pallas_call(
        functools.partial(
            attention_backward, slots=slot_count, head_dim=head_dim, scale=scale_value
        ),
        grid=(parts,),
        in_specs=[
            scalars,
            columns(row_count),
            columns(row_count),
            whole((row_count, 4)),
            columns(5),
            whole((4, slot_count, 2 * head_dim)),
            columns(row_count),
            columns(row_count),
            columns(row_count),
        ],
        out_specs=[columns(row_count)] * 3 + [columns(8)],
        out_shape=[jax.ShapeDtypeStruct((row_count, local_width), bf16)] * 3
        + [jax.ShapeDtypeStruct((8, local_width), f32)],
        compiler_params=pltpu.CompilerParams(vmem_limit_bytes=40 << 20),
        cost_estimate=cost(10 * row_count * slot_count * 2 * local_width, 4 << 20, 1 << 20),
        name="attention_backward",
    )(
        limits,
        grad_post_attn,
        heads_out,
        coefficients,
        head_vectors,
        tables,
        queries,
        keys_rot,
        values_in,
    )
    def weight_gradients(kernel, count, order, out_specs, out_shape):
        return pl.pallas_call(
            kernel,
            grid_spec=pltpu.PrefetchScalarGridSpec(
                num_scalar_prefetch=1,
                grid=(count,),
                in_specs=[pl.BlockSpec((row_count, depth), lambda j, label: (0, label[j]))] * 2
                + [pl.BlockSpec((row_count, local_width), lambda j, label: (0, 0))] * 4,
                out_specs=out_specs,
            ),
            out_shape=out_shape,
            compiler_params=big,
            cost_estimate=cost(count * row_count * depth * 8 * local_width, count << 20),
            name=kernel.__name__,
        )(order, normed_in_b, grad_middle_b, *grad_linear, post_attn_b)

    far_grads = weight_gradients(
        projection_gradient_far,
        1,
        labels[4:5],
        [pl.BlockSpec((2 * depth, local_width), lambda j, label: (0, 0))] * 2,
        [jax.ShapeDtypeStruct((2 * depth, local_width), bf16)] * 2,
    )
    order = [0, 3, 5, 2, 6, 1, 7]
    weight_grads = weight_gradients(
        projection_gradient,
        7,
        jnp.asarray(order, jnp.int32) if ring.native else ring.labels(order),
        pl.BlockSpec((1, 4 * depth, local_width), lambda j, label: (j, 0, 0)),
        jax.ShapeDtypeStruct((7, 4 * depth, local_width), bf16),
    )
    weight_grads = dict((k, weight_grads[j]) for j, k in enumerate(order))
    weight_grads[4] = far_grads
    if ring.native:
        weight_grads[4] = jnp.concatenate(far_grads, axis=0)
        weight_grads = jnp.stack([weight_grads[k] for k in range(8)])
        weight_grads = weight_grads.reshape(8, 4, fsdp_size // 8, block_rows, local_width)
        weight_grads = weight_grads.transpose(0, 2, 1, 3, 4).reshape(fsdp_size, -1, local_width)
    placed_rows = (block_rows, GROUPS * local_hidden)
    def place_ffn(token):
        return pl.pallas_call(
            ffn_placed,
            grid=(1,),
            in_specs=[scalars] + [whole((2 * block_rows, local_hidden))] * 4,
            out_specs=[whole(placed_rows), whole(placed_rows[::-1])],
            out_shape=[
                jax.ShapeDtypeStruct(placed_rows, f32),
                jax.ShapeDtypeStruct(placed_rows[::-1], f32),
            ],
            compiler_params=big,
            cost_estimate=cost(0, 6 << 20),
            name="ffn_placed",
        )(
            row_at([[(f // others - k) % GROUPS for k in fc_order] for f in range(fsdp_size)], here),
            *after(tuple(fc_spread), token),
        )

    results = {}

    def while_half(token):
        results["parts"] = [second_half(after(post, token)) for post in (post_far, post_near)]
        return fc_spread + results["parts"]

    def while_first(token):
        back_away, back_kept = pl.pallas_call(
            projection_back,
            grid=(1,),
            in_specs=[scalars, scalars]
            + [whole((row_count, local_width))] * 3
            + projection_specs(local_width, lambda j: (0, 0)),
            out_specs=half_specs,
            out_shape=halves,
            compiler_params=big,
            cost_estimate=cost(2 * row_count * model_width * 3 * local_width, 10 << 20),
            name="projection_back",
        )(labels, rank_array, *after(tuple(grad_linear), token), *blocks)
        results["back"] = back_away, back_kept
        results["core"] = group_core(*after(tuple(results["parts"]), token))
        return back_away, back_kept, results["core"]

    def by_block(vectors_in, blocks_in):
        return vectors_in.reshape(vectors_in.shape[0], blocks_in, -1).transpose(1, 0, 2)

    def while_second(token):
        grad_in_normed = side_sum(core_sum(*after(results["back"], token)))
        _, hat_in, inverse_in = norm_rows(
            my_rows(tokens).astype(f32), model_vectors[0], model_vectors[2]
        )
        grad_token_rows = grad_middle + norm_back_rows(
            grad_in_normed * model_vectors[0], hat_in, inverse_in
        )
        model_grads = (
            jnp.stack(
                [
                    jnp.sum(grad_in_normed * hat_in, axis=0),
                    jnp.sum(grad_mid_normed * hat_mid, axis=0),
                    jnp.sum(grad_in_normed, axis=0),
                    jnp.sum(grad_mid_normed, axis=0),
                    jnp.sum(grad_middle, axis=0),
                    jnp.sum(my_grad_out, axis=0),
                ]
            )
        )
        results["shares"] = group_shares(after(results["core"], token))
        results["tokens"] = grad_token_rows
        model_blocks = by_block(model_grads, fsdp_size).reshape(fsdp_size, -1)
        head_blocks = by_block(head_sums_back[:5], fsdp_size).reshape(fsdp_size, -1)
        joined = jnp.concatenate([model_blocks, head_blocks], axis=1)
        results["joined"] = jnp.sum(lax.all_to_all(joined, "fsdp", 0, 0), axis=0)
        results["placed"] = place_ffn(token)
        return [results["joined"], results["tokens"], results["shares"]] + list(results["placed"])

    def while_third(token):
        joined_s, token_rows, shares = after(
            (results["joined"], results["tokens"], results["shares"]), token
        )
        model_size = 6 * model_width // fsdp_size
        results["model_s"] = tp_sum(joined_s[None, :model_size]).reshape(6, -1)
        results["head_s"] = joined_s[model_size:].reshape(5, -1)
        results["grad_tokens"] = tp_rows_gather(token_rows, core, side)
        own, sent = group_total(shares)
        second = own + sent[0] + sent[1] + sent[2]
        out_rows = ((middle + second + model_vectors[5]) * my_keep).astype(bf16)
        results["layer_out"] = tp_rows_gather(out_rows, core, side)
        return ()

    weights_s = ring.scatter(weight_grads, [while_half, while_first, while_second, while_third])
    weights_s = weights_s.reshape(4, block_rows, local_width)
    grad_qkv_s = weights_s[:3].transpose(1, 0, 2)
    grad_out_s = weights_s[3]
    return (
        results["layer_out"],
        results["grad_tokens"],
        grad_qkv_s,
        results["head_s"][:4],
        results["head_s"][4],
        grad_out_s.T,
        results["model_s"][:2],
        results["model_s"][2:],
        *results["placed"],
        unit_s[2],
        unit_s[:2],
    )


def solution(mesh):
    placed = (
        P("fsdp", None),
        P("fsdp", None),
        P("fsdp"),
        P("fsdp", None, "tp"),
        P(None, ("tp", "fsdp")),
        P(("tp", "fsdp")),
        P("tp", "fsdp"),
        P(None, "fsdp"),
        P(None, "fsdp"),
        P("fsdp", "tp"),
        P("tp", "fsdp"),
        P(("tp", "fsdp")),
        P(None, ("tp", "fsdp")),
    )
    return jax.shard_map(
        functools.partial(per_device, fsdp_size=mesh.shape["fsdp"]),
        mesh=mesh,
        in_specs=placed,
        out_specs=(
            P("fsdp", None),
            P("fsdp", None),
            P("fsdp", None, "tp"),
            P(None, ("tp", "fsdp")),
            P(("tp", "fsdp")),
            P("tp", "fsdp"),
            P(None, "fsdp"),
            P(None, "fsdp"),
            P("fsdp", "tp"),
            P("tp", "fsdp"),
            P(("tp", "fsdp")),
            P(None, ("tp", "fsdp")),
        ),
        check_vma=False,
    )
```
